512 devices in a mesh: cells: 128 (over z, x_lo, y), harm: 4 (over x_hi, core).
Axes of the slice: x: 4 (x_hi: 2, x_lo: 2; x = x_hi * 2 + x_lo), y: 8, z: 8, core: 2. Of those that a mesh axis runs over, the one named last changes fastest.
Arguments:
- mean_adjoint: float32 [5, 262144], P(None, 'cells'), may hold values from -6 to 6
- harm_adjoint: float32 [4, 2, 5, 262144], P('harm', None, None, 'cells'), may hold values from -6 to 6
- harm_flow: float32 [4, 2, 5, 262144], P('harm', None, None, 'cells'), may hold values from -4 to 4
- flux_jacobian: float32 [5, 5, 262144], P(None, None, 'cells'), may hold values from -2.5 to 2.5
- face_weight: float32 [6, 262144], P(None, 'cells'), may hold values from 0.1 to 1
- face_links: int32 [6, 262144], P(None, 'cells'), may hold values from 0 to 4095, as said below
- face_tiles: int32 [2, 131072], P(None, 'cells'), may hold values from 0 to 2047, as said below
- pseudo_step: float32 [262144], P('cells'), may hold values from 0.1 to 0.4
- mean_source: float32 [5, 262144], P(None, 'cells'), may hold values from -6 to 6
- harm_order: int32 [4], P('harm'), may hold values from 0 to 3, each once
Outputs:
- mean_new: float32 [5, 262144], P(None, 'cells')
- harm_new: float32 [4, 2, 5, 262144], P('harm', None, None, 'cells')
The draws below stay inside these ranges and needn't reach their ends.
Inputs may be any that keep to these rules, and one draw needn't show every extreme that they name: `face_links`: an entry below 2048 names a cell of the same block; 2048 + r names entry r of the lower neighbour block's upper tile; 3072 + r names entry r of the upper neighbour block's lower tile. `face_tiles`: indices within the own block; columns b * 1024 to (b + 1) * 1024 - 1 belong to block b. `harm_order`: each index of harm holds a different harmonic.
All inputs are finite; a program needn't handle non-finite values.
Results may differ from the reference program's by a relative error of at most 0.0001.
Values sent between devices are 32-bit elements; how exact they have to be, the bound alone decides.
No kernel may reach another device: no remote copies, remote signals or barrier semaphores. Data moves between devices by JAX's collectives and lax.ppermute only.
A program may use at most 64 MiB of HBM per device.

```python
import math
import jax
import jax.numpy as jnp
from jax import lax

CELLS_DEV = 2048
FACE_DEV = 1024
VARS = 5
FACES = 6
SECTIONS = 2
HARM = 4
NC = 262144
NF = 131072
N_CELLS = 128


def draw_face_links(key, part):
    kind_key = jax.random.fold_in(key, 11)
    local_key = jax.random.fold_in(key, 12)
    rim_key = jax.random.fold_in(key, 13)
    selector = jax.random.randint(kind_key, (FACES, NC), 0, 4)
    local_cell = jax.random.randint(local_key, (FACES, NC), 0, CELLS_DEV)
    rim_cell = jax.random.randint(rim_key, (FACES, NC), CELLS_DEV, CELLS_DEV + 2 * FACE_DEV)
    return jnp.where(selector == 0, rim_cell, local_cell).astype(jnp.int32)


def draw_face_tiles(key, part):
    tile_key = jax.random.fold_in(key, 21)
    return jax.random.randint(tile_key, (2, NF), 0, CELLS_DEV).astype(jnp.int32)


def steps_of(rng, dims, pieces, least, high):
    level, own = 1.0, jax.random.fold_in(rng, 6)
    for position, parts in pieces:
        steps = jnp.exp(jax.random.uniform(jax.random.fold_in(own, position), (parts,), jnp.float32, least / len(pieces), high / len(pieces)))
        level = level * jnp.repeat(steps, dims[position] // parts).reshape([-1 if axis == position else 1 for axis in range(len(dims))])
    return level


def centred(stream_key, extent, spread, most, pieces=(), kind=jnp.bfloat16):
    values = jax.random.normal(stream_key, extent, jnp.float32) * spread
    if len(pieces) > 0:
        values = steps_of(stream_key, extent, pieces, -0.22, 0.18) * values
    return jnp.clip(values, min=-most, max=most).astype(kind)


def setup_inputs(seed: int = 0) -> dict:
    splits = jax.random.split(jax.random.key(seed), 11)
    mean_adjoint = centred(splits[0], (VARS, NC), 1.0, 6.0, ((1, 128),), jnp.float32)
    harm_adjoint = centred(splits[1], (HARM, 2, VARS, NC), 1.0, 6.0, ((0, 4), (3, 128)), jnp.float32)
    harm_flow = centred(splits[2], (HARM, 2, VARS, NC), 0.5, 4.0, ((0, 4), (3, 128)), jnp.float32)
    flux_jacobian = centred(splits[3], (VARS, VARS, NC), VARS ** -0.5, 2.5, ((2, 128),), jnp.float32)
    face_weight = jnp.clip(jnp.exp(math.log(1.0) - 2.3025851 * jax.random.uniform(splits[4], (FACES, NC), jnp.float32) ** steps_of(splits[4], (FACES, NC), ((1, 128),), -0.2, 0.2)), 0.1, 1.0)
    face_links = draw_face_links(jax.random.fold_in(splits[10], 71), 0)
    face_tiles = draw_face_tiles(jax.random.fold_in(splits[10], 71), 0)
    pseudo_step = jnp.clip(jnp.exp(math.log(0.4) - 1.3862944 * jax.random.uniform(splits[7], (NC,), jnp.float32) ** steps_of(splits[7], (NC,), ((0, 128),), -0.2, 0.2)), 0.1, 0.4)
    mean_source = centred(splits[8], (VARS, NC), 1.0, 6.0, ((1, 128),), jnp.float32)
    harm_order = jax.random.permutation(splits[9], HARM).astype(jnp.int32)
    return dict(mean_adjoint=mean_adjoint, harm_adjoint=harm_adjoint, harm_flow=harm_flow, flux_jacobian=flux_jacobian, face_weight=face_weight, face_links=face_links, face_tiles=face_tiles, pseudo_step=pseudo_step, mean_source=mean_source, harm_order=harm_order)


BASE_FREQ = 0.8


def extend(field, face_tiles):
    row_count = field.shape[0]
    blocks = field.reshape(row_count, N_CELLS, CELLS_DEV)
    tile_cells = face_tiles.reshape(2, N_CELLS, FACE_DEV)
    shape = (row_count, N_CELLS, FACE_DEV)
    lower_tile = jnp.take_along_axis(blocks, jnp.broadcast_to(tile_cells[0][None], shape), axis=2)
    upper_tile = jnp.take_along_axis(blocks, jnp.broadcast_to(tile_cells[1][None], shape), axis=2)
    return jnp.concatenate([blocks, jnp.roll(upper_tile, 1, axis=1), jnp.roll(lower_tile, -1, axis=1)], axis=2)


def gather_faces(extended, face_links, face_weight):
    row_count = extended.shape[0]
    neighbours = face_links.reshape(FACES, N_CELLS, CELLS_DEV)
    weights = face_weight.reshape(FACES, N_CELLS, CELLS_DEV)
    summed = jnp.zeros((row_count, N_CELLS, CELLS_DEV), jnp.float32)
    for face_num in range(FACES):
        index_rows = jnp.broadcast_to(neighbours[face_num][None], (row_count, N_CELLS, CELLS_DEV))
        picked = jnp.take_along_axis(extended, index_rows, axis=2)
        summed = summed + weights[face_num][None] * picked
    return summed.reshape(row_count, NC)


def apply_transpose(flux_jacobian, vectors):
    return jnp.einsum('jic,bjc->bic', flux_jacobian, vectors, precision=lax.Precision.HIGHEST)


def reference(mean_adjoint, harm_adjoint, harm_flow, flux_jacobian, face_weight, face_links, face_tiles, pseudo_step, mean_source, harm_order):
    weight_sum = jnp.sum(face_weight, axis=0)
    frequency = (BASE_FREQ * (harm_order.astype(jnp.float32) + 1.0))[:, None, None]
    mean_state = mean_adjoint
    harm_state = harm_adjoint
    for section_num in range(SECTIONS):
        section_coeff = 1.0 / (SECTIONS - section_num)
        stacked = jnp.concatenate([mean_state, harm_state.reshape(HARM * 2 * VARS, NC)], axis=0)
        gathered = gather_faces(extend(stacked, face_tiles), face_links, face_weight)
        flux_terms = weight_sum[None] * stacked - gathered
        stress = jnp.sum(harm_state[:, 0] * harm_flow[:, 0] + harm_state[:, 1] * harm_flow[:, 1], axis=0)
        mean_res = apply_transpose(flux_jacobian, (flux_terms[:VARS] - stress)[None])[0] - mean_source
        harm_terms = apply_transpose(flux_jacobian, flux_terms[VARS:].reshape(HARM * 2, VARS, NC)).reshape(HARM, 2, VARS, NC)
        real_res = harm_terms[:, 0] + frequency * harm_state[:, 1] - mean_state[None] * harm_flow[:, 0]
        imag_res = harm_terms[:, 1] - frequency * harm_state[:, 0] - mean_state[None] * harm_flow[:, 1]
        harm_res = jnp.stack([real_res, imag_res], axis=1)
        mean_state = mean_adjoint - section_coeff * pseudo_step[None] * mean_res
        harm_state = harm_adjoint - section_coeff * pseudo_step * harm_res
    return (mean_state, harm_state)
```

```python
import jax
import jax.numpy as jnp
from jax import lax
from jax.experimental import pallas as pl
from jax.experimental.pallas import tpu as pltpu
from jax.sharding import Mesh
from jax.sharding import PartitionSpec as P

VARS = 5
FACES = 6
SECTIONS = 2
ROWS = 3 * VARS
HARM = ("harm_0", "harm_1")
LANES = 128
SUBS = 8
BASE_FREQ = 0.8
F32 = jnp.float32


def struct(*shape, dtype=F32):
    return jax.ShapeDtypeStruct(shape, dtype)


def spread(row):
    return jnp.broadcast_to(row, (SUBS, LANES))


def packed(tile, first):
    sub = lax.broadcasted_iota(jnp.int32, (SUBS, LANES), 0)
    out = spread(tile(first))
    for i in range(1, SUBS):
        out = jnp.where(sub == i, spread(tile(first + i)), out)
    return out


def picked(row, count, index):
    low = index & (LANES - 1)
    high = index >> 7
    out = [None] * ROWS
    for h in range(count):
        hit = high == h
        for r in range(ROWS):
            value = jnp.take_along_axis(spread(row(r, h)), low, axis=1)
            out[r] = jnp.where(hit, value, 0.0 if h == 0 else out[r])
    return out


def store_tiles(row, tile_index, pay_a, pay_b, rows):
    for pay, index in zip((pay_a, pay_b), tile_index):
        for r, value in enumerate(picked(row, rows, index)):
            pay[r] = value


def native_row(mean_ref, harm_ref):
    def row(r, h):
        lanes = slice(h * LANES, (h + 1) * LANES)
        if r < VARS:
            return mean_ref[r : r + 1, lanes]
        part, var = divmod(r - VARS, VARS)
        return harm_ref[0, part, var : var + 1, lanes]

    return row


def open_kernel(odd_ref, mean_ref, harm_ref, flow_ref, tiles_ref, pay_a, pay_b, stress_ref, tile_idx):
    groups = mean_ref.shape[1] // LANES
    odd = odd_ref[0] == 1
    lower, upper = (
        packed(lambda t, k=k: tiles_ref[k : k + 1, t * LANES : (t + 1) * LANES], 0) for k in range(2)
    )
    first = jnp.where(odd, lower, upper)
    second = jnp.where(odd, upper, lower)
    tile_idx[0] = first
    tile_idx[1] = second
    row = native_row(mean_ref, harm_ref)
    store_tiles(row, (first, second), pay_a, pay_b, groups)
    flow = native_row(mean_ref, flow_ref)
    for v in range(VARS):
        for g in range(0, groups, SUBS):
            part = packed(
                lambda t: row(VARS + v, t) * flow(VARS + v, t) + row(2 * VARS + v, t) * flow(2 * VARS + v, t), g
            )
            stress_ref[v, g : g + SUBS, :] = part


def gather_into(row, count, first, index_ref, weight_ref, start):
    halves = index_ref.shape[0] // FACES
    out = []
    for g in range(halves):

        def face(f, acc):
            values = picked(row, count, index_ref[f * halves + g] - first)
            weight = weight_ref[f * halves + g]
            return tuple(a + weight * v for a, v in zip(acc, values))

        out.append(lax.fori_loop(0, FACES, face, tuple(start(r, g) for r in range(ROWS))))
    return out


def prepare_kernel(
    odd_ref, mean_ref, harm_ref, flow_ref, jac_ref, weight_in, links_ref, source_ref,
    acc_ref, index_ref, weight_ref, wsum_ref, state_ref, jac_out, flow_out, source_out,
):
    groups = mean_ref.shape[1] // LANES
    halves = groups // SUBS
    even = odd_ref[0] == 0
    rim = groups * LANES
    for g in range(halves):
        total = None
        for f in range(FACES):
            lane = lambda t: slice(t * LANES, (t + 1) * LANES)
            link = packed(lambda t: links_ref[f : f + 1, lane(t)], g * SUBS)
            flipped = jnp.where(link >= rim, link ^ (rim // 2), link)
            index_ref[f * halves + g] = jnp.where(even, flipped, link)
            weight = packed(lambda t: weight_in[f : f + 1, lane(t)], g * SUBS)
            weight_ref[f * halves + g] = weight
            total = weight if total is None else total + weight
        wsum_ref[g * SUBS : (g + 1) * SUBS, :] = total
    row = native_row(mean_ref, harm_ref)
    flow = native_row(mean_ref, flow_ref)
    for g in range(0, groups, SUBS):
        at = slice(g, g + SUBS)
        for r in range(ROWS):
            state_ref[r, at, :] = packed(lambda t: row(r, t), g)
        for r in range(2 * VARS):
            flow_out[r, at, :] = packed(lambda t: flow(VARS + r, t), g)
        for v in range(VARS):
            source_out[v, at, :] = packed(lambda t: source_ref[v : v + 1, t * LANES : (t + 1) * LANES], g)
        for j in range(VARS):
            for i in range(VARS):
                jac_out[j * VARS + i, at, :] = packed(
                    lambda t: jac_ref[j, i : i + 1, t * LANES : (t + 1) * LANES], g
                )
    gather_own(state_ref, index_ref, weight_ref, acc_ref)


def gather_own(state_ref, index_ref, weight_ref, acc_ref):
    zero = jnp.zeros((SUBS, LANES), F32)
    row = lambda r, h: state_ref[r, h : h + 1, :]
    out = gather_into(row, state_ref.shape[1], 0, index_ref, weight_ref, lambda r, g: zero)
    for g, values in enumerate(out):
        for r in range(ROWS):
            acc_ref[r, g * SUBS : (g + 1) * SUBS, :] = values[r]


def new_state(
    coeff, order_ref, acc_ref, rim_a, rim_b, index_ref, weight_ref, wsum_ref, state_ref, start_ref,
    jac_ref, flow_ref, source_ref, step_ref, stress_refs, out_ref,
):
    groups = acc_ref.shape[1]
    rim_rows = rim_a.shape[1]

    def row(r, h):
        ref = rim_a if h < rim_rows else rim_b
        h = h % rim_rows
        return ref[r, h : h + 1, :]

    omega = BASE_FREQ * (order_ref[0].astype(F32) + 1.0)
    gathered = gather_into(
        row, 2 * rim_rows, groups * LANES, index_ref, weight_ref,
        lambda r, g: acc_ref[r, g * SUBS : (g + 1) * SUBS, :],
    )
    for g in range(groups // SUBS):
        at = slice(g * SUBS, (g + 1) * SUBS)
        state = [state_ref[r, at, :] for r in range(ROWS)]
        wsum = wsum_ref[at, :]
        flux = [wsum * s - x for s, x in zip(state, gathered[g])]
        scale = coeff * step_ref[at, :]
        for v in range(VARS):
            total = stress_refs[0][v, at, :]
            for ref in stress_refs[1:]:
                total = total + ref[v, at, :]
            flux[v] = flux[v] - total
        for part in range(3):
            for i in range(VARS):
                r = part * VARS + i
                res = jac_ref[i, at, :] * flux[part * VARS]
                for j in range(1, VARS):
                    res = res + jac_ref[j * VARS + i, at, :] * flux[part * VARS + j]
                if part == 0:
                    res = res - source_ref[i, at, :]
                else:
                    other = state[(3 - part) * VARS + i]
                    turned = omega * other
                    res = res + turned if part == 1 else res - turned
                    res = res - state[i] * flow_ref[(part - 1) * VARS + i, at, :]
                out_ref[r, at, :] = start_ref[r, at, :] - scale * res


def middle_kernel(
    order_ref, acc_ref, rim_a, rim_b, index_ref, weight_ref, wsum_ref, state_ref,
    jac_ref, flow_ref, source_ref, step_ref, tile_idx, s0, s1, s2, s3,
    out_ref, pay_a, pay_b, stress_ref, *, coeff,
):
    new_state(
        coeff, order_ref, acc_ref, rim_a, rim_b, index_ref, weight_ref, wsum_ref, state_ref, state_ref,
        jac_ref, flow_ref, source_ref, step_ref, (s0, s1, s2, s3), out_ref,
    )
    groups = acc_ref.shape[1]
    store_tiles(lambda r, h: out_ref[r, h : h + 1, :], (tile_idx[0], tile_idx[1]), pay_a, pay_b, groups)
    for v in range(VARS):
        stress_ref[v] = out_ref[VARS + v] * flow_ref[v] + out_ref[2 * VARS + v] * flow_ref[VARS + v]


def close_kernel(
    order_ref, acc_ref, rim_a, rim_b, index_ref, weight_ref, wsum_ref, state_ref, start_ref,
    jac_ref, flow_ref, source_ref, step_ref, s0, s1, s2, s3,
    mean_out, harm_out, out_ref, *, coeff,
):
    new_state(
        coeff, order_ref, acc_ref, rim_a, rim_b, index_ref, weight_ref, wsum_ref, state_ref, start_ref,
        jac_ref, flow_ref, source_ref, step_ref, (s0, s1, s2, s3), out_ref,
    )
    for t in range(acc_ref.shape[1]):
        lanes = slice(t * LANES, (t + 1) * LANES)
        for part in range(3):
            tile = packed_vars(lambda i: out_ref[part * VARS + i, t : t + 1, :])
            if part == 0:
                mean_out[:, lanes] = tile
            else:
                harm_out[0, part - 1, :, lanes] = tile


def packed_vars(row):
    sub = lax.broadcasted_iota(jnp.int32, (SUBS, LANES), 0)
    out = spread(row(0))
    for i in range(1, VARS):
        out = jnp.where(sub == i, spread(row(i)), out)
    return out[:VARS]


def launch(body, name, out_shape, scalars, args, scratch=()):
    smem = pl.BlockSpec(memory_space=pltpu.SMEM)
    vmem = pl.BlockSpec(memory_space=pltpu.VMEM)
    return pl.pallas_call(
        body,
        name=name,
        out_shape=out_shape,
        in_specs=[smem] * len(scalars) + [vmem] * len(args),
        out_specs=[vmem] * len(out_shape),
        scratch_shapes=scratch,
    )(*scalars, *args)


def exchange(pay_a, pay_b, stress):
    count = lax.axis_size("cells")
    near = [(b, b ^ 1) for b in range(count)]
    far = [(b, (b - 1 + 2 * (b % 2)) % count) for b in range(count)]
    rim_b = lax.ppermute(pay_b, "cells", far)
    rim_a = lax.ppermute(pay_a, "cells", near)
    others = [lax.ppermute(stress, HARM, [(k, k ^ m) for k in range(4)]) for m in (1, 2, 3)]
    return rim_a, rim_b, (stress, *others)


def shards(
    mean_adjoint,
    harm_adjoint,
    harm_flow,
    flux_jacobian,
    face_weight,
    face_links,
    face_tiles,
    pseudo_step,
    mean_source,
    harm_order,
):
    cells = mean_adjoint.shape[1]
    groups = cells // LANES
    halves = groups // SUBS
    rim_rows = face_tiles.shape[1] // LANES
    odd = (lax.axis_index("cells") % 2).astype(jnp.int32)[None]
    step = pseudo_step.reshape(groups, LANES)
    pays = (struct(ROWS, rim_rows, LANES), struct(ROWS, rim_rows, LANES), struct(VARS, groups, LANES))
    pay_a, pay_b, stress, tile_idx = launch(
        open_kernel, "open", pays + (struct(2, rim_rows, LANES, dtype=jnp.int32),), (odd,),
        (mean_adjoint, harm_adjoint, harm_flow, face_tiles),
    )
    rim_a, rim_b, parts = exchange(pay_a, pay_b, stress)
    fields = struct(ROWS, groups, LANES)
    acc, index, weight, wsum, start, jac, flow, source = launch(
        prepare_kernel, "prepare",
        (
            fields,
            struct(FACES * halves, SUBS, LANES, dtype=jnp.int32),
            struct(FACES * halves, SUBS, LANES),
            struct(groups, LANES),
            fields,
            struct(VARS * VARS, groups, LANES),
            struct(2 * VARS, groups, LANES),
            struct(VARS, groups, LANES),
        ),
        (odd,),
        (mean_adjoint, harm_adjoint, harm_flow, flux_jacobian, face_weight, face_links, mean_source),
    )
    state, pay_a, pay_b, stress = launch(
        lambda *refs: middle_kernel(*refs, coeff=1.0 / SECTIONS), "middle", (fields,) + pays, (harm_order,),
        (acc, rim_a, rim_b, index, weight, wsum, start, jac, flow, source, step, tile_idx, *parts),
    )
    rim_a, rim_b, parts = exchange(pay_a, pay_b, stress)
    (acc,) = launch(gather_own, "own", (fields,), (), (state, index, weight))
    mean_new, harm_new = launch(
        lambda *refs: close_kernel(*refs, coeff=1.0), "close",
        (struct(VARS, cells), struct(1, 2, VARS, cells)), (harm_order,),
        (acc, rim_a, rim_b, index, weight, wsum, state, start, jac, flow, source, step, *parts),
        scratch=[pltpu.VMEM((ROWS, groups, LANES), F32)],
    )
    return mean_new, harm_new


def solution(mesh):
    finer = Mesh(mesh.devices.reshape(mesh.shape["cells"], 2, 2), ("cells", *HARM))
    return jax.shard_map(
        shards,
        mesh=finer,
        in_specs=(
            P(None, "cells"),
            P(HARM, None, None, "cells"),
            P(HARM, None, None, "cells"),
            P(None, None, "cells"),
            P(None, "cells"),
            P(None, "cells"),
            P(None, "cells"),
            P("cells"),
            P(None, "cells"),
            P(HARM),
        ),
        out_specs=(P(None, "cells"), P(HARM, None, None, "cells")),
        check_vma=False,
    )
```

```python
import jax
import jax.numpy as jnp
from jax import lax
from jax.experimental import pallas as pl
from jax.experimental.pallas import tpu as pltpu
from jax.sharding import Mesh
from jax.sharding import PartitionSpec as P

VARS = 5
FACES = 6
SECTIONS = 2
ROWS = 3 * VARS
HARM = ("harm_0", "harm_1")
LANES = 128
SUBS = 8
BASE_FREQ = 0.8
F32 = jnp.float32


def struct(*shape, dtype=F32):
    return pltpu.VMEM(shape, dtype)


def spread(row):
    return jnp.broadcast_to(row, (SUBS, LANES))


def packed(tile, first):
    sub = lax.broadcasted_iota(jnp.int32, (SUBS, LANES), 0)
    out = spread(tile(first))
    for i in range(1, SUBS):
        out = jnp.where(sub == i, spread(tile(first + i)), out)
    return out


def picked(row, count, index):
    low = index & (LANES - 1)
    high = index >> 7
    out = [None] * ROWS
    for h in range(count):
        hit = high == h
        for r in range(ROWS):
            value = jnp.take_along_axis(spread(row(r, h)), low, axis=1)
            out[r] = jnp.where(hit, value, 0.0 if h == 0 else out[r])
    return out


def store_tiles(row, tile_index, pay_a, pay_b, rows):
    for pay, index in zip((pay_a, pay_b), tile_index):
        for r, value in enumerate(picked(row, rows, index)):
            pay[r] = value


def native_row(mean_ref, harm_ref):
    def row(r, h):
        lanes = slice(h * LANES, (h + 1) * LANES)
        if r < VARS:
            return mean_ref[r : r + 1, lanes]
        part, var = divmod(r - VARS, VARS)
        return harm_ref[var, part : part + 1, lanes]

    return row


def fetch(sources, targets, sems):
    copies = [pltpu.make_async_copy(s, t, sems.at[i]) for i, (s, t) in enumerate(zip(sources, targets))]
    for copy in copies:
        copy.start()
    return [copy.wait for copy in copies]


def open_kernel(
    odd_ref, mean_hbm, harm_hbm, flow_hbm, tiles_hbm, pay_a, pay_b, stress_ref, tile_idx,
    tiles_ref, mean_ref, harm_ref, flow_ref, sems,
):
    waits = fetch(
        (tiles_hbm, mean_hbm, harm_hbm, flow_hbm), (tiles_ref, mean_ref, harm_ref, flow_ref), sems
    )
    for wait in waits:
        wait()
    groups = mean_ref.shape[1] // LANES
    odd = odd_ref[0] == 1
    lower, upper = (
        packed(lambda t, k=k: tiles_ref[k : k + 1, t * LANES : (t + 1) * LANES], 0) for k in range(2)
    )
    first = jnp.where(odd, lower, upper)
    second = jnp.where(odd, upper, lower)
    tile_idx[0] = first
    tile_idx[1] = second
    row = native_row(mean_ref, harm_ref)
    store_tiles(row, (first, second), pay_a, pay_b, groups)
    flow = native_row(mean_ref, flow_ref)
    for v in range(VARS):
        for g in range(0, groups, SUBS):
            part = packed(
                lambda t: row(VARS + v, t) * flow(VARS + v, t) + row(2 * VARS + v, t) * flow(2 * VARS + v, t), g
            )
            stress_ref[v, g : g + SUBS, :] = part


def gather_into(row, count, first, index_ref, weight_ref, start):
    halves = index_ref.shape[0] // FACES
    out = []
    for g in range(halves):

        def face(f, acc):
            values = picked(row, count, index_ref[f * halves + g] - first)
            weight = weight_ref[f * halves + g]
            return tuple(a + weight * v for a, v in zip(acc, values))

        out.append(lax.fori_loop(0, FACES, face, tuple(start(r, g) for r in range(ROWS))))
    return out


def prepare_kernel(
    odd_ref, mean_hbm, harm_hbm, flow_hbm, jac_hbm, weight_hbm, links_hbm, source_hbm, step_hbm,
    acc_ref, index_ref, weight_ref, wsum_ref, state_ref, jac_out, flow_out, source_out, step_out,
    links_ref, weight_in, mean_ref, harm_ref, flow_ref, source_ref, jac_ref, sems,
):
    waits = fetch(
        (links_hbm, weight_hbm, mean_hbm, harm_hbm, flow_hbm, source_hbm, jac_hbm, step_hbm),
        (links_ref, weight_in, mean_ref, harm_ref, flow_ref, source_ref, jac_ref, step_out),
        sems,
    )
    for wait in waits[:2]:
        wait()
    groups = mean_ref.shape[1] // LANES
    halves = groups // SUBS
    even = odd_ref[0] == 0
    rim = groups * LANES
    for g in range(halves):
        total = None
        for f in range(FACES):
            lane = lambda t: slice(t * LANES, (t + 1) * LANES)
            link = packed(lambda t: links_ref[f : f + 1, lane(t)], g * SUBS)
            flipped = jnp.where(link >= rim, link ^ (rim // 2), link)
            index_ref[f * halves + g] = jnp.where(even, flipped, link)
            weight = packed(lambda t: weight_in[f : f + 1, lane(t)], g * SUBS)
            weight_ref[f * halves + g] = weight
            total = weight if total is None else total + weight
        wsum_ref[g * SUBS : (g + 1) * SUBS, :] = total
    row = native_row(mean_ref, harm_ref)
    flow = native_row(mean_ref, flow_ref)
    for wait in waits[2:4]:
        wait()
    for g in range(0, groups, SUBS):
        for r in range(ROWS):
            state_ref[r, g : g + SUBS, :] = packed(lambda t: row(r, t), g)
    gather_own(state_ref, index_ref, weight_ref, acc_ref)
    for wait in waits[4:]:
        wait()
    for g in range(0, groups, SUBS):
        at = slice(g, g + SUBS)
        for r in range(2 * VARS):
            flow_out[r, at, :] = packed(lambda t: flow(VARS + r, t), g)
        for v in range(VARS):
            source_out[v, at, :] = packed(lambda t: source_ref[v : v + 1, t * LANES : (t + 1) * LANES], g)
        for j in range(VARS):
            for i in range(VARS):
                jac_out[j * VARS + i, at, :] = packed(
                    lambda t: jac_ref[j, i : i + 1, t * LANES : (t + 1) * LANES], g
                )


def gather_own(state_ref, index_ref, weight_ref, acc_ref):
    zero = jnp.zeros((SUBS, LANES), F32)
    row = lambda r, h: state_ref[r, h : h + 1, :]
    out = gather_into(row, state_ref.shape[1], 0, index_ref, weight_ref, lambda r, g: zero)
    for g, values in enumerate(out):
        for r in range(ROWS):
            acc_ref[r, g * SUBS : (g + 1) * SUBS, :] = values[r]


def new_state(
    coeff, order_ref, acc_ref, rim_a, rim_b, index_ref, weight_ref, wsum_ref, state_ref, start_ref,
    jac_ref, flow_ref, source_ref, step_ref, stress_refs, out_ref,
):
    groups = acc_ref.shape[1]
    rim_rows = rim_a.shape[1]

    def row(r, h):
        ref = rim_a if h < rim_rows else rim_b
        h = h % rim_rows
        return ref[r, h : h + 1, :]

    omega = BASE_FREQ * (order_ref[0].astype(F32) + 1.0)
    gathered = gather_into(
        row, 2 * rim_rows, groups * LANES, index_ref, weight_ref,
        lambda r, g: acc_ref[r, g * SUBS : (g + 1) * SUBS, :],
    )
    for g in range(groups // SUBS):
        at = slice(g * SUBS, (g + 1) * SUBS)
        state = [state_ref[r, at, :] for r in range(ROWS)]
        wsum = wsum_ref[at, :]
        flux = [wsum * s - x for s, x in zip(state, gathered[g])]
        scale = coeff * step_ref[at, :]
        for v in range(VARS):
            total = stress_refs[0][v, at, :]
            for ref in stress_refs[1:]:
                total = total + ref[v, at, :]
            flux[v] = flux[v] - total
        for part in range(3):
            for i in range(VARS):
                r = part * VARS + i
                res = jac_ref[i, at, :] * flux[part * VARS]
                for j in range(1, VARS):
                    res = res + jac_ref[j * VARS + i, at, :] * flux[part * VARS + j]
                if part == 0:
                    res = res - source_ref[i, at, :]
                else:
                    other = state[(3 - part) * VARS + i]
                    turned = omega * other
                    res = res + turned if part == 1 else res - turned
                    res = res - state[i] * flow_ref[(part - 1) * VARS + i, at, :]
                out_ref[r, at, :] = start_ref[r, at, :] - scale * res


def middle_kernel(
    order_ref, acc_ref, rim_a, rim_b, index_ref, weight_ref, wsum_ref, state_ref,
    jac_ref, flow_ref, source_ref, step_ref, tile_idx, s0, s1,
    out_ref, pay_a, pay_b, stress_ref, *, coeff,
):
    new_state(
        coeff, order_ref, acc_ref, rim_a, rim_b, index_ref, weight_ref, wsum_ref, state_ref, state_ref,
        jac_ref, flow_ref, source_ref, step_ref, (s0, s1), out_ref,
    )
    groups = acc_ref.shape[1]
    store_tiles(lambda r, h: out_ref[r, h : h + 1, :], (tile_idx[0], tile_idx[1]), pay_a, pay_b, groups)
    for v in range(VARS):
        stress_ref[v] = out_ref[VARS + v] * flow_ref[v] + out_ref[2 * VARS + v] * flow_ref[VARS + v]


def close_kernel(
    order_ref, acc_ref, rim_a, rim_b, index_ref, weight_ref, wsum_ref, state_ref, start_ref,
    jac_ref, flow_ref, source_ref, step_ref, s0, s1,
    mean_hbm, harm_hbm, out_ref, mean_out, harm_out, sems, *, coeff,
):
    new_state(
        coeff, order_ref, acc_ref, rim_a, rim_b, index_ref, weight_ref, wsum_ref, state_ref, start_ref,
        jac_ref, flow_ref, source_ref, step_ref, (s0, s1), out_ref,
    )
    for t in range(acc_ref.shape[1]):
        lanes = slice(t * LANES, (t + 1) * LANES)
        mean_out[:, lanes] = stacked(lambda i: out_ref[i, t : t + 1, :], VARS)
    mean_copy = pltpu.make_async_copy(mean_out, mean_hbm, sems.at[0])
    mean_copy.start()
    for t in range(acc_ref.shape[1]):
        lanes = slice(t * LANES, (t + 1) * LANES)
        for v in range(VARS):
            harm_out[v, :, lanes] = stacked(lambda i: out_ref[(i + 1) * VARS + v, t : t + 1, :], 2)
    harm_copy = pltpu.make_async_copy(harm_out, harm_hbm, sems.at[1])
    harm_copy.start()
    mean_copy.wait()
    harm_copy.wait()


def stacked(row, count):
    sub = lax.broadcasted_iota(jnp.int32, (count, LANES), 0)
    out = jnp.broadcast_to(row(0), (count, LANES))
    for i in range(1, count):
        out = jnp.where(sub == i, jnp.broadcast_to(row(i), (count, LANES)), out)
    return out


def held(*arrays):
    return [*(pltpu.VMEM(a.shape, a.dtype) for a in arrays), pltpu.SemaphoreType.DMA((SUBS,))]


def launch(body, name, out_shape, scalars, args, raw=(), scratch=()):
    smem = pl.BlockSpec(memory_space=pltpu.SMEM)
    vmem = pl.BlockSpec(memory_space=pltpu.VMEM)
    anywhere = pl.BlockSpec(memory_space=pl.ANY)
    return pl.pallas_call(
        body,
        name=name,
        out_shape=out_shape,
        in_specs=[smem] * len(scalars) + [anywhere] * len(raw) + [vmem] * len(args),
        out_specs=[anywhere if isinstance(s, jax.ShapeDtypeStruct) else vmem for s in out_shape],
        scratch_shapes=scratch,
    )(*scalars, *raw, *(pltpu.with_memory_space_constraint(a, pltpu.VMEM) for a in args))


def exchange(pay_a, pay_b, stress):
    count = lax.axis_size("cells")
    near = [(b, b ^ 1) for b in range(count)]
    far = [(b, (b - 1 + 2 * (b % 2)) % count) for b in range(count)]
    rim_b = lax.ppermute(pay_b, "cells", far)
    rim_a = lax.ppermute(pay_a, "cells", near)
    swap = [(0, 1), (1, 0)]
    chip = stress + lax.ppermute(stress, HARM[1], swap)
    return rim_a, rim_b, (chip, lax.ppermute(chip, HARM[0], swap))


def shards(
    mean_adjoint,
    harm_adjoint,
    harm_flow,
    flux_jacobian,
    face_weight,
    face_links,
    face_tiles,
    pseudo_step,
    mean_source,
    harm_order,
):
    cells = mean_adjoint.shape[1]
    groups = cells // LANES
    halves = groups // SUBS
    rim_rows = face_tiles.shape[1] // LANES
    harm_adjoint, harm_flow = (
        a[0].swapaxes(0, 1) for a in (harm_adjoint, harm_flow)
    )
    odd = (lax.axis_index("cells") % 2).astype(jnp.int32)[None]
    step = pseudo_step.reshape(groups, LANES)
    pays = (struct(ROWS, rim_rows, LANES), struct(ROWS, rim_rows, LANES), struct(VARS, groups, LANES))
    pay_a, pay_b, stress, tile_idx = launch(
        open_kernel, "open", pays + (struct(2, rim_rows, LANES, dtype=jnp.int32),), (odd,), (),
        (mean_adjoint, harm_adjoint, harm_flow, face_tiles),
        held(face_tiles, mean_adjoint, harm_adjoint, harm_flow),
    )
    rim_a, rim_b, parts = exchange(pay_a, pay_b, stress)
    fields = struct(ROWS, groups, LANES)
    acc, index, weight, wsum, start, jac, flow, source, step = launch(
        prepare_kernel, "prepare",
        (
            fields,
            struct(FACES * halves, SUBS, LANES, dtype=jnp.int32),
            struct(FACES * halves, SUBS, LANES),
            struct(groups, LANES),
            fields,
            struct(VARS * VARS, groups, LANES),
            struct(2 * VARS, groups, LANES),
            struct(VARS, groups, LANES),
            struct(groups, LANES),
        ),
        (odd,),
        (),
        (mean_adjoint, harm_adjoint, harm_flow, flux_jacobian, face_weight, face_links, mean_source, step),
        held(face_links, face_weight, mean_adjoint, harm_adjoint, harm_flow, mean_source, flux_jacobian),
    )
    state, pay_a, pay_b, stress = launch(
        lambda *refs: middle_kernel(*refs, coeff=1.0 / SECTIONS), "middle", (fields,) + pays, (harm_order,),
        (acc, rim_a, rim_b, index, weight, wsum, start, jac, flow, source, step, tile_idx, *parts),
    )
    rim_a, rim_b, parts = exchange(pay_a, pay_b, stress)
    (acc,) = launch(gather_own, "own", (fields,), (), (state, index, weight))
    outs = [jax.ShapeDtypeStruct(s, F32) for s in ((VARS, cells), (VARS, 2, cells))]
    mean_new, harm_new = launch(
        lambda *refs: close_kernel(*refs, coeff=1.0), "close",
        tuple(outs), (harm_order,),
        (acc, rim_a, rim_b, index, weight, wsum, state, start, jac, flow, source, step, *parts),
        scratch=[fields, *held(*outs)],
    )
    return mean_new, harm_new.swapaxes(0, 1)[None]


def solution(mesh):
    finer = Mesh(mesh.devices.reshape(mesh.shape["cells"], 2, 2), ("cells", *HARM))
    return jax.shard_map(
        shards,
        mesh=finer,
        in_specs=(
            P(None, "cells"),
            P(HARM, None, None, "cells"),
            P(HARM, None, None, "cells"),
            P(None, None, "cells"),
            P(None, "cells"),
            P(None, "cells"),
            P(None, "cells"),
            P("cells"),
            P(None, "cells"),
            P(HARM),
        ),
        out_specs=(P(None, "cells"), P(HARM, None, None, "cells")),
        check_vma=False,
    )
```

```python
import jax
import jax.numpy as jnp
from jax import lax
from jax.experimental import pallas as pl
from jax.experimental.pallas import tpu as pltpu
from jax.sharding import Mesh
from jax.sharding import PartitionSpec as P

VARS = 5
FACES = 6
SECTIONS = 2
ROWS = 3 * VARS
HARM = ("harm_0", "harm_1")
HARM_DEVICES = 4
LANES = 128
SUBS = 8
BASE_FREQ = 0.8
F32 = jnp.float32


def struct(*shape, dtype=F32):
    return pltpu.VMEM(shape, dtype)


def spread(row):
    return jnp.broadcast_to(row, (SUBS, LANES))


def packed(tile, first):
    sub = lax.broadcasted_iota(jnp.int32, (SUBS, LANES), 0)
    out = spread(tile(first))
    for i in range(1, SUBS):
        out = jnp.where(sub == i, spread(tile(first + i)), out)
    return out


def picked(row, fields, count, index):
    low = index & (LANES - 1)
    high = index >> 7
    out = [None] * len(fields)
    for h in range(count):
        hit = high == h
        for i, r in enumerate(fields):
            value = jnp.take_along_axis(spread(row(r, h)), low, axis=1)
            out[i] = jnp.where(hit, value, 0.0 if h == 0 else out[i])
    return out


def store_tiles(row, tile_index, pay_a, pay_b, rows):
    for pay, index in zip((pay_a, pay_b), tile_index):
        for r, value in enumerate(picked(row, range(ROWS), rows, index)):
            pay[r] = value


def native_row(mean_ref, harm_ref):
    def row(r, h):
        lanes = slice(h * LANES, (h + 1) * LANES)
        if r < VARS:
            return mean_ref[r : r + 1, lanes]
        part, var = divmod(r - VARS, VARS)
        return harm_ref[var, part : part + 1, lanes]

    return row


def fetch(sources, targets, sems):
    copies = [pltpu.make_async_copy(s, t, sems.at[i]) for i, (s, t) in enumerate(zip(sources, targets))]
    for copy in copies:
        copy.start()
    return [copy.wait for copy in copies]


def open_kernel(
    place_ref, mean_hbm, harm_hbm, tiles_hbm, pay_a, pay_b, tile_idx, tiles_ref, mean_ref, harm_ref, sems
):
    for wait in fetch((tiles_hbm, mean_hbm, harm_hbm), (tiles_ref, mean_ref, harm_ref), sems):
        wait()
    lowers_first = place_ref[0] % 2 == 1
    lower, upper = (
        packed(lambda t, k=k: tiles_ref[k : k + 1, t * LANES : (t + 1) * LANES], 0) for k in range(2)
    )
    first = jnp.where(lowers_first, lower, upper)
    second = jnp.where(lowers_first, upper, lower)
    tile_idx[0] = first
    tile_idx[1] = second
    row = native_row(mean_ref, harm_ref)
    store_tiles(row, (first, second), pay_a, pay_b, mean_ref.shape[1] // LANES)


def gather_into(row, fields, count, first, index_ref, weight_ref, begin, faces, start):
    def face(f, acc):
        values = picked(row, fields, count, index_ref[begin + f] - first)
        weight = weight_ref[begin + f]
        return tuple(a + weight * v for a, v in zip(acc, values))

    return lax.fori_loop(0, faces, face, tuple(start))


def share_of(place_ref, index_ref):
    count = index_ref.shape[0] // HARM_DEVICES
    begin = place_ref[0] // 2 * count
    return begin, count, begin // FACES


def gather_fields(row, fields, count, first, index_ref, weight_ref, start, out_ref):
    for g in range(index_ref.shape[0] // FACES):
        at = slice(g * SUBS, (g + 1) * SUBS)
        values = gather_into(
            row, fields, count, first, index_ref, weight_ref, g * FACES, FACES, [start(r, at) for r in fields]
        )
        for r, value in zip(fields, values):
            out_ref[r, at, :] = value


def zero_start(*_):
    return jnp.zeros((SUBS, LANES), F32)


def prepare_kernel(
    place_ref, mean_hbm, harm_hbm, flow_hbm, jac_hbm, weight_hbm, links_hbm, source_hbm, step_hbm,
    acc_ref, share_ref, index_ref, weight_ref, wsum_ref, mean_out, state_ref, jac_out, flow_out, source_out, step_out,
    links_ref, weight_in, mean_ref, harm_ref, flow_ref, source_ref, jac_ref, sems,
):
    waits = fetch(
        (links_hbm, weight_hbm, mean_hbm, harm_hbm, flow_hbm, source_hbm, jac_hbm, step_hbm),
        (links_ref, weight_in, mean_ref, harm_ref, flow_ref, source_ref, jac_ref, step_out),
        sems,
    )
    for wait in waits[:2]:
        wait()
    groups = mean_ref.shape[1] // LANES
    flips = place_ref[0] % 2 == 0
    rim = groups * LANES
    lane = lambda t: slice(t * LANES, (t + 1) * LANES)
    for g in range(groups // SUBS):
        total = None
        for f in range(FACES):
            link = packed(lambda t: links_ref[f : f + 1, lane(t)], g * SUBS)
            flipped = jnp.where(link >= rim, link ^ (rim // 2), link)
            index_ref[g * FACES + f] = jnp.where(flips, flipped, link)
            weight = packed(lambda t: weight_in[f : f + 1, lane(t)], g * SUBS)
            weight_ref[g * FACES + f] = weight
            total = weight if total is None else total + weight
        wsum_ref[g * SUBS : (g + 1) * SUBS, :] = total
    row = native_row(mean_ref, harm_ref)
    flow = native_row(mean_ref, flow_ref)
    for wait in waits[2:4]:
        wait()
    for g in range(0, groups, SUBS):
        at = slice(g, g + SUBS)
        for r in range(VARS):
            mean_out[r, at, :] = packed(lambda t: row(r, t), g)
        for r in range(2 * VARS):
            state_ref[r, at, :] = packed(lambda t: row(VARS + r, t), g)
    gather_fields(
        lambda r, h: state_ref[r, h : h + 1, :], range(2 * VARS), groups, 0, index_ref, weight_ref,
        zero_start, acc_ref,
    )
    begin, count, _ = share_of(place_ref, index_ref)
    values = gather_into(
        lambda r, h: mean_out[r, h : h + 1, :], range(VARS), groups, 0, index_ref, weight_ref,
        begin, count, [zero_start()] * VARS,
    )
    for r, value in enumerate(values):
        share_ref[r] = value
    for wait in waits[4:]:
        wait()
    for g in range(0, groups, SUBS):
        at = slice(g, g + SUBS)
        for r in range(2 * VARS):
            flow_out[r, at, :] = packed(lambda t: flow(VARS + r, t), g)
        for v in range(VARS):
            source_out[v, at, :] = packed(lambda t: source_ref[v : v + 1, lane(t)], g)
        for j in range(VARS):
            for i in range(VARS):
                jac_out[j * VARS + i, at, :] = packed(lambda t: jac_ref[j, i : i + 1, lane(t)], g)


def fields_row(mean_ref, harm_ref):
    def row(r, h):
        return mean_ref[r, h : h + 1, :] if r < VARS else harm_ref[r - VARS, h : h + 1, :]

    return row


def own_kernel(mean_ref, harm_ref, index_ref, weight_ref, acc_ref):
    gather_fields(
        fields_row(mean_ref, harm_ref), range(ROWS), mean_ref.shape[1], 0, index_ref, weight_ref,
        zero_start, acc_ref,
    )


def rim_row(rim_a, rim_b, lead=0):
    rows = rim_a.shape[1]

    def row(r, h):
        ref = rim_a if h < rows else rim_b
        h = h % rows
        return ref[lead + r, h : h + 1, :]

    return row


def transposed(jac_ref, at, flux):
    out = []
    for i in range(VARS):
        res = jac_ref[i, at, :] * flux[0]
        for j in range(1, VARS):
            res = res + jac_ref[j * VARS + i, at, :] * flux[j]
        out.append(res)
    return out


def harm_step(order_ref, at, mean, state, start, gathered, wsum, scale, jac_ref, flow_ref, out_ref):
    omega = BASE_FREQ * (order_ref[0].astype(F32) + 1.0)
    flux = [wsum * s - x for s, x in zip(state, gathered)]
    for part in range(2):
        res = transposed(jac_ref, at, flux[part * VARS : (part + 1) * VARS])
        for i in range(VARS):
            r = part * VARS + i
            turned = omega * state[(1 - part) * VARS + i]
            full = res[i] + turned if part == 0 else res[i] - turned
            full = full - mean[i] * flow_ref[r, at, :]
            out_ref[r, at, :] = start[r] - scale * full


def middle_kernel(
    place_ref, order_ref, acc_ref, share_ref, rim_a, rim_b, index_ref, weight_ref, wsum_ref, mean_ref, state_ref,
    jac_ref, flow_ref, source_ref, step_ref, out_ref, part_ref, full_ref, mean_acc, *, coeff,
):
    groups = acc_ref.shape[1]
    rim_rows = rim_a.shape[1]
    begin, count, half = share_of(place_ref, index_ref)
    lead = place_ref[0] // 2 == 0
    gather_fields(
        rim_row(rim_a, rim_b, VARS), range(2 * VARS), 2 * rim_rows, groups * LANES, index_ref, weight_ref,
        lambda r, at: acc_ref[r, at, :], full_ref,
    )
    values = gather_into(
        rim_row(rim_a, rim_b), range(VARS), 2 * rim_rows, groups * LANES, index_ref, weight_ref,
        begin, count, [share_ref[r] for r in range(VARS)],
    )
    mean_acc[...] = jnp.zeros(mean_acc.shape, F32)
    for r, value in enumerate(values):
        mean_acc[r, pl.ds(pl.multiple_of(half * SUBS, SUBS), SUBS), :] = value
    for g in range(groups // SUBS):
        at = slice(g * SUBS, (g + 1) * SUBS)
        mean = [mean_ref[v, at, :] for v in range(VARS)]
        state = [state_ref[r, at, :] for r in range(2 * VARS)]
        wsum = wsum_ref[at, :]
        scale = coeff * step_ref[at, :]
        flux = []
        for v in range(VARS):
            stress = state[v] * flow_ref[v, at, :] + state[VARS + v] * flow_ref[VARS + v, at, :]
            flux.append(jnp.where(lead, wsum * mean[v], 0.0) - mean_acc[v, at, :] - stress)
        for v, res in enumerate(transposed(jac_ref, at, flux)):
            own = jnp.where(lead, mean[v] + scale * source_ref[v, at, :], 0.0)
            part_ref[v, at, :] = own - scale * res
        gathered = [full_ref[r, at, :] for r in range(2 * VARS)]
        harm_step(order_ref, at, mean, state, state, gathered, wsum, scale, jac_ref, flow_ref, out_ref)
        for v in range(VARS):
            part_ref[VARS + v, at, :] = (
                out_ref[v, at, :] * flow_ref[v, at, :] + out_ref[VARS + v, at, :] * flow_ref[VARS + v, at, :]
            )


def join_kernel(parts_ref, state_ref, tile_idx, mean_ref, stress_ref, pay_a, pay_b):
    for v in range(VARS):
        for ref, r in ((mean_ref, v), (stress_ref, VARS + v)):
            total = parts_ref[0, r]
            for k in range(1, HARM_DEVICES):
                total = total + parts_ref[k, r]
            ref[v] = total
    row = fields_row(mean_ref, state_ref)
    store_tiles(row, (tile_idx[0], tile_idx[1]), pay_a, pay_b, mean_ref.shape[1])


def close_kernel(
    order_ref, acc_ref, rim_a, rim_b, index_ref, weight_ref, wsum_ref, mean_ref, state_ref, mean_start, harm_start,
    jac_ref, flow_ref, source_ref, step_ref, stress_ref,
    mean_hbm, harm_hbm, full_ref, new_mean, new_harm, mean_out, harm_out, sems, *, coeff,
):
    groups = acc_ref.shape[1]
    gather_fields(
        rim_row(rim_a, rim_b), range(ROWS), 2 * rim_a.shape[1], groups * LANES, index_ref, weight_ref,
        lambda r, at: acc_ref[r, at, :], full_ref,
    )
    for g in range(groups // SUBS):
        at = slice(g * SUBS, (g + 1) * SUBS)
        mean = [mean_ref[v, at, :] for v in range(VARS)]
        state = [state_ref[r, at, :] for r in range(2 * VARS)]
        wsum = wsum_ref[at, :]
        scale = coeff * step_ref[at, :]
        flux = [wsum * m - full_ref[v, at, :] - stress_ref[v, at, :] for v, m in enumerate(mean)]
        for v, res in enumerate(transposed(jac_ref, at, flux)):
            new_mean[v, at, :] = mean_start[v, at, :] - scale * (res - source_ref[v, at, :])
        gathered = [full_ref[VARS + r, at, :] for r in range(2 * VARS)]
        start = [harm_start[r, at, :] for r in range(2 * VARS)]
        harm_step(order_ref, at, mean, state, start, gathered, wsum, scale, jac_ref, flow_ref, new_harm)
    for t in range(groups):
        lanes = slice(t * LANES, (t + 1) * LANES)
        mean_out[:, lanes] = stacked(lambda i: new_mean[i, t : t + 1, :], VARS)
    mean_copy = pltpu.make_async_copy(mean_out, mean_hbm, sems.at[0])
    mean_copy.start()
    for t in range(groups):
        lanes = slice(t * LANES, (t + 1) * LANES)
        for v in range(VARS):
            harm_out[v, :, lanes] = stacked(lambda i: new_harm[i * VARS + v, t : t + 1, :], 2)
    harm_copy = pltpu.make_async_copy(harm_out, harm_hbm, sems.at[1])
    harm_copy.start()
    mean_copy.wait()
    harm_copy.wait()


def stacked(row, count):
    sub = lax.broadcasted_iota(jnp.int32, (count, LANES), 0)
    out = jnp.broadcast_to(row(0), (count, LANES))
    for i in range(1, count):
        out = jnp.where(sub == i, jnp.broadcast_to(row(i), (count, LANES)), out)
    return out


def held(*arrays):
    return [*(pltpu.VMEM(a.shape, a.dtype) for a in arrays), pltpu.SemaphoreType.DMA((SUBS,))]


def launch(body, name, out_shape, scalars, args, raw=(), scratch=()):
    smem = pl.BlockSpec(memory_space=pltpu.SMEM)
    vmem = pl.BlockSpec(memory_space=pltpu.VMEM)
    anywhere = pl.BlockSpec(memory_space=pl.ANY)
    return pl.pallas_call(
        body,
        name=name,
        out_shape=out_shape,
        in_specs=[smem] * len(scalars) + [anywhere] * len(raw) + [vmem] * len(args),
        out_specs=[anywhere if isinstance(s, jax.ShapeDtypeStruct) else vmem for s in out_shape],
        scratch_shapes=scratch,
    )(*scalars, *raw, *(pltpu.with_memory_space_constraint(a, pltpu.VMEM) for a in args))


def exchange(pay_a, pay_b):
    count = lax.axis_size("cells")
    near = [(b, b ^ 1) for b in range(count)]
    far = [(b, (b - 1 + 2 * (b % 2)) % count) for b in range(count)]
    return lax.ppermute(pay_a, "cells", far), lax.ppermute(pay_b, "cells", near)


def shards(
    mean_adjoint,
    harm_adjoint,
    harm_flow,
    flux_jacobian,
    face_weight,
    face_links,
    face_tiles,
    pseudo_step,
    mean_source,
    harm_order,
):
    cells = mean_adjoint.shape[1]
    groups = cells // LANES
    halves = groups // SUBS
    rim_rows = face_tiles.shape[1] // LANES
    harm_adjoint, harm_flow = (
        a[0].swapaxes(0, 1) for a in (harm_adjoint, harm_flow)
    )
    place = (1 - lax.axis_index("cells") % 2 + 2 * lax.axis_index(HARM)).astype(jnp.int32)[None]
    step = pseudo_step.reshape(groups, LANES)
    mean_fields, harm_fields = struct(VARS, groups, LANES), struct(2 * VARS, groups, LANES)
    pays = (struct(ROWS, rim_rows, LANES), struct(ROWS, rim_rows, LANES))
    pay_a, pay_b, tile_idx = launch(
        open_kernel, "open", pays + (struct(2, rim_rows, LANES, dtype=jnp.int32),), (place,), (),
        (mean_adjoint, harm_adjoint, face_tiles),
        held(face_tiles, mean_adjoint, harm_adjoint),
    )
    rim_a, rim_b = exchange(pay_a, pay_b)
    registers = FACES * halves
    acc, share, index, weight, wsum, mean_start, harm_start, jac, flow, source, step = launch(
        prepare_kernel, "prepare",
        (
            harm_fields,
            struct(VARS, SUBS, LANES),
            struct(registers, SUBS, LANES, dtype=jnp.int32),
            struct(registers, SUBS, LANES),
            struct(groups, LANES),
            mean_fields,
            harm_fields,
            struct(VARS * VARS, groups, LANES),
            harm_fields,
            mean_fields,
            struct(groups, LANES),
        ),
        (place,),
        (),
        (mean_adjoint, harm_adjoint, harm_flow, flux_jacobian, face_weight, face_links, mean_source, step),
        held(face_links, face_weight, mean_adjoint, harm_adjoint, harm_flow, mean_source, flux_jacobian),
    )
    state, part = launch(
        lambda *refs: middle_kernel(*refs, coeff=1.0 / SECTIONS), "middle", (harm_fields, harm_fields),
        (place, harm_order),
        (acc, share, rim_a, rim_b, index, weight, wsum, mean_start, harm_start, jac, flow, source, step),
        scratch=[harm_fields, mean_fields],
    )
    parts = lax.all_gather(part, HARM)
    mean, stress, pay_a, pay_b = launch(
        join_kernel, "join", (mean_fields, mean_fields) + pays, (), (parts, state, tile_idx)
    )
    rim_a, rim_b = exchange(pay_a, pay_b)
    fields = struct(ROWS, groups, LANES)
    (acc,) = launch(own_kernel, "own", (fields,), (), (mean, state, index, weight))
    outs = [jax.ShapeDtypeStruct(s, F32) for s in ((VARS, cells), (VARS, 2, cells))]
    mean_new, harm_new = launch(
        lambda *refs: close_kernel(*refs, coeff=1.0), "close", tuple(outs), (harm_order,),
        (acc, rim_a, rim_b, index, weight, wsum, mean, state, mean_start, harm_start,
         jac, flow, source, step, stress),
        scratch=[fields, mean_fields, harm_fields, *held(*outs)],
    )
    return mean_new, harm_new.swapaxes(0, 1)[None]


def solution(mesh):
    finer = Mesh(mesh.devices.reshape(mesh.shape["cells"], 2, 2), ("cells", *HARM))
    return jax.shard_map(
        shards,
        mesh=finer,
        in_specs=(
            P(None, "cells"),
            P(HARM, None, None, "cells"),
            P(HARM, None, None, "cells"),
            P(None, None, "cells"),
            P(None, "cells"),
            P(None, "cells"),
            P(None, "cells"),
            P("cells"),
            P(None, "cells"),
            P(HARM),
        ),
        out_specs=(P(None, "cells"), P(HARM, None, None, "cells")),
        check_vma=False,
    )
```

```python
import jax
import jax.numpy as jnp
from jax import lax
from jax.experimental import pallas as pl
from jax.experimental.pallas import tpu as pltpu
from jax.sharding import Mesh
from jax.sharding import PartitionSpec as P

VARS = 5
FACES = 6
SECTIONS = 2
ROWS = 3 * VARS
MEAN_FIELDS = range(VARS)
HARM_FIELDS = range(VARS, ROWS)
ALL_FIELDS = range(ROWS)
HARM = ("harm_0", "harm_1")
HARM_DEVICES = 4
LANES = 128
SUBS = 8
BASE_FREQ = 0.8
F32 = jnp.float32


def struct(*shape, dtype=F32):
    return pltpu.VMEM(shape, dtype)


def spread(row):
    return jnp.broadcast_to(row, (SUBS, LANES))


def packed(tile, first):
    sub = lax.broadcasted_iota(jnp.int32, (SUBS, LANES), 0)
    out = spread(tile(first))
    for i in range(1, SUBS):
        out = jnp.where(sub == i, spread(tile(first + i)), out)
    return out


def picked(row, fields, count, index):
    low = index & (LANES - 1)
    high = index >> 7
    out = [None] * len(fields)
    for h in range(count):
        hit = high == h
        for i, r in enumerate(fields):
            value = jnp.take_along_axis(spread(row(r, h)), low, axis=1)
            out[i] = jnp.where(hit, value, jnp.zeros_like(value) if h == 0 else out[i])
    return out


def store_tiles(row, tile_index, pay_a, pay_b, rows):
    for pay, index in zip((pay_a, pay_b), tile_index):
        for r, value in enumerate(picked(row, range(ROWS), rows, index)):
            pay[r] = value


def native_row(mean_ref, harm_ref):
    def row(r, h):
        lanes = slice(h * LANES, (h + 1) * LANES)
        if r < VARS:
            return mean_ref[r : r + 1, lanes]
        part, var = divmod(r - VARS, VARS)
        return harm_ref[var, part : part + 1, lanes]

    return row


def fetch(sources, targets, sems):
    copies = [pltpu.make_async_copy(s, t, sems.at[i]) for i, (s, t) in enumerate(zip(sources, targets))]
    for copy in copies:
        copy.start()
    return [copy.wait for copy in copies]


def open_kernel(
    place_ref, tiles_hbm, mean_hbm, harm_hbm, links_hbm, weight_hbm, flow_hbm, jac_hbm, source_hbm, step_hbm,
    pay_a, pay_b, tile_idx, mean_ref, harm_ref, links_ref, weight_ref, flow_ref, jac_ref, source_ref, step_ref,
    tiles_ref, sems,
):
    waits = fetch(
        (tiles_hbm, mean_hbm, harm_hbm, links_hbm, weight_hbm, flow_hbm, jac_hbm, source_hbm, step_hbm),
        (tiles_ref, mean_ref, harm_ref, links_ref, weight_ref, flow_ref, jac_ref, source_ref, step_ref),
        sems,
    )
    for wait in waits[:3]:
        wait()
    lowers_first = place_ref[0] % 2 == 1
    lower, upper = (
        packed(lambda t, k=k: tiles_ref[k : k + 1, t * LANES : (t + 1) * LANES], 0) for k in range(2)
    )
    first = jnp.where(lowers_first, lower, upper)
    second = jnp.where(lowers_first, upper, lower)
    tile_idx[0] = first
    tile_idx[1] = second
    row = native_row(mean_ref, harm_ref)
    store_tiles(row, (first, second), pay_a, pay_b, mean_ref.shape[1] // LANES)
    for wait in waits[3:]:
        wait()


TOP = float(2**20 - 1)


def largest(values):
    top = jnp.abs(values[0])
    for value in values[1:]:
        top = jnp.maximum(top, jnp.abs(value))
    top = jnp.max(jnp.max(top, axis=0, keepdims=True), axis=1, keepdims=True)
    return jnp.maximum(jnp.broadcast_to(top, (SUBS, LANES)), 1e-30)


def pack_table(load, blocks, fields, words_ref):
    unit = {}
    scale = {}
    for kind in ([r for r in fields if r < VARS], [r for r in fields if r >= VARS]):
        if kind:
            top = largest([load(r, g) for r in kind for g in range(blocks)])
            for r in kind:
                unit[r] = top * (1.0 / TOP)
                scale[r] = TOP / top
    fixed = lambda r, g: jnp.floor(load(r, g) * scale[r] + 0.5).astype(jnp.int32)
    for i in range(len(fields) // 3):
        for g in range(blocks):
            at = slice(g * SUBS, (g + 1) * SUBS)
            first, second, third = (fixed(r, g) for r in fields[3 * i : 3 * i + 3])
            words_ref[2 * i, at, :] = (first << 11) | ((third >> 10) & 0x7FF)
            words_ref[2 * i + 1, at, :] = (second << 11) | (third & 0x3FF)
    return unit


def gather_into(row, fields, count, words_ref, first, index_ref, weight_ref, begin, faces, unit, start):
    triples = len(fields) // 3
    words = 2 * triples
    rest = fields[3 * triples :]

    def word(w, h):
        return words_ref[w, h : h + 1, :] if w < words else row(rest[w - words], h)

    def face(f, acc):
        found = picked(word, range(words + len(rest)), count, index_ref[begin + f] - first)
        weight = weight_ref[begin + f]
        values = []
        for i in range(triples):
            one, two = found[2 * i], found[2 * i + 1]
            values += [one >> 11, two >> 11, ((one << 21) >> 11) | (two & 0x3FF)]
        values = [v.astype(F32) for v in values] + found[words:]
        return tuple(a + weight * v for a, v in zip(acc, values))

    sums = lax.fori_loop(0, faces, face, (jnp.zeros((SUBS, LANES), F32),) * len(fields))
    return [
        s + (a if i >= 3 * triples else unit[r] * a) for i, (r, s, a) in enumerate(zip(fields, start, sums))
    ]


def share_of(place_ref, index_ref):
    count = index_ref.shape[0] // HARM_DEVICES
    begin = place_ref[0] // 2 * count
    return begin, count, begin // FACES


def gather_fields(row, fields, count, words_ref, first, index_ref, weight_ref, unit, start, out_ref, lead=0):
    for g in range(index_ref.shape[0] // FACES):
        at = slice(g * SUBS, (g + 1) * SUBS)
        values = gather_into(
            row, fields, count, words_ref, first, index_ref, weight_ref, g * FACES, FACES, unit,
            [start(r - lead, at) for r in fields],
        )
        for r, value in zip(fields, values):
            out_ref[r - lead, at, :] = value


def zero_start(*_):
    return jnp.zeros((SUBS, LANES), F32)


def prepare_kernel(
    place_ref, mean_ref, harm_ref, links_ref, weight_in, flow_ref, jac_ref, source_ref,
    acc_ref, share_ref, index_ref, weight_ref, wsum_ref, mean_out, state_ref, jac_out, flow_out, source_out,
    words_ref, mean_words,
):
    groups = mean_ref.shape[1] // LANES
    flips = place_ref[0] % 2 == 0
    rim = groups * LANES
    lane = lambda t: slice(t * LANES, (t + 1) * LANES)
    for g in range(groups // SUBS):
        total = None
        for f in range(FACES):
            link = packed(lambda t: links_ref[f : f + 1, lane(t)], g * SUBS)
            flipped = jnp.where(link >= rim, link ^ (rim // 2), link)
            index_ref[g * FACES + f] = jnp.where(flips, flipped, link)
            weight = packed(lambda t: weight_in[f : f + 1, lane(t)], g * SUBS)
            weight_ref[g * FACES + f] = weight
            total = weight if total is None else total + weight
        wsum_ref[g * SUBS : (g + 1) * SUBS, :] = total
    row = native_row(mean_ref, harm_ref)
    flow = native_row(mean_ref, flow_ref)
    for g in range(0, groups, SUBS):
        at = slice(g, g + SUBS)
        for r in range(VARS):
            mean_out[r, at, :] = packed(lambda t: row(r, t), g)
        for r in range(2 * VARS):
            state_ref[r, at, :] = packed(lambda t: row(VARS + r, t), g)
    row = fields_row(mean_out, state_ref)
    load = fields_block(mean_out, state_ref)
    unit = pack_table(load, groups // SUBS, HARM_FIELDS, words_ref)
    mean_unit = pack_table(load, groups // SUBS, MEAN_FIELDS, mean_words)
    gather_fields(
        row, HARM_FIELDS, groups, words_ref, 0, index_ref, weight_ref, unit, zero_start, acc_ref, VARS
    )
    begin, count, _ = share_of(place_ref, index_ref)
    values = gather_into(
        row, MEAN_FIELDS, groups, mean_words, 0, index_ref, weight_ref, begin, count, mean_unit,
        [zero_start()] * VARS,
    )
    for r, value in enumerate(values):
        share_ref[r] = value
    for g in range(0, groups, SUBS):
        at = slice(g, g + SUBS)
        for r in range(2 * VARS):
            flow_out[r, at, :] = packed(lambda t: flow(VARS + r, t), g)
        for v in range(VARS):
            source_out[v, at, :] = packed(lambda t: source_ref[v : v + 1, lane(t)], g)
        for j in range(VARS):
            for i in range(VARS):
                jac_out[j * VARS + i, at, :] = packed(lambda t: jac_ref[j, i : i + 1, lane(t)], g)


def fields_row(mean_ref, harm_ref):
    def row(r, h):
        return mean_ref[r, h : h + 1, :] if r < VARS else harm_ref[r - VARS, h : h + 1, :]

    return row


def fields_block(mean_ref, harm_ref):
    def load(r, g):
        at = slice(g * SUBS, (g + 1) * SUBS)
        return mean_ref[r, at, :] if r < VARS else harm_ref[r - VARS, at, :]

    return load


def own_kernel(mean_ref, harm_ref, index_ref, weight_ref, acc_ref, words_ref):
    groups = mean_ref.shape[1]
    unit = pack_table(fields_block(mean_ref, harm_ref), groups // SUBS, ALL_FIELDS, words_ref)
    gather_fields(
        fields_row(mean_ref, harm_ref), ALL_FIELDS, groups, words_ref, 0, index_ref, weight_ref, unit,
        zero_start, acc_ref,
    )


def rim_row(rim_a, rim_b):
    rows = rim_a.shape[1]

    def row(r, h):
        ref = rim_a if h < rows else rim_b
        h = h % rows
        return ref[r, h : h + 1, :]

    return row


def rim_block(rim_a, rim_b):
    blocks = rim_a.shape[1] // SUBS

    def load(r, g):
        ref = rim_a if g < blocks else rim_b
        g = g % blocks
        return ref[r, g * SUBS : (g + 1) * SUBS, :]

    return load


def transposed(jac_ref, at, flux):
    out = []
    for i in range(VARS):
        res = jac_ref[i, at, :] * flux[0]
        for j in range(1, VARS):
            res = res + jac_ref[j * VARS + i, at, :] * flux[j]
        out.append(res)
    return out


def harm_step(order_ref, at, mean, state, start, gathered, wsum, scale, jac_ref, flow_ref, out_ref):
    omega = BASE_FREQ * (order_ref[0].astype(F32) + 1.0)
    flux = [wsum * s - x for s, x in zip(state, gathered)]
    for part in range(2):
        res = transposed(jac_ref, at, flux[part * VARS : (part + 1) * VARS])
        for i in range(VARS):
            r = part * VARS + i
            turned = omega * state[(1 - part) * VARS + i]
            full = res[i] + turned if part == 0 else res[i] - turned
            full = full - mean[i] * flow_ref[r, at, :]
            out_ref[r, at, :] = start[r] - scale * full


def middle_kernel(
    place_ref, order_ref, acc_ref, share_ref, rim_a, rim_b, index_ref, weight_ref, wsum_ref, mean_ref, state_ref,
    jac_ref, flow_ref, source_ref, step_ref, out_ref, part_ref, full_ref, mean_acc, words_ref, mean_words, *, coeff,
):
    groups = acc_ref.shape[1]
    rim_rows = rim_a.shape[1]
    begin, count, half = share_of(place_ref, index_ref)
    lead = place_ref[0] // 2 == 0
    row, load = rim_row(rim_a, rim_b), rim_block(rim_a, rim_b)
    unit = pack_table(load, 2 * rim_rows // SUBS, HARM_FIELDS, words_ref)
    mean_unit = pack_table(load, 2 * rim_rows // SUBS, MEAN_FIELDS, mean_words)
    gather_fields(
        row, HARM_FIELDS, 2 * rim_rows, words_ref, groups * LANES, index_ref, weight_ref, unit,
        lambda r, at: acc_ref[r, at, :], full_ref, VARS,
    )
    values = gather_into(
        row, MEAN_FIELDS, 2 * rim_rows, mean_words, groups * LANES, index_ref, weight_ref,
        begin, count, mean_unit, [share_ref[r] for r in range(VARS)],
    )
    mean_acc[...] = jnp.zeros(mean_acc.shape, F32)
    for r, value in enumerate(values):
        mean_acc[r, pl.ds(pl.multiple_of(half * SUBS, SUBS), SUBS), :] = value
    for g in range(groups // SUBS):
        at = slice(g * SUBS, (g + 1) * SUBS)
        mean = [mean_ref[v, at, :] for v in range(VARS)]
        state = [state_ref[r, at, :] for r in range(2 * VARS)]
        wsum = wsum_ref[at, :]
        scale = coeff * step_ref[at, :]
        flux = []
        for v in range(VARS):
            stress = state[v] * flow_ref[v, at, :] + state[VARS + v] * flow_ref[VARS + v, at, :]
            flux.append(jnp.where(lead, wsum * mean[v], 0.0) - mean_acc[v, at, :] - stress)
        for v, res in enumerate(transposed(jac_ref, at, flux)):
            own = jnp.where(lead, mean[v] + scale * source_ref[v, at, :], 0.0)
            part_ref[v, at, :] = own - scale * res
        gathered = [full_ref[r, at, :] for r in range(2 * VARS)]
        harm_step(order_ref, at, mean, state, state, gathered, wsum, scale, jac_ref, flow_ref, out_ref)
        for v in range(VARS):
            part_ref[VARS + v, at, :] = (
                out_ref[v, at, :] * flow_ref[v, at, :] + out_ref[VARS + v, at, :] * flow_ref[VARS + v, at, :]
            )


def join_kernel(parts_ref, state_ref, tile_idx, mean_ref, stress_ref, pay_a, pay_b):
    for v in range(VARS):
        for ref, r in ((mean_ref, v), (stress_ref, VARS + v)):
            total = parts_ref[0, r]
            for k in range(1, HARM_DEVICES):
                total = total + parts_ref[k, r]
            ref[v] = total
    row = fields_row(mean_ref, state_ref)
    store_tiles(row, (tile_idx[0], tile_idx[1]), pay_a, pay_b, mean_ref.shape[1])


def close_kernel(
    order_ref, acc_ref, rim_a, rim_b, index_ref, weight_ref, wsum_ref, mean_ref, state_ref, mean_start, harm_start,
    jac_ref, flow_ref, source_ref, step_ref, stress_ref,
    mean_hbm, harm_hbm, full_ref, new_mean, new_harm, words_ref, mean_out, harm_out, sems, *, coeff,
):
    groups = acc_ref.shape[1]
    rim_rows = rim_a.shape[1]
    unit = pack_table(rim_block(rim_a, rim_b), 2 * rim_rows // SUBS, ALL_FIELDS, words_ref)
    gather_fields(
        rim_row(rim_a, rim_b), ALL_FIELDS, 2 * rim_rows, words_ref, groups * LANES, index_ref, weight_ref, unit,
        lambda r, at: acc_ref[r, at, :], full_ref,
    )
    for g in range(groups // SUBS):
        at = slice(g * SUBS, (g + 1) * SUBS)
        mean = [mean_ref[v, at, :] for v in range(VARS)]
        state = [state_ref[r, at, :] for r in range(2 * VARS)]
        wsum = wsum_ref[at, :]
        scale = coeff * step_ref[at, :]
        flux = [wsum * m - full_ref[v, at, :] - stress_ref[v, at, :] for v, m in enumerate(mean)]
        for v, res in enumerate(transposed(jac_ref, at, flux)):
            new_mean[v, at, :] = mean_start[v, at, :] - scale * (res - source_ref[v, at, :])
        gathered = [full_ref[VARS + r, at, :] for r in range(2 * VARS)]
        start = [harm_start[r, at, :] for r in range(2 * VARS)]
        harm_step(order_ref, at, mean, state, start, gathered, wsum, scale, jac_ref, flow_ref, new_harm)
    for t in range(groups):
        lanes = slice(t * LANES, (t + 1) * LANES)
        mean_out[:, lanes] = stacked(lambda i: new_mean[i, t : t + 1, :], VARS)
    mean_copy = pltpu.make_async_copy(mean_out, mean_hbm, sems.at[0])
    mean_copy.start()
    for t in range(groups):
        lanes = slice(t * LANES, (t + 1) * LANES)
        for v in range(VARS):
            harm_out[v, :, lanes] = stacked(lambda i: new_harm[i * VARS + v, t : t + 1, :], 2)
    harm_copy = pltpu.make_async_copy(harm_out, harm_hbm, sems.at[1])
    harm_copy.start()
    mean_copy.wait()
    harm_copy.wait()


def stacked(row, count):
    sub = lax.broadcasted_iota(jnp.int32, (count, LANES), 0)
    out = jnp.broadcast_to(row(0), (count, LANES))
    for i in range(1, count):
        out = jnp.where(sub == i, jnp.broadcast_to(row(i), (count, LANES)), out)
    return out


def held(*arrays):
    return [*(pltpu.VMEM(a.shape, a.dtype) for a in arrays), pltpu.SemaphoreType.DMA((SUBS,))]


def launch(body, name, out_shape, scalars, args, raw=(), scratch=()):
    smem = pl.BlockSpec(memory_space=pltpu.SMEM)
    vmem = pl.BlockSpec(memory_space=pltpu.VMEM)
    anywhere = pl.BlockSpec(memory_space=pl.ANY)
    return pl.pallas_call(
        body,
        name=name,
        out_shape=out_shape,
        in_specs=[smem] * len(scalars) + [anywhere] * len(raw) + [vmem] * len(args),
        out_specs=[anywhere if isinstance(s, jax.ShapeDtypeStruct) else vmem for s in out_shape],
        scratch_shapes=scratch,
    )(*scalars, *raw, *(pltpu.with_memory_space_constraint(a, pltpu.VMEM) for a in args))


def exchange(pay_a, pay_b):
    count = lax.axis_size("cells")
    near = [(b, b ^ 1) for b in range(count)]
    far = [(b, (b - 1 + 2 * (b % 2)) % count) for b in range(count)]
    return lax.ppermute(pay_a, "cells", far), lax.ppermute(pay_b, "cells", near)


def shards(
    mean_adjoint,
    harm_adjoint,
    harm_flow,
    flux_jacobian,
    face_weight,
    face_links,
    face_tiles,
    pseudo_step,
    mean_source,
    harm_order,
):
    cells = mean_adjoint.shape[1]
    groups = cells // LANES
    halves = groups // SUBS
    rim_rows = face_tiles.shape[1] // LANES
    harm_adjoint, harm_flow = (
        a[0].swapaxes(0, 1) for a in (harm_adjoint, harm_flow)
    )
    place = (1 - lax.axis_index("cells") % 2 + 2 * lax.axis_index(HARM)).astype(jnp.int32)[None]
    step = pseudo_step.reshape(groups, LANES)
    mean_fields, harm_fields = struct(VARS, groups, LANES), struct(2 * VARS, groups, LANES)
    pays = (struct(ROWS, rim_rows, LANES), struct(ROWS, rim_rows, LANES))
    raw = (
        mean_adjoint, harm_adjoint, face_links, face_weight, harm_flow, flux_jacobian, mean_source, step
    )
    held_raw = tuple(struct(*a.shape, dtype=a.dtype) for a in raw)
    pay_a, pay_b, tile_idx, *inside, step = launch(
        open_kernel, "open", pays + (struct(2, rim_rows, LANES, dtype=jnp.int32),) + held_raw, (place,), (),
        (face_tiles, *raw), [pltpu.VMEM(face_tiles.shape, jnp.int32), pltpu.SemaphoreType.DMA((9,))],
    )
    rim_a, rim_b = exchange(pay_a, pay_b)
    registers = FACES * halves
    words = lambda fields: struct(max(len(fields) // 3 * 2, 1), groups, LANES, dtype=jnp.int32)
    harm_words, mean_words = words(HARM_FIELDS), words(MEAN_FIELDS)
    acc, share, index, weight, wsum, mean_start, harm_start, jac, flow, source = launch(
        prepare_kernel, "prepare",
        (
            harm_fields,
            struct(VARS, SUBS, LANES),
            struct(registers, SUBS, LANES, dtype=jnp.int32),
            struct(registers, SUBS, LANES),
            struct(groups, LANES),
            mean_fields,
            harm_fields,
            struct(VARS * VARS, groups, LANES),
            harm_fields,
            mean_fields,
        ),
        (place,), inside,
        scratch=[harm_words, mean_words],
    )
    state, part = launch(
        lambda *refs: middle_kernel(*refs, coeff=1.0 / SECTIONS), "middle", (harm_fields, harm_fields),
        (place, harm_order),
        (acc, share, rim_a, rim_b, index, weight, wsum, mean_start, harm_start, jac, flow, source, step),
        scratch=[harm_fields, mean_fields, harm_words, mean_words],
    )
    parts = lax.all_gather(part, HARM)
    mean, stress, pay_a, pay_b = launch(
        join_kernel, "join", (mean_fields, mean_fields) + pays, (), (parts, state, tile_idx)
    )
    rim_a, rim_b = exchange(pay_a, pay_b)
    fields = struct(ROWS, groups, LANES)
    (acc,) = launch(own_kernel, "own", (fields,), (), (mean, state, index, weight), scratch=[words(ALL_FIELDS)])
    outs = [jax.ShapeDtypeStruct(s, F32) for s in ((VARS, cells), (VARS, 2, cells))]
    mean_new, harm_new = launch(
        lambda *refs: close_kernel(*refs, coeff=1.0), "close", tuple(outs), (harm_order,),
        (acc, rim_a, rim_b, index, weight, wsum, mean, state, mean_start, harm_start,
         jac, flow, source, step, stress),
        scratch=[fields, mean_fields, harm_fields, words(ALL_FIELDS), *held(*outs)],
    )
    return mean_new, harm_new.swapaxes(0, 1)[None]


def solution(mesh):
    finer = Mesh(mesh.devices.reshape(mesh.shape["cells"], 2, 2), ("cells", *HARM))
    return jax.shard_map(
        shards,
        mesh=finer,
        in_specs=(
            P(None, "cells"),
            P(HARM, None, None, "cells"),
            P(HARM, None, None, "cells"),
            P(None, None, "cells"),
            P(None, "cells"),
            P(None, "cells"),
            P(None, "cells"),
            P("cells"),
            P(None, "cells"),
            P(HARM),
        ),
        out_specs=(P(None, "cells"), P(HARM, None, None, "cells")),
        check_vma=False,
    )
```

```python
import jax
import jax.numpy as jnp
from jax import lax
from jax.experimental import pallas as pl
from jax.experimental.pallas import tpu as pltpu
from jax.sharding import Mesh
from jax.sharding import PartitionSpec as P

VARS = 5
FACES = 6
SECTIONS = 2
ROWS = 3 * VARS
MEAN_FIELDS = range(VARS)
HARM_FIELDS = range(VARS, ROWS)
ALL_FIELDS = range(ROWS)
HARM = ("harm_0", "harm_1")
HARM_DEVICES = 4
LANES = 128
SUBS = 8
BASE_FREQ = 0.8
F32 = jnp.float32


def struct(*shape, dtype=F32):
    return pltpu.VMEM(shape, dtype)


def spread(row):
    return jnp.broadcast_to(row, (SUBS, LANES))


def packed(tile, first):
    sub = lax.broadcasted_iota(jnp.int32, (SUBS, LANES), 0)
    out = spread(tile(first))
    for i in range(1, SUBS):
        out = jnp.where(sub == i, spread(tile(first + i)), out)
    return out


def picked(row, fields, count, index):
    low = index & (LANES - 1)
    high = index >> 7
    out = [None] * len(fields)
    for h in range(count):
        hit = high == h
        for i, r in enumerate(fields):
            value = jnp.take_along_axis(spread(row(r, h)), low, axis=1)
            out[i] = jnp.where(hit, value, jnp.zeros_like(value) if h == 0 else out[i])
    return out


def store_tiles(row, tile_index, pay_a, pay_b, rows):
    for pay, index in zip((pay_a, pay_b), tile_index):
        for r, value in enumerate(picked(row, range(ROWS), rows, index)):
            pay[r] = value


def native_row(mean_ref, harm_ref):
    def row(r, h):
        lanes = slice(h * LANES, (h + 1) * LANES)
        if r < VARS:
            return mean_ref[r : r + 1, lanes]
        part, var = divmod(r - VARS, VARS)
        return harm_ref[var, part : part + 1, lanes]

    return row


def fetch(sources, targets, sems):
    copies = [pltpu.make_async_copy(s, t, sems.at[i]) for i, (s, t) in enumerate(zip(sources, targets))]
    for copy in copies:
        copy.start()
    return [copy.wait for copy in copies]


def open_kernel(
    place_ref, tiles_hbm, mean_hbm, harm_hbm, links_hbm, weight_hbm, flow_hbm, jac_hbm, source_hbm, step_hbm,
    pay_a, pay_b, tile_idx, mean_ref, harm_ref, links_ref, weight_ref, flow_ref, jac_ref, source_ref, step_ref,
    tiles_ref, sems,
):
    waits = fetch(
        (tiles_hbm, mean_hbm, harm_hbm, links_hbm, weight_hbm, flow_hbm, jac_hbm, source_hbm, step_hbm),
        (tiles_ref, mean_ref, harm_ref, links_ref, weight_ref, flow_ref, jac_ref, source_ref, step_ref),
        sems,
    )
    for wait in waits[:3]:
        wait()
    lowers_first = place_ref[0] % 2 == 1
    lower, upper = (
        packed(lambda t, k=k: tiles_ref[k : k + 1, t * LANES : (t + 1) * LANES], 0) for k in range(2)
    )
    first = jnp.where(lowers_first, lower, upper)
    second = jnp.where(lowers_first, upper, lower)
    tile_idx[0] = first
    tile_idx[1] = second
    row = native_row(mean_ref, harm_ref)
    store_tiles(row, (first, second), pay_a, pay_b, mean_ref.shape[1] // LANES)
    for wait in waits[3:]:
        wait()


TOP = float(2**20 - 1)


def largest(values):
    top = jnp.abs(values[0])
    for value in values[1:]:
        top = jnp.maximum(top, jnp.abs(value))
    top = jnp.max(jnp.max(top, axis=0, keepdims=True), axis=1, keepdims=True)
    return jnp.maximum(jnp.broadcast_to(top, (SUBS, LANES)), 1e-30)


def pack_table(load, blocks, fields, words_ref):
    unit = {}
    scale = {}
    for kind in ([r for r in fields if r < VARS], [r for r in fields if r >= VARS]):
        if kind:
            top = largest([load(r, g) for r in kind for g in range(blocks)])
            for r in kind:
                unit[r] = top * (1.0 / TOP)
                scale[r] = TOP / top
    fixed = lambda r, g: jnp.floor(load(r, g) * scale[r] + 0.5).astype(jnp.int32)
    for i in range(len(fields) // 3):
        for g in range(blocks):
            at = slice(g * SUBS, (g + 1) * SUBS)
            first, second, third = (fixed(r, g) for r in fields[3 * i : 3 * i + 3])
            words_ref[2 * i, at, :] = (first << 11) | ((third >> 10) & 0x7FF)
            words_ref[2 * i + 1, at, :] = (second << 11) | (third & 0x3FF)
    return unit


def gather_into(row, fields, count, words_ref, first, index_ref, weight_ref, begin, faces, unit, start):
    triples = len(fields) // 3
    words = 2 * triples
    rest = fields[3 * triples :]

    def word(w, h):
        return words_ref[w, h : h + 1, :] if w < words else row(rest[w - words], h)

    def face(f, acc):
        found = picked(word, range(words + len(rest)), count, index_ref[begin + f] - first)
        weight = weight_ref[begin + f]
        values = []
        for i in range(triples):
            one, two = found[2 * i], found[2 * i + 1]
            values += [one >> 11, two >> 11, ((one << 21) >> 11) | (two & 0x3FF)]
        values = [v.astype(F32) for v in values] + found[words:]
        return tuple(a + weight * v for a, v in zip(acc, values))

    sums = (jnp.zeros((SUBS, LANES), F32),) * len(fields)
    for f in range(faces):
        sums = face(f, sums)
    return [
        s + (a if i >= 3 * triples else unit[r] * a) for i, (r, s, a) in enumerate(zip(fields, start, sums))
    ]


def share_of(place_ref, index_ref):
    count = index_ref.shape[0] // HARM_DEVICES
    begin = place_ref[0] // 2 * count
    return begin, count, begin // FACES


def gather_fields(row, fields, count, words_ref, first, index_ref, weight_ref, unit, start, out_ref, lead=0):
    for g in range(index_ref.shape[0] // FACES):
        at = slice(g * SUBS, (g + 1) * SUBS)
        values = gather_into(
            row, fields, count, words_ref, first, index_ref, weight_ref, g * FACES, FACES, unit,
            [start(r - lead, at) for r in fields],
        )
        for r, value in zip(fields, values):
            out_ref[r - lead, at, :] = value


def zero_start(*_):
    return jnp.zeros((SUBS, LANES), F32)


def prepare_kernel(
    place_ref, mean_ref, harm_ref, links_ref, weight_in, flow_ref, jac_ref, source_ref,
    acc_ref, share_ref, index_ref, weight_ref, wsum_ref, mean_out, state_ref, jac_out, flow_out, source_out,
    words_ref, mean_words,
):
    groups = mean_ref.shape[1] // LANES
    flips = place_ref[0] % 2 == 0
    rim = groups * LANES
    lane = lambda t: slice(t * LANES, (t + 1) * LANES)
    for g in range(groups // SUBS):
        total = None
        for f in range(FACES):
            link = packed(lambda t: links_ref[f : f + 1, lane(t)], g * SUBS)
            flipped = jnp.where(link >= rim, link ^ (rim // 2), link)
            index_ref[g * FACES + f] = jnp.where(flips, flipped, link)
            weight = packed(lambda t: weight_in[f : f + 1, lane(t)], g * SUBS)
            weight_ref[g * FACES + f] = weight
            total = weight if total is None else total + weight
        wsum_ref[g * SUBS : (g + 1) * SUBS, :] = total
    row = native_row(mean_ref, harm_ref)
    flow = native_row(mean_ref, flow_ref)
    for g in range(0, groups, SUBS):
        at = slice(g, g + SUBS)
        for r in range(VARS):
            mean_out[r, at, :] = packed(lambda t: row(r, t), g)
        for r in range(2 * VARS):
            state_ref[r, at, :] = packed(lambda t: row(VARS + r, t), g)
    row = fields_row(mean_out, state_ref)
    load = fields_block(mean_out, state_ref)
    unit = pack_table(load, groups // SUBS, HARM_FIELDS, words_ref)
    mean_unit = pack_table(load, groups // SUBS, MEAN_FIELDS, mean_words)
    gather_fields(
        row, HARM_FIELDS, groups, words_ref, 0, index_ref, weight_ref, unit, zero_start, acc_ref, VARS
    )
    begin, count, _ = share_of(place_ref, index_ref)
    values = gather_into(
        row, MEAN_FIELDS, groups, mean_words, 0, index_ref, weight_ref, begin, count, mean_unit,
        [zero_start()] * VARS,
    )
    for r, value in enumerate(values):
        share_ref[r] = value
    for g in range(0, groups, SUBS):
        at = slice(g, g + SUBS)
        for r in range(2 * VARS):
            flow_out[r, at, :] = packed(lambda t: flow(VARS + r, t), g)
        for v in range(VARS):
            source_out[v, at, :] = packed(lambda t: source_ref[v : v + 1, lane(t)], g)
        for j in range(VARS):
            for i in range(VARS):
                jac_out[j * VARS + i, at, :] = packed(lambda t: jac_ref[j, i : i + 1, lane(t)], g)


def fields_row(mean_ref, harm_ref):
    def row(r, h):
        return mean_ref[r, h : h + 1, :] if r < VARS else harm_ref[r - VARS, h : h + 1, :]

    return row


def fields_block(mean_ref, harm_ref):
    def load(r, g):
        at = slice(g * SUBS, (g + 1) * SUBS)
        return mean_ref[r, at, :] if r < VARS else harm_ref[r - VARS, at, :]

    return load


def rim_row(rim_a, rim_b):
    rows = rim_a.shape[1]

    def row(r, h):
        ref = rim_a if h < rows else rim_b
        h = h % rows
        return ref[r, h : h + 1, :]

    return row


def rim_block(rim_a, rim_b):
    blocks = rim_a.shape[1] // SUBS

    def load(r, g):
        ref = rim_a if g < blocks else rim_b
        g = g % blocks
        return ref[r, g * SUBS : (g + 1) * SUBS, :]

    return load


def transposed(jac_ref, at, flux):
    out = []
    for i in range(VARS):
        res = jac_ref[i, at, :] * flux[0]
        for j in range(1, VARS):
            res = res + jac_ref[j * VARS + i, at, :] * flux[j]
        out.append(res)
    return out


def harm_step(order_ref, at, mean, state, start, gathered, wsum, scale, jac_ref, flow_ref, out_ref):
    omega = BASE_FREQ * (order_ref[0].astype(F32) + 1.0)
    flux = [wsum * s - x for s, x in zip(state, gathered)]
    for part in range(2):
        res = transposed(jac_ref, at, flux[part * VARS : (part + 1) * VARS])
        for i in range(VARS):
            r = part * VARS + i
            turned = omega * state[(1 - part) * VARS + i]
            full = res[i] + turned if part == 0 else res[i] - turned
            full = full - mean[i] * flow_ref[r, at, :]
            out_ref[r, at, :] = start[r] - scale * full


def middle_kernel(
    place_ref, order_ref, acc_ref, share_ref, rim_a, rim_b, index_ref, weight_ref, wsum_ref, mean_ref, state_ref,
    jac_ref, flow_ref, source_ref, step_ref, out_ref, part_ref, full_ref, mean_acc, words_ref, mean_words, *, coeff,
):
    groups = acc_ref.shape[1]
    rim_rows = rim_a.shape[1]
    begin, count, half = share_of(place_ref, index_ref)
    lead = place_ref[0] // 2 == 0
    row, load = rim_row(rim_a, rim_b), rim_block(rim_a, rim_b)
    unit = pack_table(load, 2 * rim_rows // SUBS, HARM_FIELDS, words_ref)
    mean_unit = pack_table(load, 2 * rim_rows // SUBS, MEAN_FIELDS, mean_words)
    gather_fields(
        row, HARM_FIELDS, 2 * rim_rows, words_ref, groups * LANES, index_ref, weight_ref, unit,
        lambda r, at: acc_ref[r, at, :], full_ref, VARS,
    )
    values = gather_into(
        row, MEAN_FIELDS, 2 * rim_rows, mean_words, groups * LANES, index_ref, weight_ref,
        begin, count, mean_unit, [share_ref[r] for r in range(VARS)],
    )
    mean_acc[...] = jnp.zeros(mean_acc.shape, F32)
    for r, value in enumerate(values):
        mean_acc[r, pl.ds(pl.multiple_of(half * SUBS, SUBS), SUBS), :] = value
    for g in range(groups // SUBS):
        at = slice(g * SUBS, (g + 1) * SUBS)
        mean = [mean_ref[v, at, :] for v in range(VARS)]
        state = [state_ref[r, at, :] for r in range(2 * VARS)]
        wsum = wsum_ref[at, :]
        scale = coeff * step_ref[at, :]
        flux = []
        for v in range(VARS):
            stress = state[v] * flow_ref[v, at, :] + state[VARS + v] * flow_ref[VARS + v, at, :]
            flux.append(jnp.where(lead, wsum * mean[v], 0.0) - mean_acc[v, at, :] - stress)
        for v, res in enumerate(transposed(jac_ref, at, flux)):
            own = jnp.where(lead, mean[v] + scale * source_ref[v, at, :], 0.0)
            part_ref[v, at, :] = own - scale * res
        gathered = [full_ref[r, at, :] for r in range(2 * VARS)]
        harm_step(order_ref, at, mean, state, state, gathered, wsum, scale, jac_ref, flow_ref, out_ref)
        for v in range(VARS):
            part_ref[VARS + v, at, :] = (
                out_ref[v, at, :] * flow_ref[v, at, :] + out_ref[VARS + v, at, :] * flow_ref[VARS + v, at, :]
            )


def join_kernel(parts_ref, state_ref, tile_idx, mean_ref, stress_ref, pay_a, pay_b):
    for v in range(VARS):
        for ref, r in ((mean_ref, v), (stress_ref, VARS + v)):
            total = parts_ref[0, r]
            for k in range(1, HARM_DEVICES):
                total = total + parts_ref[k, r]
            ref[v] = total
    row = fields_row(mean_ref, state_ref)
    store_tiles(row, (tile_idx[0], tile_idx[1]), pay_a, pay_b, mean_ref.shape[1])


def own_kernel(
    order_ref, index_ref, weight_ref, wsum_ref, mean_ref, state_ref, mean_start, harm_start,
    jac_ref, flow_ref, source_ref, step_ref, stress_ref, mean_base, harm_base, full_ref, words_ref, *, coeff,
):
    groups = mean_ref.shape[1]
    unit = pack_table(fields_block(mean_ref, state_ref), groups // SUBS, ALL_FIELDS, words_ref)
    gather_fields(
        fields_row(mean_ref, state_ref), ALL_FIELDS, groups, words_ref, 0, index_ref, weight_ref, unit,
        zero_start, full_ref,
    )
    for g in range(groups // SUBS):
        at = slice(g * SUBS, (g + 1) * SUBS)
        mean = [mean_ref[v, at, :] for v in range(VARS)]
        state = [state_ref[r, at, :] for r in range(2 * VARS)]
        wsum = wsum_ref[at, :]
        scale = coeff * step_ref[at, :]
        flux = [wsum * m - full_ref[v, at, :] - stress_ref[v, at, :] for v, m in enumerate(mean)]
        for v, res in enumerate(transposed(jac_ref, at, flux)):
            mean_base[v, at, :] = mean_start[v, at, :] - scale * (res - source_ref[v, at, :])
        gathered = [full_ref[VARS + r, at, :] for r in range(2 * VARS)]
        start = [harm_start[r, at, :] for r in range(2 * VARS)]
        harm_step(order_ref, at, mean, state, start, gathered, wsum, scale, jac_ref, flow_ref, harm_base)


def close_kernel(
    rim_a, rim_b, index_ref, weight_ref, jac_ref, step_ref, mean_base, harm_base,
    mean_hbm, harm_hbm, full_ref, words_ref, mean_out, harm_out, sems, *, coeff,
):
    groups = mean_base.shape[1]
    rim_rows = rim_a.shape[1]
    unit = pack_table(rim_block(rim_a, rim_b), 2 * rim_rows // SUBS, ALL_FIELDS, words_ref)
    gather_fields(
        rim_row(rim_a, rim_b), ALL_FIELDS, 2 * rim_rows, words_ref, groups * LANES, index_ref, weight_ref, unit,
        zero_start, full_ref,
    )
    base = fields_block(mean_base, harm_base)
    for g in range(groups // SUBS):
        at = slice(g * SUBS, (g + 1) * SUBS)
        scale = coeff * step_ref[at, :]
        for first in range(0, ROWS, VARS):
            values = [full_ref[first + v, at, :] for v in range(VARS)]
            for v, res in enumerate(transposed(jac_ref, at, values)):
                full_ref[first + v, at, :] = base(first + v, g) + scale * res
    for t in range(groups):
        lanes = slice(t * LANES, (t + 1) * LANES)
        mean_out[:, lanes] = stacked(lambda i: full_ref[i, t : t + 1, :], VARS)
    mean_copy = pltpu.make_async_copy(mean_out, mean_hbm, sems.at[0])
    mean_copy.start()
    for t in range(groups):
        lanes = slice(t * LANES, (t + 1) * LANES)
        for v in range(VARS):
            harm_out[v, :, lanes] = stacked(lambda i: full_ref[(i + 1) * VARS + v, t : t + 1, :], 2)
    harm_copy = pltpu.make_async_copy(harm_out, harm_hbm, sems.at[1])
    harm_copy.start()
    mean_copy.wait()
    harm_copy.wait()


def stacked(row, count):
    sub = lax.broadcasted_iota(jnp.int32, (count, LANES), 0)
    out = jnp.broadcast_to(row(0), (count, LANES))
    for i in range(1, count):
        out = jnp.where(sub == i, jnp.broadcast_to(row(i), (count, LANES)), out)
    return out


def held(*arrays):
    return [*(pltpu.VMEM(a.shape, a.dtype) for a in arrays), pltpu.SemaphoreType.DMA((SUBS,))]


def launch(body, name, out_shape, scalars, args, raw=(), scratch=()):
    smem = pl.BlockSpec(memory_space=pltpu.SMEM)
    vmem = pl.BlockSpec(memory_space=pltpu.VMEM)
    anywhere = pl.BlockSpec(memory_space=pl.ANY)
    return pl.pallas_call(
        body,
        name=name,
        out_shape=out_shape,
        in_specs=[smem] * len(scalars) + [anywhere] * len(raw) + [vmem] * len(args),
        out_specs=[anywhere if isinstance(s, jax.ShapeDtypeStruct) else vmem for s in out_shape],
        scratch_shapes=scratch,
    )(*scalars, *raw, *(pltpu.with_memory_space_constraint(a, pltpu.VMEM) for a in args))


def exchange(pay_a, pay_b):
    count = lax.axis_size("cells")
    near = [(b, b ^ 1) for b in range(count)]
    far = [(b, (b - 1 + 2 * (b % 2)) % count) for b in range(count)]
    return lax.ppermute(pay_a, "cells", far), lax.ppermute(pay_b, "cells", near)


def shards(
    mean_adjoint,
    harm_adjoint,
    harm_flow,
    flux_jacobian,
    face_weight,
    face_links,
    face_tiles,
    pseudo_step,
    mean_source,
    harm_order,
):
    cells = mean_adjoint.shape[1]
    groups = cells // LANES
    halves = groups // SUBS
    rim_rows = face_tiles.shape[1] // LANES
    harm_adjoint, harm_flow = (
        a[0].swapaxes(0, 1) for a in (harm_adjoint, harm_flow)
    )
    place = (1 - lax.axis_index("cells") % 2 + 2 * lax.axis_index(HARM)).astype(jnp.int32)[None]
    step = pseudo_step.reshape(groups, LANES)
    mean_fields, harm_fields = struct(VARS, groups, LANES), struct(2 * VARS, groups, LANES)
    pays = (struct(ROWS, rim_rows, LANES), struct(ROWS, rim_rows, LANES))
    raw = (
        mean_adjoint, harm_adjoint, face_links, face_weight, harm_flow, flux_jacobian, mean_source, step
    )
    held_raw = tuple(struct(*a.shape, dtype=a.dtype) for a in raw)
    pay_a, pay_b, tile_idx, *inside, step = launch(
        open_kernel, "open", pays + (struct(2, rim_rows, LANES, dtype=jnp.int32),) + held_raw, (place,), (),
        (face_tiles, *raw), [pltpu.VMEM(face_tiles.shape, jnp.int32), pltpu.SemaphoreType.DMA((9,))],
    )
    rim_a, rim_b = exchange(pay_a, pay_b)
    registers = FACES * halves
    words = lambda fields: struct(max(len(fields) // 3 * 2, 1), groups, LANES, dtype=jnp.int32)
    harm_words, mean_words = words(HARM_FIELDS), words(MEAN_FIELDS)
    acc, share, index, weight, wsum, mean_start, harm_start, jac, flow, source = launch(
        prepare_kernel, "prepare",
        (
            harm_fields,
            struct(VARS, SUBS, LANES),
            struct(registers, SUBS, LANES, dtype=jnp.int32),
            struct(registers, SUBS, LANES),
            struct(groups, LANES),
            mean_fields,
            harm_fields,
            struct(VARS * VARS, groups, LANES),
            harm_fields,
            mean_fields,
        ),
        (place,), inside,
        scratch=[harm_words, mean_words],
    )
    state, part = launch(
        lambda *refs: middle_kernel(*refs, coeff=1.0 / SECTIONS), "middle", (harm_fields, harm_fields),
        (place, harm_order),
        (acc, share, rim_a, rim_b, index, weight, wsum, mean_start, harm_start, jac, flow, source, step),
        scratch=[harm_fields, mean_fields, harm_words, mean_words],
    )
    parts = lax.all_gather(part, HARM)
    mean, stress, pay_a, pay_b = launch(
        join_kernel, "join", (mean_fields, mean_fields) + pays, (), (parts, state, tile_idx)
    )
    rim_a, rim_b = exchange(pay_a, pay_b)
    fields = struct(ROWS, groups, LANES)
    mean_base, harm_base = launch(
        lambda *refs: own_kernel(*refs, coeff=1.0), "own", (mean_fields, harm_fields), (harm_order,),
        (index, weight, wsum, mean, state, mean_start, harm_start, jac, flow, source, step, stress),
        scratch=[fields, words(ALL_FIELDS)],
    )
    outs = [jax.ShapeDtypeStruct(s, F32) for s in ((VARS, cells), (VARS, 2, cells))]
    mean_new, harm_new = launch(
        lambda *refs: close_kernel(*refs, coeff=1.0), "close", tuple(outs), (),
        (rim_a, rim_b, index, weight, jac, step, mean_base, harm_base),
        scratch=[fields, words(ALL_FIELDS), *held(*outs)],
    )
    return mean_new, harm_new.swapaxes(0, 1)[None]


def solution(mesh):
    finer = Mesh(mesh.devices.reshape(mesh.shape["cells"], 2, 2), ("cells", *HARM))
    return jax.shard_map(
        shards,
        mesh=finer,
        in_specs=(
            P(None, "cells"),
            P(HARM, None, None, "cells"),
            P(HARM, None, None, "cells"),
            P(None, None, "cells"),
            P(None, "cells"),
            P(None, "cells"),
            P(None, "cells"),
            P("cells"),
            P(None, "cells"),
            P(HARM),
        ),
        out_specs=(P(None, "cells"), P(HARM, None, None, "cells")),
        check_vma=False,
    )
```

```python
import jax
import jax.numpy as jnp
from jax import lax
from jax.experimental import pallas as pl
from jax.experimental.pallas import tpu as pltpu
from jax.sharding import Mesh
from jax.sharding import PartitionSpec as P

VARS = 5
FACES = 6
SECTIONS = 2
ROWS = 3 * VARS
MEAN_FIELDS = range(VARS)
HARM_FIELDS = range(VARS, ROWS)
ALL_FIELDS = range(ROWS)
HARM = ("harm_0", "harm_1")
HARM_DEVICES = 4
LANES = 128
SUBS = 8
BASE_FREQ = 0.8
F32 = jnp.float32


def struct(*shape, dtype=F32):
    return pltpu.VMEM(shape, dtype)


def spread(row):
    return jnp.broadcast_to(row, (SUBS, LANES))


def packed(tile, first):
    sub = lax.broadcasted_iota(jnp.int32, (SUBS, LANES), 0)
    out = spread(tile(first))
    for i in range(1, SUBS):
        out = jnp.where(sub == i, spread(tile(first + i)), out)
    return out


def picked(row, fields, count, index):
    low = index & (LANES - 1)
    high = index >> 7
    out = [None] * len(fields)
    for h in range(count):
        hit = high == h
        for i, r in enumerate(fields):
            value = jnp.take_along_axis(spread(row(r, h)), low, axis=1)
            out[i] = jnp.where(hit, value, jnp.zeros_like(value) if h == 0 else out[i])
    return out


def store_tiles(row, tile_index, pay_a, pay_b, rows):
    for pay, index in zip((pay_a, pay_b), tile_index):
        for r, value in enumerate(picked(row, range(ROWS), rows, index)):
            pay[r] = value


def native_row(mean_ref, harm_ref):
    def row(r, h):
        lanes = slice(h * LANES, (h + 1) * LANES)
        if r < VARS:
            return mean_ref[r : r + 1, lanes]
        part, var = divmod(r - VARS, VARS)
        return harm_ref[var, part : part + 1, lanes]

    return row


def fetch(sources, targets, sems):
    copies = [pltpu.make_async_copy(s, t, sems.at[i]) for i, (s, t) in enumerate(zip(sources, targets))]
    for copy in copies:
        copy.start()
    return [copy.wait for copy in copies]


def open_kernel(
    place_ref, tiles_hbm, mean_hbm, harm_hbm, links_hbm, weight_hbm, flow_hbm, jac_hbm, source_hbm, step_hbm,
    pay_a, pay_b, tile_idx, mean_ref, harm_ref, links_ref, weight_ref, flow_ref, jac_ref, source_ref, step_ref,
    tiles_ref, sems,
):
    waits = fetch(
        (tiles_hbm, mean_hbm, harm_hbm, links_hbm, weight_hbm, flow_hbm, jac_hbm, source_hbm, step_hbm),
        (tiles_ref, mean_ref, harm_ref, links_ref, weight_ref, flow_ref, jac_ref, source_ref, step_ref),
        sems,
    )
    for wait in waits[:3]:
        wait()
    lowers_first = place_ref[0] % 2 == 1
    lower, upper = (
        packed(lambda t, k=k: tiles_ref[k : k + 1, t * LANES : (t + 1) * LANES], 0) for k in range(2)
    )
    first = jnp.where(lowers_first, lower, upper)
    second = jnp.where(lowers_first, upper, lower)
    tile_idx[0] = first
    tile_idx[1] = second
    row = native_row(mean_ref, harm_ref)
    store_tiles(row, (first, second), pay_a, pay_b, mean_ref.shape[1] // LANES)
    for wait in waits[3:]:
        wait()


TOP = float(2**20 - 1)


def largest(values):
    top = jnp.abs(values[0])
    for value in values[1:]:
        top = jnp.maximum(top, jnp.abs(value))
    top = jnp.max(jnp.max(top, axis=0, keepdims=True), axis=1, keepdims=True)
    return jnp.maximum(jnp.broadcast_to(top, (SUBS, LANES)), 1e-30)


def pack_table(load, blocks, fields, words_ref):
    unit = {}
    scale = {}
    for kind in ([r for r in fields if r < VARS], [r for r in fields if r >= VARS]):
        if kind:
            top = largest([load(r, g) for r in kind for g in range(blocks)])
            for r in kind:
                unit[r] = top * (1.0 / TOP)
                scale[r] = TOP / top
    fixed = lambda r, g: jnp.floor(load(r, g) * scale[r] + 0.5).astype(jnp.int32)
    for i in range(len(fields) // 3):
        for g in range(blocks):
            at = slice(g * SUBS, (g + 1) * SUBS)
            first, second, third = (fixed(r, g) for r in fields[3 * i : 3 * i + 3])
            words_ref[2 * i, at, :] = (first << 11) | ((third >> 10) & 0x7FF)
            words_ref[2 * i + 1, at, :] = (second << 11) | (third & 0x3FF)
    return unit


def gather_into(row, fields, count, words_ref, first, index_ref, weight_ref, begin, faces, unit, start):
    triples = len(fields) // 3
    words = 2 * triples
    rest = fields[3 * triples :]

    def word(w, h):
        return words_ref[w, h : h + 1, :] if w < words else row(rest[w - words], h)

    def face(f, acc):
        found = picked(word, range(words + len(rest)), count, index_ref[begin + f] - first)
        weight = weight_ref[begin + f]
        values = []
        for i in range(triples):
            one, two = found[2 * i], found[2 * i + 1]
            values += [one >> 11, two >> 11, ((one << 21) >> 11) | (two & 0x3FF)]
        values = [v.astype(F32) for v in values] + found[words:]
        return tuple(a + weight * v for a, v in zip(acc, values))

    sums = (jnp.zeros((SUBS, LANES), F32),) * len(fields)
    for f in range(faces):
        sums = face(f, sums)
    return [
        s + (a if i >= 3 * triples else unit[r] * a) for i, (r, s, a) in enumerate(zip(fields, start, sums))
    ]


def share_of(place_ref, index_ref):
    count = index_ref.shape[0] // HARM_DEVICES
    begin = place_ref[0] // 2 * count
    return begin, count, begin // FACES


def gather_fields(row, fields, count, words_ref, first, index_ref, weight_ref, unit, start, out_ref, lead=0):
    for g in range(index_ref.shape[0] // FACES):
        at = slice(g * SUBS, (g + 1) * SUBS)
        values = gather_into(
            row, fields, count, words_ref, first, index_ref, weight_ref, g * FACES, FACES, unit,
            [start(r - lead, at) for r in fields],
        )
        for r, value in zip(fields, values):
            out_ref[r - lead, at, :] = value


def zero_start(*_):
    return jnp.zeros((SUBS, LANES), F32)


def prepare_kernel(
    place_ref, mean_ref, harm_ref, links_ref, weight_in, flow_ref, jac_ref, source_ref,
    acc_ref, share_ref, index_ref, weight_ref, wsum_ref, mean_out, state_ref, jac_out, flow_out, source_out,
    words_ref, mean_words,
):
    groups = mean_ref.shape[1] // LANES
    flips = place_ref[0] % 2 == 0
    rim = groups * LANES
    lane = lambda t: slice(t * LANES, (t + 1) * LANES)
    for g in range(groups // SUBS):
        total = None
        for f in range(FACES):
            link = packed(lambda t: links_ref[f : f + 1, lane(t)], g * SUBS)
            flipped = jnp.where(link >= rim, link ^ (rim // 2), link)
            index_ref[g * FACES + f] = jnp.where(flips, flipped, link)
            weight = packed(lambda t: weight_in[f : f + 1, lane(t)], g * SUBS)
            weight_ref[g * FACES + f] = weight
            total = weight if total is None else total + weight
        wsum_ref[g * SUBS : (g + 1) * SUBS, :] = total
    row = native_row(mean_ref, harm_ref)
    flow = native_row(mean_ref, flow_ref)
    for g in range(0, groups, SUBS):
        at = slice(g, g + SUBS)
        for r in range(VARS):
            mean_out[r, at, :] = packed(lambda t: row(r, t), g)
        for r in range(2 * VARS):
            state_ref[r, at, :] = packed(lambda t: row(VARS + r, t), g)
    row = fields_row(mean_out, state_ref)
    load = fields_block(mean_out, state_ref)
    unit = pack_table(load, groups // SUBS, HARM_FIELDS, words_ref)
    mean_unit = pack_table(load, groups // SUBS, MEAN_FIELDS, mean_words)
    gather_fields(
        row, HARM_FIELDS, groups, words_ref, 0, index_ref, weight_ref, unit, zero_start, acc_ref, VARS
    )
    begin, count, _ = share_of(place_ref, index_ref)
    values = gather_into(
        row, MEAN_FIELDS, groups, mean_words, 0, index_ref, weight_ref, begin, count, mean_unit,
        [zero_start()] * VARS,
    )
    for r, value in enumerate(values):
        share_ref[r] = value
    for g in range(0, groups, SUBS):
        at = slice(g, g + SUBS)
        for r in range(2 * VARS):
            flow_out[r, at, :] = packed(lambda t: flow(VARS + r, t), g)
        for v in range(VARS):
            source_out[v, at, :] = packed(lambda t: source_ref[v : v + 1, lane(t)], g)
        for j in range(VARS):
            for i in range(VARS):
                jac_out[j * VARS + i, at, :] = packed(lambda t: jac_ref[j, i : i + 1, lane(t)], g)


def fields_row(mean_ref, harm_ref):
    def row(r, h):
        return mean_ref[r, h : h + 1, :] if r < VARS else harm_ref[r - VARS, h : h + 1, :]

    return row


def fields_block(mean_ref, harm_ref):
    def load(r, g):
        at = slice(g * SUBS, (g + 1) * SUBS)
        return mean_ref[r, at, :] if r < VARS else harm_ref[r - VARS, at, :]

    return load


def rim_row(rim):
    return lambda r, h: rim[r, h : h + 1, :]


def rim_block(rim):
    return lambda r, g: rim[r, g * SUBS : (g + 1) * SUBS, :]


def shared_rim(place_ref, acc_ref, share_ref, rim, first, index_ref, weight_ref, words_ref, mean_words, out_ref):
    rows = rim.shape[1]
    row, load = rim_row(rim), rim_block(rim)
    unit = pack_table(load, rows // SUBS, HARM_FIELDS, words_ref)
    mean_unit = pack_table(load, rows // SUBS, MEAN_FIELDS, mean_words)
    gather_fields(
        row, HARM_FIELDS, rows, words_ref, first, index_ref, weight_ref, unit,
        lambda r, at: acc_ref[r, at, :], out_ref, VARS,
    )
    begin, count, _ = share_of(place_ref, index_ref)
    return gather_into(
        row, MEAN_FIELDS, rows, mean_words, first, index_ref, weight_ref,
        begin, count, mean_unit, [share_ref[r] for r in range(VARS)],
    )


def near_share_kernel(
    place_ref, acc_ref, share_ref, rim, index_ref, weight_ref, out_ref, share_out, words_ref, mean_words
):
    first = (acc_ref.shape[1] + rim.shape[1]) * LANES
    values = shared_rim(
        place_ref, acc_ref, share_ref, rim, first, index_ref, weight_ref, words_ref, mean_words, out_ref
    )
    for r, value in enumerate(values):
        share_out[r] = value


def near_kernel(rim, index_ref, weight_ref, out_ref, words_ref):
    rows = rim.shape[1]
    first = (out_ref.shape[1] + rows) * LANES
    unit = pack_table(rim_block(rim), rows // SUBS, ALL_FIELDS, words_ref)
    gather_fields(
        rim_row(rim), ALL_FIELDS, rows, words_ref, first, index_ref, weight_ref, unit, zero_start, out_ref
    )


def transposed(jac_ref, at, flux):
    out = []
    for i in range(VARS):
        res = jac_ref[i, at, :] * flux[0]
        for j in range(1, VARS):
            res = res + jac_ref[j * VARS + i, at, :] * flux[j]
        out.append(res)
    return out


def harm_step(order_ref, at, mean, state, start, gathered, wsum, scale, jac_ref, flow_ref, out_ref):
    omega = BASE_FREQ * (order_ref[0].astype(F32) + 1.0)
    flux = [wsum * s - x for s, x in zip(state, gathered)]
    for part in range(2):
        res = transposed(jac_ref, at, flux[part * VARS : (part + 1) * VARS])
        for i in range(VARS):
            r = part * VARS + i
            turned = omega * state[(1 - part) * VARS + i]
            full = res[i] + turned if part == 0 else res[i] - turned
            full = full - mean[i] * flow_ref[r, at, :]
            out_ref[r, at, :] = start[r] - scale * full


def middle_kernel(
    place_ref, order_ref, acc_ref, share_ref, rim, index_ref, weight_ref, wsum_ref, mean_ref, state_ref,
    jac_ref, flow_ref, source_ref, step_ref, out_ref, part_ref, full_ref, mean_acc, words_ref, mean_words, *, coeff,
):
    groups = acc_ref.shape[1]
    _, _, half = share_of(place_ref, index_ref)
    lead = place_ref[0] // 2 == 0
    values = shared_rim(
        place_ref, acc_ref, share_ref, rim, groups * LANES, index_ref, weight_ref, words_ref, mean_words, full_ref
    )
    mean_acc[...] = jnp.zeros(mean_acc.shape, F32)
    for r, value in enumerate(values):
        mean_acc[r, pl.ds(pl.multiple_of(half * SUBS, SUBS), SUBS), :] = value
    for g in range(groups // SUBS):
        at = slice(g * SUBS, (g + 1) * SUBS)
        mean = [mean_ref[v, at, :] for v in range(VARS)]
        state = [state_ref[r, at, :] for r in range(2 * VARS)]
        wsum = wsum_ref[at, :]
        scale = coeff * step_ref[at, :]
        flux = []
        for v in range(VARS):
            stress = state[v] * flow_ref[v, at, :] + state[VARS + v] * flow_ref[VARS + v, at, :]
            flux.append(jnp.where(lead, wsum * mean[v], 0.0) - mean_acc[v, at, :] - stress)
        for v, res in enumerate(transposed(jac_ref, at, flux)):
            own = jnp.where(lead, mean[v] + scale * source_ref[v, at, :], 0.0)
            part_ref[v, at, :] = own - scale * res
        gathered = [full_ref[r, at, :] for r in range(2 * VARS)]
        harm_step(order_ref, at, mean, state, state, gathered, wsum, scale, jac_ref, flow_ref, out_ref)
        for v in range(VARS):
            part_ref[VARS + v, at, :] = (
                out_ref[v, at, :] * flow_ref[v, at, :] + out_ref[VARS + v, at, :] * flow_ref[VARS + v, at, :]
            )


def join_kernel(parts_ref, state_ref, tile_idx, mean_ref, stress_ref, pay_a, pay_b):
    for v in range(VARS):
        for ref, r in ((mean_ref, v), (stress_ref, VARS + v)):
            total = parts_ref[0, r]
            for k in range(1, HARM_DEVICES):
                total = total + parts_ref[k, r]
            ref[v] = total
    row = fields_row(mean_ref, state_ref)
    store_tiles(row, (tile_idx[0], tile_idx[1]), pay_a, pay_b, mean_ref.shape[1])


def own_kernel(
    order_ref, index_ref, weight_ref, wsum_ref, mean_ref, state_ref, mean_start, harm_start,
    jac_ref, flow_ref, source_ref, step_ref, stress_ref, mean_base, harm_base, full_ref, words_ref, *, coeff,
):
    groups = mean_ref.shape[1]
    unit = pack_table(fields_block(mean_ref, state_ref), groups // SUBS, ALL_FIELDS, words_ref)
    gather_fields(
        fields_row(mean_ref, state_ref), ALL_FIELDS, groups, words_ref, 0, index_ref, weight_ref, unit,
        zero_start, full_ref,
    )
    for g in range(groups // SUBS):
        at = slice(g * SUBS, (g + 1) * SUBS)
        mean = [mean_ref[v, at, :] for v in range(VARS)]
        state = [state_ref[r, at, :] for r in range(2 * VARS)]
        wsum = wsum_ref[at, :]
        scale = coeff * step_ref[at, :]
        flux = [wsum * m - full_ref[v, at, :] - stress_ref[v, at, :] for v, m in enumerate(mean)]
        for v, res in enumerate(transposed(jac_ref, at, flux)):
            mean_base[v, at, :] = mean_start[v, at, :] - scale * (res - source_ref[v, at, :])
        gathered = [full_ref[VARS + r, at, :] for r in range(2 * VARS)]
        start = [harm_start[r, at, :] for r in range(2 * VARS)]
        harm_step(order_ref, at, mean, state, start, gathered, wsum, scale, jac_ref, flow_ref, harm_base)


def close_kernel(
    rim, index_ref, weight_ref, jac_ref, step_ref, mean_base, harm_base, near_ref,
    mean_hbm, harm_hbm, full_ref, words_ref, mean_out, harm_out, sems, *, coeff,
):
    groups = mean_base.shape[1]
    rows = rim.shape[1]
    unit = pack_table(rim_block(rim), rows // SUBS, ALL_FIELDS, words_ref)
    base = fields_block(mean_base, harm_base)
    copies = []
    for g in range(groups // SUBS):
        at = slice(g * SUBS, (g + 1) * SUBS)
        full = gather_into(
            rim_row(rim), ALL_FIELDS, rows, words_ref, groups * LANES, index_ref, weight_ref, g * FACES, FACES,
            unit, [near_ref[r, at, :] for r in ALL_FIELDS],
        )
        scale = coeff * step_ref[at, :]
        for first in range(0, ROWS, VARS):
            for v, res in enumerate(transposed(jac_ref, at, full[first : first + VARS])):
                full_ref[first + v, at, :] = base(first + v, g) + scale * res
        for t in range(g * SUBS, (g + 1) * SUBS):
            lanes = slice(t * LANES, (t + 1) * LANES)
            mean_out[:, lanes] = stacked(lambda i: full_ref[i, t : t + 1, :], VARS)
            for v in range(VARS):
                harm_out[v, :, lanes] = stacked(lambda i: full_ref[(i + 1) * VARS + v, t : t + 1, :], 2)
        part = pl.ds(g * SUBS * LANES, SUBS * LANES)
        for i, (out, hbm) in enumerate(
            ((mean_out.at[:, part], mean_hbm.at[:, part]), (harm_out.at[:, :, part], harm_hbm.at[:, :, part]))
        ):
            copies.append(pltpu.make_async_copy(out, hbm, sems.at[2 * g + i]))
            copies[-1].start()
    for copy in copies:
        copy.wait()


def stacked(row, count):
    sub = lax.broadcasted_iota(jnp.int32, (count, LANES), 0)
    out = jnp.broadcast_to(row(0), (count, LANES))
    for i in range(1, count):
        out = jnp.where(sub == i, jnp.broadcast_to(row(i), (count, LANES)), out)
    return out


def held(*arrays):
    return [*(pltpu.VMEM(a.shape, a.dtype) for a in arrays), pltpu.SemaphoreType.DMA((SUBS,))]


def launch(body, out_shape, scalars, args, raw=(), scratch=()):
    smem = pl.BlockSpec(memory_space=pltpu.SMEM)
    vmem = pl.BlockSpec(memory_space=pltpu.VMEM)
    anywhere = pl.BlockSpec(memory_space=pl.ANY)
    return pl.pallas_call(
        body,
        out_shape=out_shape,
        in_specs=[smem] * len(scalars) + [anywhere] * len(raw) + [vmem] * len(args),
        out_specs=[anywhere if isinstance(s, jax.ShapeDtypeStruct) else vmem for s in out_shape],
        scratch_shapes=scratch,
    )(*scalars, *raw, *(pltpu.with_memory_space_constraint(a, pltpu.VMEM) for a in args))


def exchange(pay_a, pay_b):
    count = lax.axis_size("cells")
    near = [(b, b ^ 1) for b in range(count)]
    far = [(b, (b - 1 + 2 * (b % 2)) % count) for b in range(count)]
    rim_a = lax.ppermute(pay_a, "cells", far)
    rim_b = lax.ppermute(pay_b, "cells", near)
    return rim_a, rim_b


def shards(
    mean_adjoint,
    harm_adjoint,
    harm_flow,
    flux_jacobian,
    face_weight,
    face_links,
    face_tiles,
    pseudo_step,
    mean_source,
    harm_order,
):
    cells = mean_adjoint.shape[1]
    groups = cells // LANES
    halves = groups // SUBS
    rim_rows = face_tiles.shape[1] // LANES
    harm_adjoint, harm_flow = (
        a[0].swapaxes(0, 1) for a in (harm_adjoint, harm_flow)
    )
    place = (1 - lax.axis_index("cells") % 2 + 2 * lax.axis_index(HARM)).astype(jnp.int32)[None]
    step = pseudo_step.reshape(groups, LANES)
    mean_fields, harm_fields = struct(VARS, groups, LANES), struct(2 * VARS, groups, LANES)
    pays = (struct(ROWS, rim_rows, LANES), struct(ROWS, rim_rows, LANES))
    raw = (
        mean_adjoint, harm_adjoint, face_links, face_weight, harm_flow, flux_jacobian, mean_source, step
    )
    held_raw = tuple(struct(*a.shape, dtype=a.dtype) for a in raw)
    pay_a, pay_b, tile_idx, *inside, step = launch(
        open_kernel, pays + (struct(2, rim_rows, LANES, dtype=jnp.int32),) + held_raw, (place,), (),
        (face_tiles, *raw), [pltpu.VMEM(face_tiles.shape, jnp.int32), pltpu.SemaphoreType.DMA((9,))],
    )
    rim_a, rim_b = exchange(pay_a, pay_b)
    registers = FACES * halves
    words = lambda fields: struct(max(len(fields) // 3 * 2, 1), groups, LANES, dtype=jnp.int32)
    harm_words, mean_words = words(HARM_FIELDS), words(MEAN_FIELDS)
    acc, share, index, weight, wsum, mean_start, harm_start, jac, flow, source = launch(
        prepare_kernel,
        (
            harm_fields,
            struct(VARS, SUBS, LANES),
            struct(registers, SUBS, LANES, dtype=jnp.int32),
            struct(registers, SUBS, LANES),
            struct(groups, LANES),
            mean_fields,
            harm_fields,
            struct(VARS * VARS, groups, LANES),
            harm_fields,
            mean_fields,
        ),
        (place,), inside,
        scratch=[harm_words, mean_words],
    )
    acc, share = launch(
        near_share_kernel, (harm_fields, struct(VARS, SUBS, LANES)), (place,),
        (acc, share, rim_b, index, weight), scratch=[harm_words, mean_words],
    )
    state, part = launch(
        lambda *refs: middle_kernel(*refs, coeff=1.0 / SECTIONS), (harm_fields, harm_fields),
        (place, harm_order),
        (acc, share, rim_a, index, weight, wsum, mean_start, harm_start, jac, flow, source, step),
        scratch=[harm_fields, mean_fields, harm_words, mean_words],
    )
    parts = lax.all_gather(part, HARM)
    mean, stress, pay_a, pay_b = launch(join_kernel, (mean_fields, mean_fields) + pays, (), (parts, state, tile_idx))
    rim_a, rim_b = exchange(pay_a, pay_b)
    fields = struct(ROWS, groups, LANES)
    mean_base, harm_base = launch(
        lambda *refs: own_kernel(*refs, coeff=1.0), (mean_fields, harm_fields), (harm_order,),
        (index, weight, wsum, mean, state, mean_start, harm_start, jac, flow, source, step, stress),
        scratch=[fields, words(ALL_FIELDS)],
    )
    (near,) = launch(near_kernel, (fields,), (), (rim_b, index, weight), scratch=[words(ALL_FIELDS)])
    outs = [jax.ShapeDtypeStruct(s, F32) for s in ((VARS, cells), (VARS, 2, cells))]
    mean_new, harm_new = launch(
        lambda *refs: close_kernel(*refs, coeff=1.0), tuple(outs), (),
        (rim_a, index, weight, jac, step, mean_base, harm_base, near),
        scratch=[fields, words(ALL_FIELDS), *held(*outs)],
    )
    return mean_new, harm_new.swapaxes(0, 1)[None]


def solution(mesh):
    finer = Mesh(mesh.devices.reshape(mesh.shape["cells"], 2, 2), ("cells", *HARM))
    return jax.shard_map(
        shards,
        mesh=finer,
        in_specs=(
            P(None, "cells"),
            P(HARM, None, None, "cells"),
            P(HARM, None, None, "cells"),
            P(None, None, "cells"),
            P(None, "cells"),
            P(None, "cells"),
            P(None, "cells"),
            P("cells"),
            P(None, "cells"),
            P(HARM),
        ),
        out_specs=(P(None, "cells"), P(HARM, None, None, "cells")),
        check_vma=False,
    )
```

```python
import jax
import jax.numpy as jnp
from jax import lax
from jax.experimental import pallas as pl
from jax.experimental.pallas import tpu as pltpu
from jax.sharding import Mesh
from jax.sharding import PartitionSpec as P

VARS = 5
FACES = 6
SECTIONS = 2
ROWS = 3 * VARS
MEAN_FIELDS = range(VARS)
HARM_FIELDS = range(VARS, ROWS)
ALL_FIELDS = range(ROWS)
HARM = ("harm_0", "harm_1")
LANES = 128
SUBS = 8
BASE_FREQ = 0.8
F32 = jnp.float32


def struct(*shape, dtype=F32):
    return pltpu.VMEM(shape, dtype)


def spread(row):
    return jnp.broadcast_to(row, (SUBS, LANES))


def packed(tile, first):
    sub = lax.broadcasted_iota(jnp.int32, (SUBS, LANES), 0)
    out = spread(tile(first))
    for i in range(1, SUBS):
        out = jnp.where(sub == i, spread(tile(first + i)), out)
    return out


def picked(row, fields, count, index):
    low = index & (LANES - 1)
    high = index >> 7
    out = [None] * len(fields)
    for h in range(count):
        hit = high == h
        for i, r in enumerate(fields):
            value = jnp.take_along_axis(spread(row(r, h)), low, axis=1)
            out[i] = jnp.where(hit, value, jnp.zeros_like(value) if h == 0 else out[i])
    return out


def store_tiles(row, tile_index, pay_a, pay_b, rows):
    for pay, index in zip((pay_a, pay_b), tile_index):
        for r, value in enumerate(picked(row, range(ROWS), rows, index)):
            pay[r] = value


def native_row(mean_ref, harm_ref):
    def row(r, h):
        lanes = slice(h * LANES, (h + 1) * LANES)
        if r < VARS:
            return mean_ref[r : r + 1, lanes]
        part, var = divmod(r - VARS, VARS)
        return harm_ref[var, part : part + 1, lanes]

    return row


def fetch(sources, targets, sems):
    copies = [pltpu.make_async_copy(s, t, sems.at[i]) for i, (s, t) in enumerate(zip(sources, targets))]
    for copy in copies:
        copy.start()
    return [copy.wait for copy in copies]


def open_kernel(
    place_ref, tiles_hbm, mean_hbm, harm_hbm, flow_hbm, links_hbm, weight_hbm, jac_hbm, source_hbm, step_hbm,
    pay_a, pay_b, stress_ref, tile_idx, mean_ref, harm_ref, flow_ref, links_ref, weight_ref, jac_ref, source_ref,
    step_ref, tiles_ref, sems,
):
    waits = fetch(
        (tiles_hbm, mean_hbm, harm_hbm, flow_hbm, links_hbm, weight_hbm, jac_hbm, source_hbm, step_hbm),
        (tiles_ref, mean_ref, harm_ref, flow_ref, links_ref, weight_ref, jac_ref, source_ref, step_ref),
        sems,
    )
    for wait in waits[:3]:
        wait()
    lowers_first = place_ref[0] % 2 == 1
    lower, upper = (
        packed(lambda t, k=k: tiles_ref[k : k + 1, t * LANES : (t + 1) * LANES], 0) for k in range(2)
    )
    first = jnp.where(lowers_first, lower, upper)
    second = jnp.where(lowers_first, upper, lower)
    tile_idx[0] = first
    tile_idx[1] = second
    row = native_row(mean_ref, harm_ref)
    groups = mean_ref.shape[1] // LANES
    store_tiles(row, (first, second), pay_a, pay_b, groups)
    waits[3]()
    flow = native_row(mean_ref, flow_ref)
    product = lambda r, t: row(r, t) * flow(r, t)
    for v in range(VARS):
        for g in range(0, groups, SUBS):
            stress_ref[v, g : g + SUBS, :] = packed(
                lambda t: product(VARS + v, t) + product(2 * VARS + v, t), g
            )
    for wait in waits[4:]:
        wait()


TOP = float(2**20 - 1)


def largest(values):
    top = jnp.abs(values[0])
    for value in values[1:]:
        top = jnp.maximum(top, jnp.abs(value))
    top = jnp.max(jnp.max(top, axis=0, keepdims=True), axis=1, keepdims=True)
    return jnp.maximum(jnp.broadcast_to(top, (SUBS, LANES)), 1e-30)


def pack_table(load, blocks, fields, words_ref):
    unit = {}
    scale = {}
    for kind in ([r for r in fields if r < VARS], [r for r in fields if r >= VARS]):
        if kind:
            top = largest([load(r, g) for r in kind for g in range(blocks)])
            for r in kind:
                unit[r] = top * (1.0 / TOP)
                scale[r] = TOP / top
    fixed = lambda r, g: jnp.floor(load(r, g) * scale[r] + 0.5).astype(jnp.int32)
    for i in range(len(fields) // 3):
        for g in range(blocks):
            at = slice(g * SUBS, (g + 1) * SUBS)
            first, second, third = (fixed(r, g) for r in fields[3 * i : 3 * i + 3])
            words_ref[2 * i, at, :] = (first << 11) | ((third >> 10) & 0x7FF)
            words_ref[2 * i + 1, at, :] = (second << 11) | (third & 0x3FF)
    return unit


def gather_into(row, fields, count, words_ref, first, index_ref, weight_ref, begin, faces, unit, start):
    triples = len(fields) // 3
    words = 2 * triples
    rest = fields[3 * triples :]

    def word(w, h):
        return words_ref[w, h : h + 1, :] if w < words else row(rest[w - words], h)

    def face(f, acc):
        found = picked(word, range(words + len(rest)), count, index_ref[begin + f] - first)
        weight = weight_ref[begin + f]
        values = []
        for i in range(triples):
            one, two = found[2 * i], found[2 * i + 1]
            values += [one >> 11, two >> 11, ((one << 21) >> 11) | (two & 0x3FF)]
        values = [v.astype(F32) for v in values] + found[words:]
        return tuple(a + weight * v for a, v in zip(acc, values))

    sums = (jnp.zeros((SUBS, LANES), F32),) * len(fields)
    for f in range(faces):
        sums = face(f, sums)
    return [
        s + (a if i >= 3 * triples else unit[r] * a) for i, (r, s, a) in enumerate(zip(fields, start, sums))
    ]


def core_of(place_ref):
    return place_ref[0] // 2


def gather_fields(row, fields, count, words_ref, first, index_ref, weight_ref, unit, start, out_ref, lead=0):
    for g in range(index_ref.shape[0] // FACES):
        at = slice(g * SUBS, (g + 1) * SUBS)
        values = gather_into(
            row, fields, count, words_ref, first, index_ref, weight_ref, g * FACES, FACES, unit,
            [start(r - lead, at) for r in fields],
        )
        for r, value in zip(fields, values):
            out_ref[r - lead, at, :] = value


def zero_start(*_):
    return jnp.zeros((SUBS, LANES), F32)


def prepare_kernel(
    place_ref, mean_ref, harm_ref, flow_ref, links_ref, weight_in, jac_ref, source_ref,
    acc_ref, share_ref, index_ref, weight_ref, wsum_ref, mean_out, state_ref, jac_out, flow_out, source_out,
    words_ref, mean_words,
):
    groups = mean_ref.shape[1] // LANES
    flips = place_ref[0] % 2 == 0
    rim = groups * LANES
    lane = lambda t: slice(t * LANES, (t + 1) * LANES)
    for g in range(groups // SUBS):
        total = None
        for f in range(FACES):
            link = packed(lambda t: links_ref[f : f + 1, lane(t)], g * SUBS)
            flipped = jnp.where(link >= rim, link ^ (rim // 2), link)
            index_ref[g * FACES + f] = jnp.where(flips, flipped, link)
            weight = packed(lambda t: weight_in[f : f + 1, lane(t)], g * SUBS)
            weight_ref[g * FACES + f] = weight
            total = weight if total is None else total + weight
        wsum_ref[g * SUBS : (g + 1) * SUBS, :] = total
    row = native_row(mean_ref, harm_ref)
    flow = native_row(mean_ref, flow_ref)
    for g in range(0, groups, SUBS):
        at = slice(g, g + SUBS)
        for r in range(VARS):
            mean_out[r, at, :] = packed(lambda t: row(r, t), g)
        for r in range(2 * VARS):
            state_ref[r, at, :] = packed(lambda t: row(VARS + r, t), g)
    row = fields_row(mean_out, state_ref)
    load = fields_block(mean_out, state_ref)
    unit = pack_table(load, groups // SUBS, HARM_FIELDS, words_ref)
    mean_unit = pack_table(load, groups // SUBS, MEAN_FIELDS, mean_words)
    gather_fields(
        row, HARM_FIELDS, groups, words_ref, 0, index_ref, weight_ref, unit, zero_start, acc_ref, VARS
    )
    values = gather_into(
        row, MEAN_FIELDS, groups, mean_words, 0, index_ref, weight_ref, core_of(place_ref) * FACES, FACES, mean_unit,
        [zero_start()] * VARS,
    )
    for r, value in enumerate(values):
        share_ref[r] = value
    for g in range(0, groups, SUBS):
        at = slice(g, g + SUBS)
        for r in range(2 * VARS):
            flow_out[r, at, :] = packed(lambda t: flow(VARS + r, t), g)
        for v in range(VARS):
            source_out[v, at, :] = packed(lambda t: source_ref[v : v + 1, lane(t)], g)
        for j in range(VARS):
            for i in range(VARS):
                jac_out[j * VARS + i, at, :] = packed(lambda t: jac_ref[j, i : i + 1, lane(t)], g)


def fields_row(mean_ref, harm_ref):
    def row(r, h):
        return mean_ref[r, h : h + 1, :] if r < VARS else harm_ref[r - VARS, h : h + 1, :]

    return row


def fields_block(mean_ref, harm_ref):
    def load(r, g):
        at = slice(g * SUBS, (g + 1) * SUBS)
        return mean_ref[r, at, :] if r < VARS else harm_ref[r - VARS, at, :]

    return load


def rim_row(*rims):
    rows = rims[0].shape[1]
    return lambda r, h: rims[h // rows][r, h % rows : h % rows + 1, :]


def rim_block(*rims):
    blocks = rims[0].shape[1] // SUBS
    return lambda r, g: rims[g // blocks][r, g % blocks * SUBS : (g % blocks + 1) * SUBS, :]


def near_kernel(rim, index_ref, weight_ref, out_ref, words_ref):
    rows = rim.shape[1]
    first = (out_ref.shape[1] + rows) * LANES
    unit = pack_table(rim_block(rim), rows // SUBS, ALL_FIELDS, words_ref)
    gather_fields(
        rim_row(rim), ALL_FIELDS, rows, words_ref, first, index_ref, weight_ref, unit, zero_start, out_ref
    )


def transposed(jac_ref, at, flux):
    out = []
    for i in range(VARS):
        res = jac_ref[i, at, :] * flux[0]
        for j in range(1, VARS):
            res = res + jac_ref[j * VARS + i, at, :] * flux[j]
        out.append(res)
    return out


def harm_step(order_ref, at, mean, state, start, gathered, wsum, scale, jac_ref, flow_ref, out_ref):
    omega = BASE_FREQ * (order_ref[0].astype(F32) + 1.0)
    flux = [wsum * s - x for s, x in zip(state, gathered)]
    for part in range(2):
        res = transposed(jac_ref, at, flux[part * VARS : (part + 1) * VARS])
        for i in range(VARS):
            r = part * VARS + i
            turned = omega * state[(1 - part) * VARS + i]
            full = res[i] + turned if part == 0 else res[i] - turned
            full = full - mean[i] * flow_ref[r, at, :]
            out_ref[r, at, :] = start[r] - scale * full


def middle_kernel(
    place_ref, order_ref, acc_ref, share_ref, rim_a, rim_b, stress_a, stress_b, index_ref, weight_ref, wsum_ref, mean_ref, state_ref,
    jac_ref, flow_ref, source_ref, step_ref, out_ref, part_ref, full_ref, mean_acc, words_ref, mean_words, *, coeff,
):
    groups = acc_ref.shape[1]
    rows = 2 * rim_a.shape[1]
    row, load = rim_row(rim_a, rim_b), rim_block(rim_a, rim_b)
    unit = pack_table(load, rows // SUBS, HARM_FIELDS, words_ref)
    mean_unit = pack_table(load, rows // SUBS, MEAN_FIELDS, mean_words)
    gather_fields(
        row, HARM_FIELDS, rows, words_ref, groups * LANES, index_ref, weight_ref, unit,
        lambda r, at: acc_ref[r, at, :], full_ref, VARS,
    )
    half = core_of(place_ref)
    lead = half == 0
    values = gather_into(
        row, MEAN_FIELDS, rows, mean_words, groups * LANES, index_ref, weight_ref, half * FACES, FACES,
        mean_unit, [share_ref[r] for r in range(VARS)],
    )
    mean_acc[...] = jnp.zeros(mean_acc.shape, F32)
    for r, value in enumerate(values):
        mean_acc[r, pl.ds(pl.multiple_of(half * SUBS, SUBS), SUBS), :] = value
    for g in range(groups // SUBS):
        at = slice(g * SUBS, (g + 1) * SUBS)
        mean = [mean_ref[v, at, :] for v in range(VARS)]
        state = [state_ref[r, at, :] for r in range(2 * VARS)]
        wsum = wsum_ref[at, :]
        scale = coeff * step_ref[at, :]
        flux = []
        for v in range(VARS):
            stress = stress_a[v, at, :] + stress_b[v, at, :]
            flux.append(jnp.where(lead, wsum * mean[v], 0.0) - mean_acc[v, at, :] - stress)
        for v, res in enumerate(transposed(jac_ref, at, flux)):
            own = jnp.where(lead, mean[v] + scale * source_ref[v, at, :], 0.0)
            part_ref[v, at, :] = own - scale * res
        gathered = [full_ref[r, at, :] for r in range(2 * VARS)]
        harm_step(order_ref, at, mean, state, state, gathered, wsum, scale, jac_ref, flow_ref, out_ref)
        for v in range(VARS):
            part_ref[VARS + v, at, :] = (
                out_ref[v, at, :] * flow_ref[v, at, :] + out_ref[VARS + v, at, :] * flow_ref[VARS + v, at, :]
            )


def join_kernel(parts_ref, state_ref, tile_idx, mean_ref, stress_ref, pay_a, pay_b):
    for v in range(VARS):
        for ref, r in ((mean_ref, v), (stress_ref, VARS + v)):
            ref[v] = parts_ref[0, r] + parts_ref[1, r]
    row = fields_row(mean_ref, state_ref)
    store_tiles(row, (tile_idx[0], tile_idx[1]), pay_a, pay_b, mean_ref.shape[1])


def own_kernel(
    order_ref, index_ref, weight_ref, wsum_ref, mean_ref, state_ref, mean_start, harm_start,
    jac_ref, flow_ref, source_ref, step_ref, mean_base, harm_base, full_ref, words_ref, *, coeff,
):
    groups = mean_ref.shape[1]
    unit = pack_table(fields_block(mean_ref, state_ref), groups // SUBS, ALL_FIELDS, words_ref)
    gather_fields(
        fields_row(mean_ref, state_ref), ALL_FIELDS, groups, words_ref, 0, index_ref, weight_ref, unit,
        zero_start, full_ref,
    )
    for g in range(groups // SUBS):
        at = slice(g * SUBS, (g + 1) * SUBS)
        mean = [mean_ref[v, at, :] for v in range(VARS)]
        state = [state_ref[r, at, :] for r in range(2 * VARS)]
        wsum = wsum_ref[at, :]
        scale = coeff * step_ref[at, :]
        flux = [wsum * m - full_ref[v, at, :] for v, m in enumerate(mean)]
        for v, res in enumerate(transposed(jac_ref, at, flux)):
            mean_base[v, at, :] = mean_start[v, at, :] - scale * (res - source_ref[v, at, :])
        gathered = [full_ref[VARS + r, at, :] for r in range(2 * VARS)]
        start = [harm_start[r, at, :] for r in range(2 * VARS)]
        harm_step(order_ref, at, mean, state, start, gathered, wsum, scale, jac_ref, flow_ref, harm_base)


def close_kernel(
    rim, index_ref, weight_ref, jac_ref, step_ref, mean_base, harm_base, near_ref, stress_a, stress_b,
    mean_hbm, harm_hbm, full_ref, words_ref, mean_out, harm_out, sems, *, coeff,
):
    groups = mean_base.shape[1]
    rows = rim.shape[1]
    unit = pack_table(rim_block(rim), rows // SUBS, ALL_FIELDS, words_ref)
    base = fields_block(mean_base, harm_base)
    copies = []
    for g in range(groups // SUBS):
        at = slice(g * SUBS, (g + 1) * SUBS)
        full = gather_into(
            rim_row(rim), ALL_FIELDS, rows, words_ref, groups * LANES, index_ref, weight_ref, g * FACES, FACES,
            unit, [near_ref[r, at, :] for r in ALL_FIELDS],
        )
        for v in range(VARS):
            full[v] = full[v] + (stress_a[v, at, :] + stress_b[v, at, :])
        scale = coeff * step_ref[at, :]
        for first in range(0, ROWS, VARS):
            for v, res in enumerate(transposed(jac_ref, at, full[first : first + VARS])):
                full_ref[first + v, at, :] = base(first + v, g) + scale * res
        for t in range(g * SUBS, (g + 1) * SUBS):
            lanes = slice(t * LANES, (t + 1) * LANES)
            mean_out[:, lanes] = stacked(lambda i: full_ref[i, t : t + 1, :], VARS)
            for v in range(VARS):
                harm_out[v, :, lanes] = stacked(lambda i: full_ref[(i + 1) * VARS + v, t : t + 1, :], 2)
        part = pl.ds(g * SUBS * LANES, SUBS * LANES)
        for i, (out, hbm) in enumerate(
            ((mean_out.at[:, part], mean_hbm.at[:, part]), (harm_out.at[:, :, part], harm_hbm.at[:, :, part]))
        ):
            copies.append(pltpu.make_async_copy(out, hbm, sems.at[2 * g + i]))
            copies[-1].start()
    for copy in copies:
        copy.wait()


def stacked(row, count):
    sub = lax.broadcasted_iota(jnp.int32, (count, LANES), 0)
    out = jnp.broadcast_to(row(0), (count, LANES))
    for i in range(1, count):
        out = jnp.where(sub == i, jnp.broadcast_to(row(i), (count, LANES)), out)
    return out


def held(*arrays):
    return [*(pltpu.VMEM(a.shape, a.dtype) for a in arrays), pltpu.SemaphoreType.DMA((SUBS,))]


def launch(body, out_shape, scalars, args, raw=(), scratch=()):
    smem = pl.BlockSpec(memory_space=pltpu.SMEM)
    vmem = pl.BlockSpec(memory_space=pltpu.VMEM)
    anywhere = pl.BlockSpec(memory_space=pl.ANY)
    return pl.pallas_call(
        body,
        out_shape=out_shape,
        in_specs=[smem] * len(scalars) + [anywhere] * len(raw) + [vmem] * len(args),
        out_specs=[anywhere if isinstance(s, jax.ShapeDtypeStruct) else vmem for s in out_shape],
        scratch_shapes=scratch,
    )(*scalars, *raw, *(pltpu.with_memory_space_constraint(a, pltpu.VMEM) for a in args))


def exchange(pay_a, pay_b, stress):
    count = lax.axis_size("cells")
    near = [(b, b ^ 1) for b in range(count)]
    far = [(b, (b - 1 + 2 * (b % 2)) % count) for b in range(count)]
    rim_a = lax.ppermute(pay_a, "cells", far)
    rim_b = lax.ppermute(pay_b, "cells", near)
    other = lax.ppermute(stress, HARM[0], [(0, 1), (1, 0)])
    return rim_a, rim_b, other


def shards(
    mean_adjoint,
    harm_adjoint,
    harm_flow,
    flux_jacobian,
    face_weight,
    face_links,
    face_tiles,
    pseudo_step,
    mean_source,
    harm_order,
):
    cells = mean_adjoint.shape[1]
    groups = cells // LANES
    halves = groups // SUBS
    rim_rows = face_tiles.shape[1] // LANES
    harm_adjoint, harm_flow = (
        a[0].swapaxes(0, 1) for a in (harm_adjoint, harm_flow)
    )
    place = (1 - lax.axis_index("cells") % 2 + 2 * lax.axis_index(HARM[1])).astype(jnp.int32)[None]
    step = pseudo_step.reshape(groups, LANES)
    mean_fields, harm_fields = struct(VARS, groups, LANES), struct(2 * VARS, groups, LANES)
    pays = (struct(ROWS, rim_rows, LANES), struct(ROWS, rim_rows, LANES))
    raw = (
        mean_adjoint, harm_adjoint, harm_flow, face_links, face_weight, flux_jacobian, mean_source, step
    )
    held_raw = tuple(struct(*a.shape, dtype=a.dtype) for a in raw)
    pay_a, pay_b, stress, tile_idx, *inside, step = launch(
        open_kernel, pays + (mean_fields, struct(2, rim_rows, LANES, dtype=jnp.int32),) + held_raw, (place,), (),
        (face_tiles, *raw), [pltpu.VMEM(face_tiles.shape, jnp.int32), pltpu.SemaphoreType.DMA((9,))],
    )
    rim_a, rim_b, other = exchange(pay_a, pay_b, stress)
    registers = FACES * halves
    words = lambda fields: struct(max(len(fields) // 3 * 2, 1), groups, LANES, dtype=jnp.int32)
    harm_words, mean_words = words(HARM_FIELDS), words(MEAN_FIELDS)
    acc, share, index, weight, wsum, mean_start, harm_start, jac, flow, source = launch(
        prepare_kernel,
        (
            harm_fields,
            struct(VARS, SUBS, LANES),
            struct(registers, SUBS, LANES, dtype=jnp.int32),
            struct(registers, SUBS, LANES),
            struct(groups, LANES),
            mean_fields,
            harm_fields,
            struct(VARS * VARS, groups, LANES),
            harm_fields,
            mean_fields,
        ),
        (place,), inside,
        scratch=[harm_words, mean_words],
    )
    state, part = launch(
        lambda *refs: middle_kernel(*refs, coeff=1.0 / SECTIONS), (harm_fields, harm_fields),
        (place, harm_order),
        (acc, share, rim_a, rim_b, stress, other, index, weight, wsum, mean_start, harm_start, jac, flow, source, step),
        scratch=[harm_fields, mean_fields, harm_words, mean_words],
    )
    parts = lax.all_gather(part, HARM[1])
    mean, stress, pay_a, pay_b = launch(join_kernel, (mean_fields, mean_fields) + pays, (), (parts, state, tile_idx))
    rim_a, rim_b, other = exchange(pay_a, pay_b, stress)
    fields = struct(ROWS, groups, LANES)
    mean_base, harm_base = launch(
        lambda *refs: own_kernel(*refs, coeff=1.0), (mean_fields, harm_fields), (harm_order,),
        (index, weight, wsum, mean, state, mean_start, harm_start, jac, flow, source, step),
        scratch=[fields, words(ALL_FIELDS)],
    )
    (near,) = launch(near_kernel, (fields,), (), (rim_b, index, weight), scratch=[words(ALL_FIELDS)])
    outs = [jax.ShapeDtypeStruct(s, F32) for s in ((VARS, cells), (VARS, 2, cells))]
    mean_new, harm_new = launch(
        lambda *refs: close_kernel(*refs, coeff=1.0), tuple(outs), (),
        (rim_a, index, weight, jac, step, mean_base, harm_base, near, stress, other),
        scratch=[fields, words(ALL_FIELDS), *held(*outs)],
    )
    return mean_new, harm_new.swapaxes(0, 1)[None]


def solution(mesh):
    finer = Mesh(mesh.devices.reshape(mesh.shape["cells"], 2, 2), ("cells", *HARM))
    return jax.shard_map(
        shards,
        mesh=finer,
        in_specs=(
            P(None, "cells"),
            P(HARM, None, None, "cells"),
            P(HARM, None, None, "cells"),
            P(None, None, "cells"),
            P(None, "cells"),
            P(None, "cells"),
            P(None, "cells"),
            P("cells"),
            P(None, "cells"),
            P(HARM),
        ),
        out_specs=(P(None, "cells"), P(HARM, None, None, "cells")),
        check_vma=False,
    )
```

```python
import jax
import jax.numpy as jnp
from jax import lax
from jax.experimental import pallas as pl
from jax.experimental.pallas import tpu as pltpu
from jax.sharding import Mesh
from jax.sharding import PartitionSpec as P

VARS = 5
FACES = 6
SECTIONS = 2
ROWS = 3 * VARS
MEAN_FIELDS = range(VARS)
HARM_FIELDS = range(VARS, ROWS)
ALL_FIELDS = range(ROWS)
HARM = ("harm_0", "harm_1")
LANES = 128
SUBS = 8
BASE_FREQ = 0.8
F32 = jnp.float32


def struct(*shape, dtype=F32):
    return pltpu.VMEM(shape, dtype)


def spread(row):
    return jnp.broadcast_to(row, (SUBS, LANES))


def packed(tile, first):
    sub = lax.broadcasted_iota(jnp.int32, (SUBS, LANES), 0)
    out = spread(tile(first))
    for i in range(1, SUBS):
        out = jnp.where(sub == i, spread(tile(first + i)), out)
    return out


def picked(row, fields, count, index):
    low = index & (LANES - 1)
    high = index >> 7
    out = [None] * len(fields)
    for h in range(count):
        hit = high == h
        for i, r in enumerate(fields):
            value = jnp.take_along_axis(spread(row(r, h)), low, axis=1)
            out[i] = jnp.where(hit, value, jnp.zeros_like(value) if h == 0 else out[i])
    return out


def store_tiles(row, tile_index, pay_a, pay_b, rows):
    for pay, index in zip((pay_a, pay_b), tile_index):
        for r, value in enumerate(picked(row, range(ROWS), rows, index)):
            pay[r] = value


def native_row(mean_ref, harm_ref):
    def row(r, h):
        lanes = slice(h * LANES, (h + 1) * LANES)
        if r < VARS:
            return mean_ref[r : r + 1, lanes]
        part, var = divmod(r - VARS, VARS)
        return harm_ref[var, part : part + 1, lanes]

    return row


def fetch(sources, targets, sems):
    copies = [pltpu.make_async_copy(s, t, sems.at[i]) for i, (s, t) in enumerate(zip(sources, targets))]
    for copy in copies:
        copy.start()
    return [copy.wait for copy in copies]


def open_kernel(
    place_ref, tiles_hbm, mean_hbm, harm_hbm, flow_hbm, links_hbm, weight_hbm, jac_hbm, source_hbm, step_hbm,
    pay_a, pay_b, stress_ref, tile_idx, mean_ref, harm_ref, flow_ref, links_ref, weight_ref, jac_ref, source_ref,
    step_ref, tiles_ref, sems,
):
    waits = fetch(
        (tiles_hbm, mean_hbm, harm_hbm, flow_hbm, links_hbm, weight_hbm, jac_hbm, source_hbm, step_hbm),
        (tiles_ref, mean_ref, harm_ref, flow_ref, links_ref, weight_ref, jac_ref, source_ref, step_ref),
        sems,
    )
    for wait in waits[:3]:
        wait()
    lowers_first = place_ref[0] % 2 == 1
    lower, upper = (
        packed(lambda t, k=k: tiles_ref[k : k + 1, t * LANES : (t + 1) * LANES], 0) for k in range(2)
    )
    first = jnp.where(lowers_first, lower, upper)
    second = jnp.where(lowers_first, upper, lower)
    tile_idx[0] = first
    tile_idx[1] = second
    row = native_row(mean_ref, harm_ref)
    groups = mean_ref.shape[1] // LANES
    store_tiles(row, (first, second), pay_a, pay_b, groups)
    waits[3]()
    flow = native_row(mean_ref, flow_ref)
    product = lambda r, t: row(r, t) * flow(r, t)
    for v in range(VARS):
        for g in range(0, groups, SUBS):
            stress_ref[v, g : g + SUBS, :] = packed(
                lambda t: product(VARS + v, t) + product(2 * VARS + v, t), g
            )
    for wait in waits[4:]:
        wait()


TOP = float(2**20 - 1)


def largest(values):
    top = jnp.abs(values[0])
    for value in values[1:]:
        top = jnp.maximum(top, jnp.abs(value))
    top = jnp.max(jnp.max(top, axis=0, keepdims=True), axis=1, keepdims=True)
    return jnp.maximum(jnp.broadcast_to(top, (SUBS, LANES)), 1e-30)


def pack_table(load, blocks, fields, words_ref):
    unit = {}
    scale = {}
    for kind in ([r for r in fields if r < VARS], [r for r in fields if r >= VARS]):
        if kind:
            top = largest([load(r, g) for r in kind for g in range(blocks)])
            for r in kind:
                unit[r] = top * (1.0 / TOP)
                scale[r] = TOP / top
    fixed = lambda r, g: jnp.floor(load(r, g) * scale[r] + 0.5).astype(jnp.int32)
    for i in range(len(fields) // 3):
        for g in range(blocks):
            at = slice(g * SUBS, (g + 1) * SUBS)
            first, second, third = (fixed(r, g) for r in fields[3 * i : 3 * i + 3])
            words_ref[2 * i, at, :] = (first << 11) | ((third >> 10) & 0x7FF)
            words_ref[2 * i + 1, at, :] = (second << 11) | (third & 0x3FF)
    return unit


def gather_into(row, fields, count, words_ref, first, index_ref, weight_ref, begin, faces, unit, start):
    triples = len(fields) // 3
    words = 2 * triples
    rest = fields[3 * triples :]

    def word(w, h):
        return words_ref[w, h : h + 1, :] if w < words else row(rest[w - words], h)

    def face(f, acc):
        found = picked(word, range(words + len(rest)), count, index_ref[begin + f] - first)
        weight = weight_ref[begin + f]
        values = []
        for i in range(triples):
            one, two = found[2 * i], found[2 * i + 1]
            values += [one >> 11, two >> 11, ((one << 21) >> 11) | (two & 0x3FF)]
        values = [v.astype(F32) for v in values] + found[words:]
        return tuple(a + weight * v for a, v in zip(acc, values))

    sums = (jnp.zeros((SUBS, LANES), F32),) * len(fields)
    for f in range(faces):
        sums = face(f, sums)
    return [
        s + (a if i >= 3 * triples else unit[r] * a) for i, (r, s, a) in enumerate(zip(fields, start, sums))
    ]


def core_of(place_ref):
    return place_ref[0] // 2


def gather_fields(row, fields, count, words_ref, first, index_ref, weight_ref, unit, start, out_ref, lead=0):
    for g in range(index_ref.shape[0] // FACES):
        at = slice(g * SUBS, (g + 1) * SUBS)
        values = gather_into(
            row, fields, count, words_ref, first, index_ref, weight_ref, g * FACES, FACES, unit,
            [start(r - lead, at) for r in fields],
        )
        for r, value in zip(fields, values):
            out_ref[r - lead, at, :] = value


def zero_start(*_):
    return jnp.zeros((SUBS, LANES), F32)


def prepare_kernel(
    place_ref, mean_ref, harm_ref, flow_ref, links_ref, weight_in, jac_ref, source_ref,
    acc_ref, share_ref, index_ref, weight_ref, wsum_ref, mean_out, state_ref, jac_out, flow_out, source_out,
    words_ref, mean_words,
):
    groups = mean_ref.shape[1] // LANES
    flips = place_ref[0] % 2 == 0
    rim = groups * LANES
    lane = lambda t: slice(t * LANES, (t + 1) * LANES)
    for g in range(groups // SUBS):
        total = None
        for f in range(FACES):
            link = packed(lambda t: links_ref[f : f + 1, lane(t)], g * SUBS)
            flipped = jnp.where(link >= rim, link ^ (rim // 2), link)
            index_ref[g * FACES + f] = jnp.where(flips, flipped, link)
            weight = packed(lambda t: weight_in[f : f + 1, lane(t)], g * SUBS)
            weight_ref[g * FACES + f] = weight
            total = weight if total is None else total + weight
        wsum_ref[g * SUBS : (g + 1) * SUBS, :] = total
    row = native_row(mean_ref, harm_ref)
    flow = native_row(mean_ref, flow_ref)
    for g in range(0, groups, SUBS):
        at = slice(g, g + SUBS)
        for r in range(VARS):
            mean_out[r, at, :] = packed(lambda t: row(r, t), g)
        for r in range(2 * VARS):
            state_ref[r, at, :] = packed(lambda t: row(VARS + r, t), g)
    row = fields_row(mean_out, state_ref)
    load = fields_block(mean_out, state_ref)
    unit = pack_table(load, groups // SUBS, HARM_FIELDS, words_ref)
    mean_unit = pack_table(load, groups // SUBS, MEAN_FIELDS, mean_words)
    gather_fields(
        row, HARM_FIELDS, groups, words_ref, 0, index_ref, weight_ref, unit, zero_start, acc_ref, VARS
    )
    values = gather_into(
        row, MEAN_FIELDS, groups, mean_words, 0, index_ref, weight_ref, core_of(place_ref) * FACES, FACES, mean_unit,
        [zero_start()] * VARS,
    )
    for r, value in enumerate(values):
        share_ref[r] = value
    for g in range(0, groups, SUBS):
        at = slice(g, g + SUBS)
        for r in range(2 * VARS):
            flow_out[r, at, :] = packed(lambda t: flow(VARS + r, t), g)
        for v in range(VARS):
            source_out[v, at, :] = packed(lambda t: source_ref[v : v + 1, lane(t)], g)
        for j in range(VARS):
            for i in range(VARS):
                jac_out[j * VARS + i, at, :] = packed(lambda t: jac_ref[j, i : i + 1, lane(t)], g)


def fields_row(mean_ref, harm_ref):
    def row(r, h):
        return mean_ref[r, h : h + 1, :] if r < VARS else harm_ref[r - VARS, h : h + 1, :]

    return row


def fields_block(mean_ref, harm_ref):
    def load(r, g):
        at = slice(g * SUBS, (g + 1) * SUBS)
        return mean_ref[r, at, :] if r < VARS else harm_ref[r - VARS, at, :]

    return load


def rim_row(*rims):
    rows = rims[0].shape[1]
    return lambda r, h: rims[h // rows][r, h % rows : h % rows + 1, :]


def rim_block(*rims):
    blocks = rims[0].shape[1] // SUBS
    return lambda r, g: rims[g // blocks][r, g % blocks * SUBS : (g % blocks + 1) * SUBS, :]


def near_kernel(rim, index_ref, weight_ref, out_ref, words_ref):
    rows = rim.shape[1]
    first = (out_ref.shape[1] + rows) * LANES
    unit = pack_table(rim_block(rim), rows // SUBS, ALL_FIELDS, words_ref)
    gather_fields(
        rim_row(rim), ALL_FIELDS, rows, words_ref, first, index_ref, weight_ref, unit, zero_start, out_ref
    )


def transposed(jac_ref, at, flux):
    out = []
    for i in range(VARS):
        res = jac_ref[i, at, :] * flux[0]
        for j in range(1, VARS):
            res = res + jac_ref[j * VARS + i, at, :] * flux[j]
        out.append(res)
    return out


def harm_step(order_ref, at, mean, state, start, gathered, wsum, scale, jac_ref, flow_ref, out_ref):
    omega = BASE_FREQ * (order_ref[0].astype(F32) + 1.0)
    flux = [wsum * s - x for s, x in zip(state, gathered)]
    for part in range(2):
        res = transposed(jac_ref, at, flux[part * VARS : (part + 1) * VARS])
        for i in range(VARS):
            r = part * VARS + i
            turned = omega * state[(1 - part) * VARS + i]
            full = res[i] + turned if part == 0 else res[i] - turned
            full = full - mean[i] * flow_ref[r, at, :]
            out_ref[r, at, :] = start[r] - scale * full


def rims_kernel(
    place_ref, acc_ref, share_ref, rim_a, rim_b, index_ref, weight_ref, full_ref, mean_acc, words_ref, mean_words
):
    groups = acc_ref.shape[1]
    rows = 2 * rim_a.shape[1]
    row, load = rim_row(rim_a, rim_b), rim_block(rim_a, rim_b)
    unit = pack_table(load, rows // SUBS, HARM_FIELDS, words_ref)
    mean_unit = pack_table(load, rows // SUBS, MEAN_FIELDS, mean_words)
    gather_fields(
        row, HARM_FIELDS, rows, words_ref, groups * LANES, index_ref, weight_ref, unit,
        lambda r, at: acc_ref[r, at, :], full_ref, VARS,
    )
    half = core_of(place_ref)
    values = gather_into(
        row, MEAN_FIELDS, rows, mean_words, groups * LANES, index_ref, weight_ref, half * FACES, FACES,
        mean_unit, [share_ref[r] for r in range(VARS)],
    )
    mean_acc[...] = jnp.zeros(mean_acc.shape, F32)
    for r, value in enumerate(values):
        mean_acc[r, pl.ds(pl.multiple_of(half * SUBS, SUBS), SUBS), :] = value


def middle_kernel(
    place_ref, order_ref, full_ref, mean_acc, stress_a, stress_b, wsum_ref, mean_ref, state_ref,
    jac_ref, flow_ref, source_ref, step_ref, out_ref, part_ref, *, coeff,
):
    groups = full_ref.shape[1]
    lead = core_of(place_ref) == 0
    for g in range(groups // SUBS):
        at = slice(g * SUBS, (g + 1) * SUBS)
        mean = [mean_ref[v, at, :] for v in range(VARS)]
        state = [state_ref[r, at, :] for r in range(2 * VARS)]
        wsum = wsum_ref[at, :]
        scale = coeff * step_ref[at, :]
        flux = []
        for v in range(VARS):
            stress = stress_a[v, at, :] + stress_b[v, at, :]
            flux.append(jnp.where(lead, wsum * mean[v], 0.0) - mean_acc[v, at, :] - stress)
        for v, res in enumerate(transposed(jac_ref, at, flux)):
            own = jnp.where(lead, mean[v] + scale * source_ref[v, at, :], 0.0)
            part_ref[v, at, :] = own - scale * res
        gathered = [full_ref[r, at, :] for r in range(2 * VARS)]
        harm_step(order_ref, at, mean, state, state, gathered, wsum, scale, jac_ref, flow_ref, out_ref)
        for v in range(VARS):
            part_ref[VARS + v, at, :] = (
                out_ref[v, at, :] * flow_ref[v, at, :] + out_ref[VARS + v, at, :] * flow_ref[VARS + v, at, :]
            )


def join_kernel(parts_ref, state_ref, tile_idx, mean_ref, stress_ref, pay_a, pay_b):
    for v in range(VARS):
        for ref, r in ((mean_ref, v), (stress_ref, VARS + v)):
            ref[v] = parts_ref[0, r] + parts_ref[1, r]
    row = fields_row(mean_ref, state_ref)
    store_tiles(row, (tile_idx[0], tile_idx[1]), pay_a, pay_b, mean_ref.shape[1])


def own_kernel(
    order_ref, index_ref, weight_ref, wsum_ref, mean_ref, state_ref, mean_start, harm_start,
    jac_ref, flow_ref, source_ref, step_ref, mean_base, harm_base, full_ref, words_ref, *, coeff,
):
    groups = mean_ref.shape[1]
    unit = pack_table(fields_block(mean_ref, state_ref), groups // SUBS, ALL_FIELDS, words_ref)
    gather_fields(
        fields_row(mean_ref, state_ref), ALL_FIELDS, groups, words_ref, 0, index_ref, weight_ref, unit,
        zero_start, full_ref,
    )
    for g in range(groups // SUBS):
        at = slice(g * SUBS, (g + 1) * SUBS)
        mean = [mean_ref[v, at, :] for v in range(VARS)]
        state = [state_ref[r, at, :] for r in range(2 * VARS)]
        wsum = wsum_ref[at, :]
        scale = coeff * step_ref[at, :]
        flux = [wsum * m - full_ref[v, at, :] for v, m in enumerate(mean)]
        for v, res in enumerate(transposed(jac_ref, at, flux)):
            mean_base[v, at, :] = mean_start[v, at, :] - scale * (res - source_ref[v, at, :])
        gathered = [full_ref[VARS + r, at, :] for r in range(2 * VARS)]
        start = [harm_start[r, at, :] for r in range(2 * VARS)]
        harm_step(order_ref, at, mean, state, start, gathered, wsum, scale, jac_ref, flow_ref, harm_base)


def close_kernel(
    rim, index_ref, weight_ref, jac_ref, step_ref, mean_base, harm_base, near_ref, stress_a, stress_b,
    mean_hbm, harm_hbm, full_ref, words_ref, mean_out, harm_out, sems, *, coeff,
):
    groups = mean_base.shape[1]
    rows = rim.shape[1]
    unit = pack_table(rim_block(rim), rows // SUBS, ALL_FIELDS, words_ref)
    base = fields_block(mean_base, harm_base)
    copies = []
    for g in range(groups // SUBS):
        at = slice(g * SUBS, (g + 1) * SUBS)
        full = gather_into(
            rim_row(rim), ALL_FIELDS, rows, words_ref, groups * LANES, index_ref, weight_ref, g * FACES, FACES,
            unit, [near_ref[r, at, :] for r in ALL_FIELDS],
        )
        for v in range(VARS):
            full[v] = full[v] + (stress_a[v, at, :] + stress_b[v, at, :])
        scale = coeff * step_ref[at, :]
        for first in range(0, ROWS, VARS):
            for v, res in enumerate(transposed(jac_ref, at, full[first : first + VARS])):
                full_ref[first + v, at, :] = base(first + v, g) + scale * res
        for t in range(g * SUBS, (g + 1) * SUBS):
            lanes = slice(t * LANES, (t + 1) * LANES)
            mean_out[:, lanes] = stacked(lambda i: full_ref[i, t : t + 1, :], VARS)
            for v in range(VARS):
                harm_out[v, :, lanes] = stacked(lambda i: full_ref[(i + 1) * VARS + v, t : t + 1, :], 2)
        part = pl.ds(g * SUBS * LANES, SUBS * LANES)
        for i, (out, hbm) in enumerate(
            ((mean_out.at[:, part], mean_hbm.at[:, part]), (harm_out.at[:, :, part], harm_hbm.at[:, :, part]))
        ):
            copies.append(pltpu.make_async_copy(out, hbm, sems.at[2 * g + i]))
            copies[-1].start()
    for copy in copies:
        copy.wait()


def stacked(row, count):
    sub = lax.broadcasted_iota(jnp.int32, (count, LANES), 0)
    out = jnp.broadcast_to(row(0), (count, LANES))
    for i in range(1, count):
        out = jnp.where(sub == i, jnp.broadcast_to(row(i), (count, LANES)), out)
    return out


def held(*arrays):
    return [*(pltpu.VMEM(a.shape, a.dtype) for a in arrays), pltpu.SemaphoreType.DMA((SUBS,))]


def launch(body, out_shape, scalars, args, raw=(), scratch=()):
    smem = pl.BlockSpec(memory_space=pltpu.SMEM)
    vmem = pl.BlockSpec(memory_space=pltpu.VMEM)
    anywhere = pl.BlockSpec(memory_space=pl.ANY)
    return pl.pallas_call(
        body,
        out_shape=out_shape,
        in_specs=[smem] * len(scalars) + [anywhere] * len(raw) + [vmem] * len(args),
        out_specs=[anywhere if isinstance(s, jax.ShapeDtypeStruct) else vmem for s in out_shape],
        scratch_shapes=scratch,
    )(*scalars, *raw, *(pltpu.with_memory_space_constraint(a, pltpu.VMEM) for a in args))


def exchange(pay_a, pay_b, stress):
    count = lax.axis_size("cells")
    near = [(b, b ^ 1) for b in range(count)]
    far = [(b, (b - 1 + 2 * (b % 2)) % count) for b in range(count)]
    rim_a = lax.ppermute(pay_a, "cells", far)
    rim_b = lax.ppermute(pay_b, "cells", near)
    other = lax.ppermute(stress, HARM[0], [(0, 1), (1, 0)])
    return rim_a, rim_b, other


def shards(
    mean_adjoint,
    harm_adjoint,
    harm_flow,
    flux_jacobian,
    face_weight,
    face_links,
    face_tiles,
    pseudo_step,
    mean_source,
    harm_order,
):
    cells = mean_adjoint.shape[1]
    groups = cells // LANES
    halves = groups // SUBS
    rim_rows = face_tiles.shape[1] // LANES
    harm_adjoint, harm_flow = (
        a[0].swapaxes(0, 1) for a in (harm_adjoint, harm_flow)
    )
    place = (1 - lax.axis_index("cells") % 2 + 2 * lax.axis_index(HARM[1])).astype(jnp.int32)[None]
    step = pseudo_step.reshape(groups, LANES)
    mean_fields, harm_fields = struct(VARS, groups, LANES), struct(2 * VARS, groups, LANES)
    pays = (struct(ROWS, rim_rows, LANES), struct(ROWS, rim_rows, LANES))
    raw = (
        mean_adjoint, harm_adjoint, harm_flow, face_links, face_weight, flux_jacobian, mean_source, step
    )
    held_raw = tuple(struct(*a.shape, dtype=a.dtype) for a in raw)
    pay_a, pay_b, stress, tile_idx, *inside, step = launch(
        open_kernel, pays + (mean_fields, struct(2, rim_rows, LANES, dtype=jnp.int32),) + held_raw, (place,), (),
        (face_tiles, *raw), [pltpu.VMEM(face_tiles.shape, jnp.int32), pltpu.SemaphoreType.DMA((9,))],
    )
    rim_a, rim_b, other = exchange(pay_a, pay_b, stress)
    registers = FACES * halves
    words = lambda fields: struct(max(len(fields) // 3 * 2, 1), groups, LANES, dtype=jnp.int32)
    harm_words, mean_words = words(HARM_FIELDS), words(MEAN_FIELDS)
    acc, share, index, weight, wsum, mean_start, harm_start, jac, flow, source = launch(
        prepare_kernel,
        (
            harm_fields,
            struct(VARS, SUBS, LANES),
            struct(registers, SUBS, LANES, dtype=jnp.int32),
            struct(registers, SUBS, LANES),
            struct(groups, LANES),
            mean_fields,
            harm_fields,
            struct(VARS * VARS, groups, LANES),
            harm_fields,
            mean_fields,
        ),
        (place,), inside,
        scratch=[harm_words, mean_words],
    )
    full, mean_acc = launch(
        rims_kernel, (harm_fields, mean_fields), (place,), (acc, share, rim_a, rim_b, index, weight),
        scratch=[harm_words, mean_words],
    )
    state, part = launch(
        lambda *refs: middle_kernel(*refs, coeff=1.0 / SECTIONS), (harm_fields, harm_fields),
        (place, harm_order),
        (full, mean_acc, stress, other, wsum, mean_start, harm_start, jac, flow, source, step),
    )
    parts = lax.all_gather(part, HARM[1])
    mean, stress, pay_a, pay_b = launch(join_kernel, (mean_fields, mean_fields) + pays, (), (parts, state, tile_idx))
    rim_a, rim_b, other = exchange(pay_a, pay_b, stress)
    fields = struct(ROWS, groups, LANES)
    mean_base, harm_base = launch(
        lambda *refs: own_kernel(*refs, coeff=1.0), (mean_fields, harm_fields), (harm_order,),
        (index, weight, wsum, mean, state, mean_start, harm_start, jac, flow, source, step),
        scratch=[fields, words(ALL_FIELDS)],
    )
    (near,) = launch(near_kernel, (fields,), (), (rim_b, index, weight), scratch=[words(ALL_FIELDS)])
    outs = [jax.ShapeDtypeStruct(s, F32) for s in ((VARS, cells), (VARS, 2, cells))]
    mean_new, harm_new = launch(
        lambda *refs: close_kernel(*refs, coeff=1.0), tuple(outs), (),
        (rim_a, index, weight, jac, step, mean_base, harm_base, near, stress, other),
        scratch=[fields, words(ALL_FIELDS), *held(*outs)],
    )
    return mean_new, harm_new.swapaxes(0, 1)[None]


def solution(mesh):
    finer = Mesh(mesh.devices.reshape(mesh.shape["cells"], 2, 2), ("cells", *HARM))
    return jax.shard_map(
        shards,
        mesh=finer,
        in_specs=(
            P(None, "cells"),
            P(HARM, None, None, "cells"),
            P(HARM, None, None, "cells"),
            P(None, None, "cells"),
            P(None, "cells"),
            P(None, "cells"),
            P(None, "cells"),
            P("cells"),
            P(None, "cells"),
            P(HARM),
        ),
        out_specs=(P(None, "cells"), P(HARM, None, None, "cells")),
        check_vma=False,
    )
```

```python
import jax
import jax.numpy as jnp
from jax import lax
from jax.experimental import pallas as pl
from jax.experimental.pallas import tpu as pltpu
from jax.sharding import Mesh
from jax.sharding import PartitionSpec as P

VARS = 5
FACES = 6
SECTIONS = 2
ROWS = 3 * VARS
MEAN_FIELDS = range(VARS)
HARM_FIELDS = range(VARS, ROWS)
ALL_FIELDS = range(ROWS)
HARM = ("harm_0", "harm_1")
HARM_DEVICES = 4
LANES = 128
SUBS = 8
BASE_FREQ = 0.8
F32 = jnp.float32


def struct(*shape, dtype=F32):
    return pltpu.VMEM(shape, dtype)


def spread(row):
    return jnp.broadcast_to(row, (SUBS, LANES))


def packed(tile, first):
    sub = lax.broadcasted_iota(jnp.int32, (SUBS, LANES), 0)
    out = spread(tile(first))
    for i in range(1, SUBS):
        out = jnp.where(sub == i, spread(tile(first + i)), out)
    return out


def picked(row, fields, count, index):
    low = index & (LANES - 1)
    high = index >> 7
    out = [None] * len(fields)
    for h in range(count):
        hit = high == h
        for i, r in enumerate(fields):
            value = jnp.take_along_axis(spread(row(r, h)), low, axis=1)
            out[i] = jnp.where(hit, value, jnp.zeros_like(value) if h == 0 else out[i])
    return out


def store_tiles(row, tile_index, pay_a, pay_b, rows):
    for pay, index in zip((pay_a, pay_b), tile_index):
        for r, value in enumerate(picked(row, range(ROWS), rows, index)):
            pay[r] = value


def native_row(mean_ref, harm_ref):
    def row(r, h):
        lanes = slice(h * LANES, (h + 1) * LANES)
        if r < VARS:
            return mean_ref[r : r + 1, lanes]
        part, var = divmod(r - VARS, VARS)
        return harm_ref[var, part : part + 1, lanes]

    return row


def fetch(sources, targets, sems):
    copies = [pltpu.make_async_copy(s, t, sems.at[i]) for i, (s, t) in enumerate(zip(sources, targets))]
    for copy in copies:
        copy.start()
    return [copy.wait for copy in copies]


def open_kernel(
    place_ref, tiles_hbm, mean_hbm, harm_hbm, links_hbm, weight_hbm, flow_hbm, jac_hbm, source_hbm, step_hbm,
    pay_a, pay_b, tile_idx, mean_ref, harm_ref, links_ref, weight_ref, flow_ref, jac_ref, source_ref, step_ref,
    tiles_ref, sems,
):
    waits = fetch(
        (tiles_hbm, mean_hbm, harm_hbm, links_hbm, weight_hbm, flow_hbm, jac_hbm, source_hbm, step_hbm),
        (tiles_ref, mean_ref, harm_ref, links_ref, weight_ref, flow_ref, jac_ref, source_ref, step_ref),
        sems,
    )
    for wait in waits[:3]:
        wait()
    lowers_first = place_ref[0] % 2 == 1
    lower, upper = (
        packed(lambda t, k=k: tiles_ref[k : k + 1, t * LANES : (t + 1) * LANES], 0) for k in range(2)
    )
    first = jnp.where(lowers_first, lower, upper)
    second = jnp.where(lowers_first, upper, lower)
    tile_idx[0] = first
    tile_idx[1] = second
    row = native_row(mean_ref, harm_ref)
    store_tiles(row, (first, second), pay_a, pay_b, mean_ref.shape[1] // LANES)
    for wait in waits[3:]:
        wait()


TOP = float(2**20 - 1)


def largest(values):
    top = jnp.abs(values[0])
    for value in values[1:]:
        top = jnp.maximum(top, jnp.abs(value))
    top = jnp.max(jnp.max(top, axis=0, keepdims=True), axis=1, keepdims=True)
    return jnp.maximum(jnp.broadcast_to(top, (SUBS, LANES)), 1e-30)


def pack_table(load, blocks, fields, words_ref):
    unit = {}
    scale = {}
    for kind in ([r for r in fields if r < VARS], [r for r in fields if r >= VARS]):
        if kind:
            top = largest([load(r, g) for r in kind for g in range(blocks)])
            for r in kind:
                unit[r] = top * (1.0 / TOP)
                scale[r] = TOP / top
    fixed = lambda r, g: jnp.floor(load(r, g) * scale[r] + 0.5).astype(jnp.int32)
    for i in range(len(fields) // 3):
        for g in range(blocks):
            at = slice(g * SUBS, (g + 1) * SUBS)
            first, second, third = (fixed(r, g) for r in fields[3 * i : 3 * i + 3])
            words_ref[2 * i, at, :] = (first << 11) | ((third >> 10) & 0x7FF)
            words_ref[2 * i + 1, at, :] = (second << 11) | (third & 0x3FF)
    return unit


def gather_into(row, fields, count, words_ref, first, index_ref, weight_ref, begin, faces, unit, start):
    triples = len(fields) // 3
    words = 2 * triples
    rest = fields[3 * triples :]

    def word(w, h):
        return words_ref[w, h : h + 1, :] if w < words else row(rest[w - words], h)

    def face(f, acc):
        found = picked(word, range(words + len(rest)), count, index_ref[begin + f] - first)
        weight = weight_ref[begin + f]
        values = []
        for i in range(triples):
            one, two = found[2 * i], found[2 * i + 1]
            values += [one >> 11, two >> 11, ((one << 21) >> 11) | (two & 0x3FF)]
        values = [v.astype(F32) for v in values] + found[words:]
        return tuple(a + weight * v for a, v in zip(acc, values))

    sums = (jnp.zeros((SUBS, LANES), F32),) * len(fields)
    for f in range(faces):
        sums = face(f, sums)
    return [
        s + (a if i >= 3 * triples else unit[r] * a) for i, (r, s, a) in enumerate(zip(fields, start, sums))
    ]


def share_of(place_ref, index_ref):
    count = index_ref.shape[0] // HARM_DEVICES
    begin = place_ref[0] // 2 * count
    return begin, count, begin // FACES


def gather_fields(row, fields, count, words_ref, first, index_ref, weight_ref, unit, start, out_ref, lead=0):
    for g in range(index_ref.shape[0] // FACES):
        at = slice(g * SUBS, (g + 1) * SUBS)
        values = gather_into(
            row, fields, count, words_ref, first, index_ref, weight_ref, g * FACES, FACES, unit,
            [start(r - lead, at) for r in fields],
        )
        for r, value in zip(fields, values):
            out_ref[r - lead, at, :] = value


def half_rows(half):
    return pl.ds(pl.multiple_of(half * SUBS, SUBS), SUBS)


def zero_start(*_):
    return jnp.zeros((SUBS, LANES), F32)


def prepare_kernel(
    place_ref, order_ref, mean_ref, harm_ref, links_ref, weight_in, flow_ref, jac_ref, source_ref, step_ref,
    mean_base, harm_base, index_ref, weight_ref, wsum_ref, mean_out, state_ref, jac_out, flow_out, source_out,
    full_ref, mean_acc, words_ref, mean_words, *, coeff,
):
    groups = mean_ref.shape[1] // LANES
    flips = place_ref[0] % 2 == 0
    rim = groups * LANES
    lane = lambda t: slice(t * LANES, (t + 1) * LANES)
    for g in range(groups // SUBS):
        total = None
        for f in range(FACES):
            link = packed(lambda t: links_ref[f : f + 1, lane(t)], g * SUBS)
            flipped = jnp.where(link >= rim, link ^ (rim // 2), link)
            index_ref[g * FACES + f] = jnp.where(flips, flipped, link)
            weight = packed(lambda t: weight_in[f : f + 1, lane(t)], g * SUBS)
            weight_ref[g * FACES + f] = weight
            total = weight if total is None else total + weight
        wsum_ref[g * SUBS : (g + 1) * SUBS, :] = total
    row = native_row(mean_ref, harm_ref)
    flow = native_row(mean_ref, flow_ref)
    for g in range(0, groups, SUBS):
        at = slice(g, g + SUBS)
        for r in range(VARS):
            mean_out[r, at, :] = packed(lambda t: row(r, t), g)
        for r in range(2 * VARS):
            state_ref[r, at, :] = packed(lambda t: row(VARS + r, t), g)
    for g in range(0, groups, SUBS):
        at = slice(g, g + SUBS)
        for r in range(2 * VARS):
            flow_out[r, at, :] = packed(lambda t: flow(VARS + r, t), g)
        for v in range(VARS):
            source_out[v, at, :] = packed(lambda t: source_ref[v : v + 1, lane(t)], g)
        for j in range(VARS):
            for i in range(VARS):
                jac_out[j * VARS + i, at, :] = packed(lambda t: jac_ref[j, i : i + 1, lane(t)], g)
    row = fields_row(mean_out, state_ref)
    load = fields_block(mean_out, state_ref)
    unit = pack_table(load, groups // SUBS, HARM_FIELDS, words_ref)
    mean_unit = pack_table(load, groups // SUBS, MEAN_FIELDS, mean_words)
    gather_fields(
        row, HARM_FIELDS, groups, words_ref, 0, index_ref, weight_ref, unit, zero_start, full_ref, VARS
    )
    begin, count, half = share_of(place_ref, index_ref)
    values = gather_into(
        row, MEAN_FIELDS, groups, mean_words, 0, index_ref, weight_ref, begin, count, mean_unit,
        [zero_start()] * VARS,
    )
    mean_acc[...] = jnp.zeros(mean_acc.shape, F32)
    for r, value in enumerate(values):
        mean_acc[r, half_rows(half), :] = value
    lead = place_ref[0] // 2 == 0
    for g in range(groups // SUBS):
        at = slice(g * SUBS, (g + 1) * SUBS)
        mean = [mean_out[v, at, :] for v in range(VARS)]
        state = [state_ref[r, at, :] for r in range(2 * VARS)]
        wsum = wsum_ref[at, :]
        scale = coeff * step_ref[at, :]
        flux = []
        for v in range(VARS):
            stress = state[v] * flow_out[v, at, :] + state[VARS + v] * flow_out[VARS + v, at, :]
            flux.append(jnp.where(lead, wsum * mean[v], 0.0) - mean_acc[v, at, :] - stress)
        for v, res in enumerate(transposed(jac_out, at, flux)):
            own = jnp.where(lead, mean[v] + scale * source_out[v, at, :], 0.0)
            mean_base[v, at, :] = own - scale * res
        gathered = [full_ref[r, at, :] for r in range(2 * VARS)]
        harm_step(order_ref, at, mean, state, state, gathered, wsum, scale, jac_out, flow_out, harm_base)


def fields_row(mean_ref, harm_ref):
    def row(r, h):
        return mean_ref[r, h : h + 1, :] if r < VARS else harm_ref[r - VARS, h : h + 1, :]

    return row


def fields_block(mean_ref, harm_ref):
    def load(r, g):
        at = slice(g * SUBS, (g + 1) * SUBS)
        return mean_ref[r, at, :] if r < VARS else harm_ref[r - VARS, at, :]

    return load


def rim_row(*rims):
    rows = rims[0].shape[1]
    return lambda r, h: rims[h // rows][r, h % rows : h % rows + 1, :]


def rim_block(*rims):
    blocks = rims[0].shape[1] // SUBS
    return lambda r, g: rims[g // blocks][r, g % blocks * SUBS : (g % blocks + 1) * SUBS, :]


def near_kernel(rim, index_ref, weight_ref, out_ref, words_ref):
    rows = rim.shape[1]
    first = (out_ref.shape[1] + rows) * LANES
    unit = pack_table(rim_block(rim), rows // SUBS, ALL_FIELDS, words_ref)
    gather_fields(
        rim_row(rim), ALL_FIELDS, rows, words_ref, first, index_ref, weight_ref, unit, zero_start, out_ref
    )


def transposed(jac_ref, at, flux):
    out = []
    for i in range(VARS):
        res = jac_ref[i, at, :] * flux[0]
        for j in range(1, VARS):
            res = res + jac_ref[j * VARS + i, at, :] * flux[j]
        out.append(res)
    return out


def harm_step(order_ref, at, mean, state, start, gathered, wsum, scale, jac_ref, flow_ref, out_ref):
    omega = BASE_FREQ * (order_ref[0].astype(F32) + 1.0)
    flux = [wsum * s - x for s, x in zip(state, gathered)]
    for part in range(2):
        res = transposed(jac_ref, at, flux[part * VARS : (part + 1) * VARS])
        for i in range(VARS):
            r = part * VARS + i
            turned = omega * state[(1 - part) * VARS + i]
            full = res[i] + turned if part == 0 else res[i] - turned
            full = full - mean[i] * flow_ref[r, at, :]
            out_ref[r, at, :] = start[r] - scale * full


def middle_kernel(
    place_ref, rim_a, rim_b, index_ref, weight_ref, mean_base, harm_base, jac_ref, flow_ref, step_ref,
    out_ref, part_ref, words_ref, mean_words, *, coeff,
):
    groups = mean_base.shape[1]
    rows = 2 * rim_a.shape[1]
    row, load = rim_row(rim_a, rim_b), rim_block(rim_a, rim_b)
    unit = pack_table(load, rows // SUBS, HARM_FIELDS, words_ref)
    mean_unit = pack_table(load, rows // SUBS, MEAN_FIELDS, mean_words)
    begin, count, half = share_of(place_ref, index_ref)
    values = gather_into(
        row, MEAN_FIELDS, rows, mean_words, groups * LANES, index_ref, weight_ref, begin, count, mean_unit,
        [zero_start()] * VARS,
    )
    for v in range(VARS):
        part_ref[v] = mean_base[v]
    at = half_rows(half)
    scale = coeff * step_ref[at, :]
    for v, res in enumerate(transposed(jac_ref, at, values)):
        part_ref[v, at, :] = mean_base[v, at, :] + scale * res
    for g in range(groups // SUBS):
        at = slice(g * SUBS, (g + 1) * SUBS)
        values = gather_into(
            row, HARM_FIELDS, rows, words_ref, groups * LANES, index_ref, weight_ref, g * FACES, FACES, unit,
            [zero_start()] * (2 * VARS),
        )
        scale = coeff * step_ref[at, :]
        new = []
        for first in range(0, 2 * VARS, VARS):
            for v, res in enumerate(transposed(jac_ref, at, values[first : first + VARS])):
                new.append(harm_base[first + v, at, :] + scale * res)
        for r, value in enumerate(new):
            out_ref[r, at, :] = value
        for v in range(VARS):
            part_ref[VARS + v, at, :] = new[v] * flow_ref[v, at, :] + new[VARS + v] * flow_ref[VARS + v, at, :]


def join_kernel(parts_ref, state_ref, tile_idx, mean_ref, stress_ref, pay_a, pay_b):
    for v in range(VARS):
        for ref, r in ((mean_ref, v), (stress_ref, VARS + v)):
            total = parts_ref[0, r]
            for k in range(1, HARM_DEVICES):
                total = total + parts_ref[k, r]
            ref[v] = total
    row = fields_row(mean_ref, state_ref)
    store_tiles(row, (tile_idx[0], tile_idx[1]), pay_a, pay_b, mean_ref.shape[1])


def own_kernel(
    order_ref, index_ref, weight_ref, wsum_ref, mean_ref, state_ref, mean_start, harm_start,
    jac_ref, flow_ref, source_ref, step_ref, stress_ref, mean_base, harm_base, full_ref, words_ref, *, coeff,
):
    groups = mean_ref.shape[1]
    unit = pack_table(fields_block(mean_ref, state_ref), groups // SUBS, ALL_FIELDS, words_ref)
    gather_fields(
        fields_row(mean_ref, state_ref), ALL_FIELDS, groups, words_ref, 0, index_ref, weight_ref, unit,
        zero_start, full_ref,
    )
    for g in range(groups // SUBS):
        at = slice(g * SUBS, (g + 1) * SUBS)
        mean = [mean_ref[v, at, :] for v in range(VARS)]
        state = [state_ref[r, at, :] for r in range(2 * VARS)]
        wsum = wsum_ref[at, :]
        scale = coeff * step_ref[at, :]
        flux = [wsum * m - full_ref[v, at, :] - stress_ref[v, at, :] for v, m in enumerate(mean)]
        for v, res in enumerate(transposed(jac_ref, at, flux)):
            mean_base[v, at, :] = mean_start[v, at, :] - scale * (res - source_ref[v, at, :])
        gathered = [full_ref[VARS + r, at, :] for r in range(2 * VARS)]
        start = [harm_start[r, at, :] for r in range(2 * VARS)]
        harm_step(order_ref, at, mean, state, start, gathered, wsum, scale, jac_ref, flow_ref, harm_base)


def close_kernel(
    rim, index_ref, weight_ref, jac_ref, step_ref, mean_base, harm_base, near_ref,
    mean_hbm, harm_hbm, full_ref, words_ref, mean_out, harm_out, sems, *, coeff,
):
    groups = mean_base.shape[1]
    rows = rim.shape[1]
    unit = pack_table(rim_block(rim), rows // SUBS, ALL_FIELDS, words_ref)
    base = fields_block(mean_base, harm_base)
    copies = []
    for g in range(groups // SUBS):
        at = slice(g * SUBS, (g + 1) * SUBS)
        full = gather_into(
            rim_row(rim), ALL_FIELDS, rows, words_ref, groups * LANES, index_ref, weight_ref, g * FACES, FACES,
            unit, [near_ref[r, at, :] for r in ALL_FIELDS],
        )
        scale = coeff * step_ref[at, :]
        for first in range(0, ROWS, VARS):
            for v, res in enumerate(transposed(jac_ref, at, full[first : first + VARS])):
                full_ref[first + v, at, :] = base(first + v, g) + scale * res
        for t in range(g * SUBS, (g + 1) * SUBS):
            lanes = slice(t * LANES, (t + 1) * LANES)
            mean_out[:, lanes] = stacked(lambda i: full_ref[i, t : t + 1, :], VARS)
            for v in range(VARS):
                harm_out[v, :, lanes] = stacked(lambda i: full_ref[(i + 1) * VARS + v, t : t + 1, :], 2)
        part = pl.ds(g * SUBS * LANES, SUBS * LANES)
        for i, (out, hbm) in enumerate(
            ((mean_out.at[:, part], mean_hbm.at[:, part]), (harm_out.at[:, :, part], harm_hbm.at[:, :, part]))
        ):
            copies.append(pltpu.make_async_copy(out, hbm, sems.at[2 * g + i]))
            copies[-1].start()
    for copy in copies:
        copy.wait()


def stacked(row, count):
    sub = lax.broadcasted_iota(jnp.int32, (count, LANES), 0)
    out = jnp.broadcast_to(row(0), (count, LANES))
    for i in range(1, count):
        out = jnp.where(sub == i, jnp.broadcast_to(row(i), (count, LANES)), out)
    return out


def held(*arrays):
    return [*(pltpu.VMEM(a.shape, a.dtype) for a in arrays), pltpu.SemaphoreType.DMA((SUBS,))]


def launch(body, out_shape, scalars, args, raw=(), scratch=()):
    smem = pl.BlockSpec(memory_space=pltpu.SMEM)
    vmem = pl.BlockSpec(memory_space=pltpu.VMEM)
    anywhere = pl.BlockSpec(memory_space=pl.ANY)
    return pl.pallas_call(
        body,
        out_shape=out_shape,
        in_specs=[smem] * len(scalars) + [anywhere] * len(raw) + [vmem] * len(args),
        out_specs=[anywhere if isinstance(s, jax.ShapeDtypeStruct) else vmem for s in out_shape],
        scratch_shapes=scratch,
    )(*scalars, *raw, *(pltpu.with_memory_space_constraint(a, pltpu.VMEM) for a in args))


def exchange(pay_a, pay_b):
    count = lax.axis_size("cells")
    near = [(b, b ^ 1) for b in range(count)]
    far = [(b, (b - 1 + 2 * (b % 2)) % count) for b in range(count)]
    rim_a = lax.ppermute(pay_a, "cells", far)
    rim_b = lax.ppermute(pay_b, "cells", near)
    return rim_a, rim_b


def shards(
    mean_adjoint,
    harm_adjoint,
    harm_flow,
    flux_jacobian,
    face_weight,
    face_links,
    face_tiles,
    pseudo_step,
    mean_source,
    harm_order,
):
    cells = mean_adjoint.shape[1]
    groups = cells // LANES
    halves = groups // SUBS
    rim_rows = face_tiles.shape[1] // LANES
    harm_adjoint, harm_flow = (
        a[0].swapaxes(0, 1) for a in (harm_adjoint, harm_flow)
    )
    place = (1 - lax.axis_index("cells") % 2 + 2 * lax.axis_index(HARM)).astype(jnp.int32)[None]
    step = pseudo_step.reshape(groups, LANES)
    mean_fields, harm_fields = struct(VARS, groups, LANES), struct(2 * VARS, groups, LANES)
    pays = (struct(ROWS, rim_rows, LANES), struct(ROWS, rim_rows, LANES))
    raw = (
        mean_adjoint, harm_adjoint, face_links, face_weight, harm_flow, flux_jacobian, mean_source, step
    )
    held_raw = tuple(struct(*a.shape, dtype=a.dtype) for a in raw)
    pay_a, pay_b, tile_idx, *inside, step = launch(
        open_kernel, pays + (struct(2, rim_rows, LANES, dtype=jnp.int32),) + held_raw, (place,), (),
        (face_tiles, *raw), [pltpu.VMEM(face_tiles.shape, jnp.int32), pltpu.SemaphoreType.DMA((9,))],
    )
    rim_a, rim_b = exchange(pay_a, pay_b)
    registers = FACES * halves
    words = lambda fields: struct(max(len(fields) // 3 * 2, 1), groups, LANES, dtype=jnp.int32)
    harm_words, mean_words = words(HARM_FIELDS), words(MEAN_FIELDS)
    mean_base, harm_base, index, weight, wsum, mean_start, harm_start, jac, flow, source = launch(
        lambda *refs: prepare_kernel(*refs, coeff=1.0 / SECTIONS),
        (
            mean_fields,
            harm_fields,
            struct(registers, SUBS, LANES, dtype=jnp.int32),
            struct(registers, SUBS, LANES),
            struct(groups, LANES),
            mean_fields,
            harm_fields,
            struct(VARS * VARS, groups, LANES),
            harm_fields,
            mean_fields,
        ),
        (place, harm_order), (*inside, step),
        scratch=[harm_fields, mean_fields, harm_words, mean_words],
    )
    state, part = launch(
        lambda *refs: middle_kernel(*refs, coeff=1.0 / SECTIONS), (harm_fields, harm_fields), (place,),
        (rim_a, rim_b, index, weight, mean_base, harm_base, jac, flow, step),
        scratch=[harm_words, mean_words],
    )
    parts = lax.all_gather(part, HARM)
    mean, stress, pay_a, pay_b = launch(join_kernel, (mean_fields, mean_fields) + pays, (), (parts, state, tile_idx))
    rim_a, rim_b = exchange(pay_a, pay_b)
    fields = struct(ROWS, groups, LANES)
    mean_base, harm_base = launch(
        lambda *refs: own_kernel(*refs, coeff=1.0), (mean_fields, harm_fields), (harm_order,),
        (index, weight, wsum, mean, state, mean_start, harm_start, jac, flow, source, step, stress),
        scratch=[fields, words(ALL_FIELDS)],
    )
    (near,) = launch(near_kernel, (fields,), (), (rim_b, index, weight), scratch=[words(ALL_FIELDS)])
    outs = [jax.ShapeDtypeStruct(s, F32) for s in ((VARS, cells), (VARS, 2, cells))]
    mean_new, harm_new = launch(
        lambda *refs: close_kernel(*refs, coeff=1.0), tuple(outs), (),
        (rim_a, index, weight, jac, step, mean_base, harm_base, near),
        scratch=[fields, words(ALL_FIELDS), *held(*outs)],
    )
    return mean_new, harm_new.swapaxes(0, 1)[None]


def solution(mesh):
    finer = Mesh(mesh.devices.reshape(mesh.shape["cells"], 2, 2), ("cells", *HARM))
    return jax.shard_map(
        shards,
        mesh=finer,
        in_specs=(
            P(None, "cells"),
            P(HARM, None, None, "cells"),
            P(HARM, None, None, "cells"),
            P(None, None, "cells"),
            P(None, "cells"),
            P(None, "cells"),
            P(None, "cells"),
            P("cells"),
            P(None, "cells"),
            P(HARM),
        ),
        out_specs=(P(None, "cells"), P(HARM, None, None, "cells")),
        check_vma=False,
    )
```

```python
import jax
import jax.numpy as jnp
from jax import lax
from jax.experimental import pallas as pl
from jax.experimental.pallas import tpu as pltpu
from jax.sharding import Mesh
from jax.sharding import PartitionSpec as P

VARS = 5
FACES = 6
SECTIONS = 2
ROWS = 3 * VARS
MEAN_FIELDS = range(VARS)
HARM_FIELDS = range(VARS, ROWS)
ALL_FIELDS = range(ROWS)
HARM = ("harm_0", "harm_1")
HARM_DEVICES = 4
LANES = 128
SUBS = 8
BASE_FREQ = 0.8
F32 = jnp.float32


def struct(*shape, dtype=F32):
    return pltpu.VMEM(shape, dtype)


def spread(row):
    return jnp.broadcast_to(row, (SUBS, LANES))


def packed(tile, first):
    sub = lax.broadcasted_iota(jnp.int32, (SUBS, LANES), 0)
    out = spread(tile(first))
    for i in range(1, SUBS):
        out = jnp.where(sub == i, spread(tile(first + i)), out)
    return out


def picked(row, fields, count, index):
    low = index & (LANES - 1)
    high = index >> 7
    out = [None] * len(fields)
    for h in range(count):
        hit = high == h
        for i, r in enumerate(fields):
            value = jnp.take_along_axis(spread(row(r, h)), low, axis=1)
            out[i] = jnp.where(hit, value, jnp.zeros_like(value) if h == 0 else out[i])
    return out


def store_tiles(row, tile_index, pay_a, pay_b, rows):
    for pay, index in zip((pay_a, pay_b), tile_index):
        for r, value in enumerate(picked(row, range(ROWS), rows, index)):
            pay[r] = value


def native_row(mean_ref, harm_ref):
    def row(r, h):
        lanes = slice(h * LANES, (h + 1) * LANES)
        if r < VARS:
            return mean_ref[r : r + 1, lanes]
        part, var = divmod(r - VARS, VARS)
        return harm_ref[var, part : part + 1, lanes]

    return row


def fetch(sources, targets, sems):
    copies = [pltpu.make_async_copy(s, t, sems.at[i]) for i, (s, t) in enumerate(zip(sources, targets))]
    for copy in copies:
        copy.start()
    return [copy.wait for copy in copies]


def open_kernel(
    place_ref, tiles_hbm, mean_hbm, harm_hbm, links_hbm, weight_hbm, flow_hbm, jac_hbm, source_hbm, step_hbm,
    pay_a, pay_b, tile_idx, mean_ref, harm_ref, links_ref, weight_ref, flow_ref, jac_ref, source_ref, step_ref,
    tiles_ref, sems,
):
    waits = fetch(
        (tiles_hbm, mean_hbm, harm_hbm, links_hbm, weight_hbm, flow_hbm, jac_hbm, source_hbm, step_hbm),
        (tiles_ref, mean_ref, harm_ref, links_ref, weight_ref, flow_ref, jac_ref, source_ref, step_ref),
        sems,
    )
    for wait in waits[:3]:
        wait()
    lowers_first = place_ref[0] % 2 == 1
    lower, upper = (
        packed(lambda t, k=k: tiles_ref[k : k + 1, t * LANES : (t + 1) * LANES], 0) for k in range(2)
    )
    first = jnp.where(lowers_first, lower, upper)
    second = jnp.where(lowers_first, upper, lower)
    tile_idx[0] = first
    tile_idx[1] = second
    row = native_row(mean_ref, harm_ref)
    store_tiles(row, (first, second), pay_a, pay_b, mean_ref.shape[1] // LANES)
    for wait in waits[3:]:
        wait()


TOP = float(2**20 - 1)


def largest(values):
    top = jnp.abs(values[0])
    for value in values[1:]:
        top = jnp.maximum(top, jnp.abs(value))
    top = jnp.max(jnp.max(top, axis=0, keepdims=True), axis=1, keepdims=True)
    return jnp.maximum(jnp.broadcast_to(top, (SUBS, LANES)), 1e-30)


def pack_table(load, blocks, fields, words_ref):
    unit = {}
    scale = {}
    for kind in ([r for r in fields if r < VARS], [r for r in fields if r >= VARS]):
        if kind:
            top = largest([load(r, g) for r in kind for g in range(blocks)])
            for r in kind:
                unit[r] = top * (1.0 / TOP)
                scale[r] = TOP / top
    fixed = lambda r, g: jnp.floor(load(r, g) * scale[r] + 0.5).astype(jnp.int32)
    for i in range(len(fields) // 3):
        for g in range(blocks):
            at = slice(g * SUBS, (g + 1) * SUBS)
            first, second, third = (fixed(r, g) for r in fields[3 * i : 3 * i + 3])
            words_ref[2 * i, at, :] = (first << 11) | ((third >> 10) & 0x7FF)
            words_ref[2 * i + 1, at, :] = (second << 11) | (third & 0x3FF)
    return unit


def gather_into(row, fields, count, words_ref, first, index_ref, weight_ref, begin, faces, unit, start):
    triples = len(fields) // 3
    words = 2 * triples
    rest = fields[3 * triples :]

    def word(w, h):
        return words_ref[w, h : h + 1, :] if w < words else row(rest[w - words], h)

    def face(f, acc):
        found = picked(word, range(words + len(rest)), count, index_ref[begin + f] - first)
        weight = weight_ref[begin + f]
        values = []
        for i in range(triples):
            one, two = found[2 * i], found[2 * i + 1]
            values += [one >> 11, two >> 11, ((one << 21) >> 11) | (two & 0x3FF)]
        values = [v.astype(F32) for v in values] + found[words:]
        return tuple(a + weight * v for a, v in zip(acc, values))

    sums = (jnp.zeros((SUBS, LANES), F32),) * len(fields)
    for f in range(faces):
        sums = face(f, sums)
    return [
        s + (a if i >= 3 * triples else unit[r] * a) for i, (r, s, a) in enumerate(zip(fields, start, sums))
    ]


def share_of(place_ref, index_ref):
    count = index_ref.shape[0] // HARM_DEVICES
    begin = place_ref[0] // 2 * count
    return begin, count, begin // FACES


def gather_fields(row, fields, count, words_ref, first, index_ref, weight_ref, unit, start, out_ref, lead=0):
    for g in range(index_ref.shape[0] // FACES):
        at = slice(g * SUBS, (g + 1) * SUBS)
        values = gather_into(
            row, fields, count, words_ref, first, index_ref, weight_ref, g * FACES, FACES, unit,
            [start(r - lead, at) for r in fields],
        )
        for r, value in zip(fields, values):
            out_ref[r - lead, at, :] = value


def half_rows(half):
    return pl.ds(pl.multiple_of(half * SUBS, SUBS), SUBS)


def zero_start(*_):
    return jnp.zeros((SUBS, LANES), F32)


def prepare_kernel(
    place_ref, order_ref, mean_ref, harm_ref, links_ref, weight_in, flow_ref, jac_ref, source_ref, step_ref,
    mean_base, harm_base, index_ref, weight_ref, wsum_ref, mean_out, state_ref, jac_out, flow_out, source_out,
    full_ref, mean_acc, words_ref, mean_words, *, coeff,
):
    groups = mean_ref.shape[1] // LANES
    flips = place_ref[0] % 2 == 0
    rim = groups * LANES
    lane = lambda t: slice(t * LANES, (t + 1) * LANES)
    for g in range(groups // SUBS):
        total = None
        for f in range(FACES):
            link = packed(lambda t: links_ref[f : f + 1, lane(t)], g * SUBS)
            flipped = jnp.where(link >= rim, link ^ (rim // 2), link)
            index_ref[g * FACES + f] = jnp.where(flips, flipped, link)
            weight = packed(lambda t: weight_in[f : f + 1, lane(t)], g * SUBS)
            weight_ref[g * FACES + f] = weight
            total = weight if total is None else total + weight
        wsum_ref[g * SUBS : (g + 1) * SUBS, :] = total
    row = native_row(mean_ref, harm_ref)
    flow = native_row(mean_ref, flow_ref)
    for g in range(0, groups, SUBS):
        at = slice(g, g + SUBS)
        for r in range(VARS):
            mean_out[r, at, :] = packed(lambda t: row(r, t), g)
        for r in range(2 * VARS):
            state_ref[r, at, :] = packed(lambda t: row(VARS + r, t), g)
    for g in range(0, groups, SUBS):
        at = slice(g, g + SUBS)
        for r in range(2 * VARS):
            flow_out[r, at, :] = packed(lambda t: flow(VARS + r, t), g)
        for v in range(VARS):
            source_out[v, at, :] = packed(lambda t: source_ref[v : v + 1, lane(t)], g)
        for j in range(VARS):
            for i in range(VARS):
                jac_out[j * VARS + i, at, :] = packed(lambda t: jac_ref[j, i : i + 1, lane(t)], g)
    row = fields_row(mean_out, state_ref)
    load = fields_block(mean_out, state_ref)
    unit = pack_table(load, groups // SUBS, HARM_FIELDS, words_ref)
    mean_unit = pack_table(load, groups // SUBS, MEAN_FIELDS, mean_words)
    gather_fields(
        row, HARM_FIELDS, groups, words_ref, 0, index_ref, weight_ref, unit, zero_start, full_ref, VARS
    )
    begin, count, half = share_of(place_ref, index_ref)
    values = gather_into(
        row, MEAN_FIELDS, groups, mean_words, 0, index_ref, weight_ref, begin, count, mean_unit,
        [zero_start()] * VARS,
    )
    mean_acc[...] = jnp.zeros(mean_acc.shape, F32)
    for r, value in enumerate(values):
        mean_acc[r, half_rows(half), :] = value
    lead = place_ref[0] // 2 == 0
    for g in range(groups // SUBS):
        at = slice(g * SUBS, (g + 1) * SUBS)
        mean = [mean_out[v, at, :] for v in range(VARS)]
        state = [state_ref[r, at, :] for r in range(2 * VARS)]
        wsum = wsum_ref[at, :]
        scale = coeff * step_ref[at, :]
        flux = []
        for v in range(VARS):
            stress = state[v] * flow_out[v, at, :] + state[VARS + v] * flow_out[VARS + v, at, :]
            flux.append(jnp.where(lead, wsum * mean[v], 0.0) - mean_acc[v, at, :] - stress)
        for v, res in enumerate(transposed(jac_out, at, flux)):
            own = jnp.where(lead, mean[v] + scale * source_out[v, at, :], 0.0)
            mean_base[v, at, :] = own - scale * res
        gathered = [full_ref[r, at, :] for r in range(2 * VARS)]
        harm_step(order_ref, at, mean, state, state, gathered, wsum, scale, jac_out, flow_out, harm_base)


def fields_row(mean_ref, harm_ref):
    def row(r, h):
        return mean_ref[r, h : h + 1, :] if r < VARS else harm_ref[r - VARS, h : h + 1, :]

    return row


def fields_block(mean_ref, harm_ref):
    def load(r, g):
        at = slice(g * SUBS, (g + 1) * SUBS)
        return mean_ref[r, at, :] if r < VARS else harm_ref[r - VARS, at, :]

    return load


def rim_row(*rims):
    rows = rims[0].shape[1]
    return lambda r, h: rims[h // rows][r, h % rows : h % rows + 1, :]


def rim_block(*rims):
    blocks = rims[0].shape[1] // SUBS
    return lambda r, g: rims[g // blocks][r, g % blocks * SUBS : (g % blocks + 1) * SUBS, :]


def near_kernel(rim, index_ref, weight_ref, out_ref, words_ref):
    rows = rim.shape[1]
    first = (out_ref.shape[1] + rows) * LANES
    unit = pack_table(rim_block(rim), rows // SUBS, ALL_FIELDS, words_ref)
    gather_fields(
        rim_row(rim), ALL_FIELDS, rows, words_ref, first, index_ref, weight_ref, unit, zero_start, out_ref
    )


def transposed(jac_ref, at, flux):
    out = []
    for i in range(VARS):
        res = jac_ref[i, at, :] * flux[0]
        for j in range(1, VARS):
            res = res + jac_ref[j * VARS + i, at, :] * flux[j]
        out.append(res)
    return out


def harm_step(order_ref, at, mean, state, start, gathered, wsum, scale, jac_ref, flow_ref, out_ref):
    omega = BASE_FREQ * (order_ref[0].astype(F32) + 1.0)
    flux = [wsum * s - x for s, x in zip(state, gathered)]
    for part in range(2):
        res = transposed(jac_ref, at, flux[part * VARS : (part + 1) * VARS])
        for i in range(VARS):
            r = part * VARS + i
            turned = omega * state[(1 - part) * VARS + i]
            full = res[i] + turned if part == 0 else res[i] - turned
            full = full - mean[i] * flow_ref[r, at, :]
            out_ref[r, at, :] = start[r] - scale * full


def far_kernel(place_ref, rim, index_ref, weight_ref, full_ref, share_ref, words_ref, mean_words):
    rows = rim.shape[1]
    first = full_ref.shape[1] * LANES
    row, load = rim_row(rim), rim_block(rim)
    unit = pack_table(load, rows // SUBS, HARM_FIELDS, words_ref)
    mean_unit = pack_table(load, rows // SUBS, MEAN_FIELDS, mean_words)
    gather_fields(row, HARM_FIELDS, rows, words_ref, first, index_ref, weight_ref, unit, zero_start, full_ref, VARS)
    begin, count, _ = share_of(place_ref, index_ref)
    values = gather_into(
        row, MEAN_FIELDS, rows, mean_words, first, index_ref, weight_ref, begin, count, mean_unit,
        [zero_start()] * VARS,
    )
    for r, value in enumerate(values):
        share_ref[r] = value


def middle_kernel(
    place_ref, rim, full_ref, share_ref, index_ref, weight_ref, mean_base, harm_base, jac_ref, flow_ref, step_ref,
    out_ref, part_ref, words_ref, mean_words, *, coeff,
):
    groups = mean_base.shape[1]
    rows = rim.shape[1]
    near = (groups + rows) * LANES
    row, load = rim_row(rim), rim_block(rim)
    unit = pack_table(load, rows // SUBS, HARM_FIELDS, words_ref)
    mean_unit = pack_table(load, rows // SUBS, MEAN_FIELDS, mean_words)
    begin, count, half = share_of(place_ref, index_ref)
    values = gather_into(
        row, MEAN_FIELDS, rows, mean_words, near, index_ref, weight_ref, begin, count, mean_unit,
        [share_ref[r] for r in range(VARS)],
    )
    for v in range(VARS):
        part_ref[v] = mean_base[v]
    at = half_rows(half)
    scale = coeff * step_ref[at, :]
    for v, res in enumerate(transposed(jac_ref, at, values)):
        part_ref[v, at, :] = mean_base[v, at, :] + scale * res
    for g in range(groups // SUBS):
        at = slice(g * SUBS, (g + 1) * SUBS)
        values = gather_into(
            row, HARM_FIELDS, rows, words_ref, near, index_ref, weight_ref, g * FACES, FACES, unit,
            [full_ref[r, at, :] for r in range(2 * VARS)],
        )
        scale = coeff * step_ref[at, :]
        new = []
        for first in range(0, 2 * VARS, VARS):
            for v, res in enumerate(transposed(jac_ref, at, values[first : first + VARS])):
                new.append(harm_base[first + v, at, :] + scale * res)
        for r, value in enumerate(new):
            out_ref[r, at, :] = value
        for v in range(VARS):
            part_ref[VARS + v, at, :] = new[v] * flow_ref[v, at, :] + new[VARS + v] * flow_ref[VARS + v, at, :]


def join_kernel(parts_ref, state_ref, tile_idx, mean_ref, stress_ref, pay_a, pay_b):
    for v in range(VARS):
        for ref, r in ((mean_ref, v), (stress_ref, VARS + v)):
            total = parts_ref[0, r]
            for k in range(1, HARM_DEVICES):
                total = total + parts_ref[k, r]
            ref[v] = total
    row = fields_row(mean_ref, state_ref)
    store_tiles(row, (tile_idx[0], tile_idx[1]), pay_a, pay_b, mean_ref.shape[1])


def own_kernel(
    order_ref, index_ref, weight_ref, wsum_ref, mean_ref, state_ref, mean_start, harm_start,
    jac_ref, flow_ref, source_ref, step_ref, stress_ref, mean_base, harm_base, full_ref, words_ref, *, coeff,
):
    groups = mean_ref.shape[1]
    unit = pack_table(fields_block(mean_ref, state_ref), groups // SUBS, ALL_FIELDS, words_ref)
    gather_fields(
        fields_row(mean_ref, state_ref), ALL_FIELDS, groups, words_ref, 0, index_ref, weight_ref, unit,
        zero_start, full_ref,
    )
    for g in range(groups // SUBS):
        at = slice(g * SUBS, (g + 1) * SUBS)
        mean = [mean_ref[v, at, :] for v in range(VARS)]
        state = [state_ref[r, at, :] for r in range(2 * VARS)]
        wsum = wsum_ref[at, :]
        scale = coeff * step_ref[at, :]
        flux = [wsum * m - full_ref[v, at, :] - stress_ref[v, at, :] for v, m in enumerate(mean)]
        for v, res in enumerate(transposed(jac_ref, at, flux)):
            mean_base[v, at, :] = mean_start[v, at, :] - scale * (res - source_ref[v, at, :])
        gathered = [full_ref[VARS + r, at, :] for r in range(2 * VARS)]
        start = [harm_start[r, at, :] for r in range(2 * VARS)]
        harm_step(order_ref, at, mean, state, start, gathered, wsum, scale, jac_ref, flow_ref, harm_base)


def close_kernel(
    rim, index_ref, weight_ref, jac_ref, step_ref, mean_base, harm_base, near_ref,
    mean_hbm, harm_hbm, full_ref, words_ref, mean_out, harm_out, sems, *, coeff,
):
    groups = mean_base.shape[1]
    rows = rim.shape[1]
    unit = pack_table(rim_block(rim), rows // SUBS, ALL_FIELDS, words_ref)
    base = fields_block(mean_base, harm_base)
    copies = []
    for g in range(groups // SUBS):
        at = slice(g * SUBS, (g + 1) * SUBS)
        full = gather_into(
            rim_row(rim), ALL_FIELDS, rows, words_ref, groups * LANES, index_ref, weight_ref, g * FACES, FACES,
            unit, [near_ref[r, at, :] for r in ALL_FIELDS],
        )
        scale = coeff * step_ref[at, :]
        for first in range(0, ROWS, VARS):
            for v, res in enumerate(transposed(jac_ref, at, full[first : first + VARS])):
                full_ref[first + v, at, :] = base(first + v, g) + scale * res
        for t in range(g * SUBS, (g + 1) * SUBS):
            lanes = slice(t * LANES, (t + 1) * LANES)
            mean_out[:, lanes] = stacked(lambda i: full_ref[i, t : t + 1, :], VARS)
            for v in range(VARS):
                harm_out[v, :, lanes] = stacked(lambda i: full_ref[(i + 1) * VARS + v, t : t + 1, :], 2)
        part = pl.ds(g * SUBS * LANES, SUBS * LANES)
        for i, (out, hbm) in enumerate(
            ((mean_out.at[:, part], mean_hbm.at[:, part]), (harm_out.at[:, :, part], harm_hbm.at[:, :, part]))
        ):
            copies.append(pltpu.make_async_copy(out, hbm, sems.at[2 * g + i]))
            copies[-1].start()
    for copy in copies:
        copy.wait()


def stacked(row, count):
    sub = lax.broadcasted_iota(jnp.int32, (count, LANES), 0)
    out = jnp.broadcast_to(row(0), (count, LANES))
    for i in range(1, count):
        out = jnp.where(sub == i, jnp.broadcast_to(row(i), (count, LANES)), out)
    return out


def held(*arrays):
    return [*(pltpu.VMEM(a.shape, a.dtype) for a in arrays), pltpu.SemaphoreType.DMA((SUBS,))]


def launch(body, out_shape, scalars, args, raw=(), scratch=()):
    smem = pl.BlockSpec(memory_space=pltpu.SMEM)
    vmem = pl.BlockSpec(memory_space=pltpu.VMEM)
    anywhere = pl.BlockSpec(memory_space=pl.ANY)
    return pl.pallas_call(
        body,
        out_shape=out_shape,
        in_specs=[smem] * len(scalars) + [anywhere] * len(raw) + [vmem] * len(args),
        out_specs=[anywhere if isinstance(s, jax.ShapeDtypeStruct) else vmem for s in out_shape],
        scratch_shapes=scratch,
    )(*scalars, *raw, *(pltpu.with_memory_space_constraint(a, pltpu.VMEM) for a in args))


def exchange(pay_a, pay_b):
    count = lax.axis_size("cells")
    near = [(b, b ^ 1) for b in range(count)]
    far = [(b, (b - 1 + 2 * (b % 2)) % count) for b in range(count)]
    rim_a = lax.ppermute(pay_a, "cells", far)
    rim_b = lax.ppermute(pay_b, "cells", near)
    return rim_a, rim_b


def shards(
    mean_adjoint,
    harm_adjoint,
    harm_flow,
    flux_jacobian,
    face_weight,
    face_links,
    face_tiles,
    pseudo_step,
    mean_source,
    harm_order,
):
    cells = mean_adjoint.shape[1]
    groups = cells // LANES
    halves = groups // SUBS
    rim_rows = face_tiles.shape[1] // LANES
    harm_adjoint, harm_flow = (
        a[0].swapaxes(0, 1) for a in (harm_adjoint, harm_flow)
    )
    place = (1 - lax.axis_index("cells") % 2 + 2 * lax.axis_index(HARM)).astype(jnp.int32)[None]
    step = pseudo_step.reshape(groups, LANES)
    mean_fields, harm_fields = struct(VARS, groups, LANES), struct(2 * VARS, groups, LANES)
    pays = (struct(ROWS, rim_rows, LANES), struct(ROWS, rim_rows, LANES))
    raw = (
        mean_adjoint, harm_adjoint, face_links, face_weight, harm_flow, flux_jacobian, mean_source, step
    )
    held_raw = tuple(struct(*a.shape, dtype=a.dtype) for a in raw)
    pay_a, pay_b, tile_idx, *inside, step = launch(
        open_kernel, pays + (struct(2, rim_rows, LANES, dtype=jnp.int32),) + held_raw, (place,), (),
        (face_tiles, *raw), [pltpu.VMEM(face_tiles.shape, jnp.int32), pltpu.SemaphoreType.DMA((9,))],
    )
    rim_a, rim_b = exchange(pay_a, pay_b)
    registers = FACES * halves
    words = lambda fields: struct(max(len(fields) // 3 * 2, 1), groups, LANES, dtype=jnp.int32)
    harm_words, mean_words = words(HARM_FIELDS), words(MEAN_FIELDS)
    mean_base, harm_base, index, weight, wsum, mean_start, harm_start, jac, flow, source = launch(
        lambda *refs: prepare_kernel(*refs, coeff=1.0 / SECTIONS),
        (
            mean_fields,
            harm_fields,
            struct(registers, SUBS, LANES, dtype=jnp.int32),
            struct(registers, SUBS, LANES),
            struct(groups, LANES),
            mean_fields,
            harm_fields,
            struct(VARS * VARS, groups, LANES),
            harm_fields,
            mean_fields,
        ),
        (place, harm_order), (*inside, step),
        scratch=[harm_fields, mean_fields, harm_words, mean_words],
    )
    full, share = launch(
        far_kernel, (harm_fields, struct(VARS, SUBS, LANES)), (place,), (rim_a, index, weight),
        scratch=[harm_words, mean_words],
    )
    state, part = launch(
        lambda *refs: middle_kernel(*refs, coeff=1.0 / SECTIONS), (harm_fields, harm_fields), (place,),
        (rim_b, full, share, index, weight, mean_base, harm_base, jac, flow, step),
        scratch=[harm_words, mean_words],
    )
    parts = lax.all_gather(part, HARM)
    mean, stress, pay_a, pay_b = launch(join_kernel, (mean_fields, mean_fields) + pays, (), (parts, state, tile_idx))
    rim_a, rim_b = exchange(pay_a, pay_b)
    fields = struct(ROWS, groups, LANES)
    mean_base, harm_base = launch(
        lambda *refs: own_kernel(*refs, coeff=1.0), (mean_fields, harm_fields), (harm_order,),
        (index, weight, wsum, mean, state, mean_start, harm_start, jac, flow, source, step, stress),
        scratch=[fields, words(ALL_FIELDS)],
    )
    (near,) = launch(near_kernel, (fields,), (), (rim_b, index, weight), scratch=[words(ALL_FIELDS)])
    outs = [jax.ShapeDtypeStruct(s, F32) for s in ((VARS, cells), (VARS, 2, cells))]
    mean_new, harm_new = launch(
        lambda *refs: close_kernel(*refs, coeff=1.0), tuple(outs), (),
        (rim_a, index, weight, jac, step, mean_base, harm_base, near),
        scratch=[fields, words(ALL_FIELDS), *held(*outs)],
    )
    return mean_new, harm_new.swapaxes(0, 1)[None]


def solution(mesh):
    finer = Mesh(mesh.devices.reshape(mesh.shape["cells"], 2, 2), ("cells", *HARM))
    return jax.shard_map(
        shards,
        mesh=finer,
        in_specs=(
            P(None, "cells"),
            P(HARM, None, None, "cells"),
            P(HARM, None, None, "cells"),
            P(None, None, "cells"),
            P(None, "cells"),
            P(None, "cells"),
            P(None, "cells"),
            P("cells"),
            P(None, "cells"),
            P(HARM),
        ),
        out_specs=(P(None, "cells"), P(HARM, None, None, "cells")),
        check_vma=False,
    )
```

```python
import jax
import jax.numpy as jnp
from jax import lax
from jax.experimental import pallas as pl
from jax.experimental.pallas import tpu as pltpu
from jax.sharding import Mesh
from jax.sharding import PartitionSpec as P

VARS = 5
FACES = 6
SECTIONS = 2
ROWS = 3 * VARS
MEAN_FIELDS = range(VARS)
HARM_FIELDS = range(VARS, ROWS)
ALL_FIELDS = range(ROWS)
HARM = ("harm_0", "harm_1")
HARM_DEVICES = 4
LANES = 128
SUBS = 8
BASE_FREQ = 0.8
F32 = jnp.float32


def struct(*shape, dtype=F32):
    return pltpu.VMEM(shape, dtype)


def spread(row):
    return jnp.broadcast_to(row, (SUBS, LANES))


def packed(tile, first):
    sub = lax.broadcasted_iota(jnp.int32, (SUBS, LANES), 0)
    out = spread(tile(first))
    for i in range(1, SUBS):
        out = jnp.where(sub == i, spread(tile(first + i)), out)
    return out


def picked(row, fields, count, index):
    low = index & (LANES - 1)
    high = index >> 7
    out = [None] * len(fields)
    for h in range(count):
        hit = high == h
        for i, r in enumerate(fields):
            value = jnp.take_along_axis(spread(row(r, h)), low, axis=1)
            out[i] = jnp.where(hit, value, jnp.zeros_like(value) if h == 0 else out[i])
    return out


def store_tiles(row, tile_index, pay_a, pay_b, rows):
    def send(i, _):
        values = picked(row, range(ROWS), rows, tile_index[i])
        for k, pay in enumerate((pay_a, pay_b)):

            @pl.when(i == k)
            def _():
                for r, value in enumerate(values):
                    pay[r] = value

        return 0

    lax.fori_loop(0, 2, send, 0)


def native_row(mean_ref, harm_ref):
    def row(r, h):
        lanes = slice(h * LANES, (h + 1) * LANES)
        if r < VARS:
            return mean_ref[r : r + 1, lanes]
        part, var = divmod(r - VARS, VARS)
        return harm_ref[var, part : part + 1, lanes]

    return row


def fetch(sources, targets, sems):
    copies = [pltpu.make_async_copy(s, t, sems.at[i]) for i, (s, t) in enumerate(zip(sources, targets))]
    for copy in copies:
        copy.start()
    return [copy.wait for copy in copies]


def open_kernel(
    place_ref, tiles_hbm, mean_hbm, harm_hbm, links_hbm, weight_hbm, flow_hbm, jac_hbm, source_hbm, step_hbm,
    pay_a, pay_b, tile_idx, mean_ref, harm_ref, links_ref, weight_ref, flow_ref, jac_ref, source_ref, step_ref,
    tiles_ref, sems,
):
    waits = fetch(
        (tiles_hbm, mean_hbm, harm_hbm, links_hbm, weight_hbm, flow_hbm, jac_hbm, source_hbm, step_hbm),
        (tiles_ref, mean_ref, harm_ref, links_ref, weight_ref, flow_ref, jac_ref, source_ref, step_ref),
        sems,
    )
    for wait in waits[:3]:
        wait()
    lowers_first = place_ref[0] % 2 == 1
    lower, upper = (
        packed(lambda t, k=k: tiles_ref[k : k + 1, t * LANES : (t + 1) * LANES], 0) for k in range(2)
    )
    first = jnp.where(lowers_first, lower, upper)
    second = jnp.where(lowers_first, upper, lower)
    tile_idx[0] = first
    tile_idx[1] = second
    row = native_row(mean_ref, harm_ref)
    store_tiles(row, tile_idx, pay_a, pay_b, mean_ref.shape[1] // LANES)
    for wait in waits[3:]:
        wait()


TOP = float(2**20 - 1)


def largest(values):
    top = jnp.abs(values[0])
    for value in values[1:]:
        top = jnp.maximum(top, jnp.abs(value))
    top = jnp.max(jnp.max(top, axis=0, keepdims=True), axis=1, keepdims=True)
    return jnp.maximum(jnp.broadcast_to(top, (SUBS, LANES)), 1e-30)


def pack_table(load, blocks, fields, words_ref):
    unit = {}
    scale = {}
    for kind in ([r for r in fields if r < VARS], [r for r in fields if r >= VARS]):
        if kind:
            top = largest([load(r, g) for r in kind for g in range(blocks)])
            for r in kind:
                unit[r] = top * (1.0 / TOP)
                scale[r] = TOP / top
    fixed = lambda r, g: jnp.floor(load(r, g) * scale[r] + 0.5).astype(jnp.int32)
    for i in range(len(fields) // 3):
        for g in range(blocks):
            at = slice(g * SUBS, (g + 1) * SUBS)
            first, second, third = (fixed(r, g) for r in fields[3 * i : 3 * i + 3])
            words_ref[2 * i, at, :] = (first << 11) | ((third >> 10) & 0x7FF)
            words_ref[2 * i + 1, at, :] = (second << 11) | (third & 0x3FF)
    return unit


def gather_into(row, fields, count, words_ref, first, index_ref, weight_ref, begin, faces, unit, start):
    triples = len(fields) // 3
    words = 2 * triples
    rest = fields[3 * triples :]

    def word(w, h):
        return words_ref[w, h : h + 1, :] if w < words else row(rest[w - words], h)

    def face(f, acc):
        found = picked(word, range(words + len(rest)), count, index_ref[begin + f] - first)
        weight = weight_ref[begin + f]
        values = []
        for i in range(triples):
            one, two = found[2 * i], found[2 * i + 1]
            values += [one >> 11, two >> 11, ((one << 21) >> 11) | (two & 0x3FF)]
        values = [v.astype(F32) for v in values] + found[words:]
        return tuple(a + weight * v for a, v in zip(acc, values))

    sums = (jnp.zeros((SUBS, LANES), F32),) * len(fields)
    for f in range(faces):
        sums = face(f, sums)
    return [
        s + (a if i >= 3 * triples else unit[r] * a) for i, (r, s, a) in enumerate(zip(fields, start, sums))
    ]


def share_of(place_ref, index_ref):
    count = index_ref.shape[0] // HARM_DEVICES
    begin = place_ref[0] // 2 * count
    return begin, count, begin // FACES


def gather_fields(row, fields, count, words_ref, first, index_ref, weight_ref, unit, start, out_ref, lead=0):
    for g in range(index_ref.shape[0] // FACES):
        at = slice(g * SUBS, (g + 1) * SUBS)
        values = gather_into(
            row, fields, count, words_ref, first, index_ref, weight_ref, g * FACES, FACES, unit,
            [start(r - lead, at) for r in fields],
        )
        for r, value in zip(fields, values):
            out_ref[r - lead, at, :] = value


def half_rows(half):
    return pl.ds(pl.multiple_of(half * SUBS, SUBS), SUBS)


def zero_start(*_):
    return jnp.zeros((SUBS, LANES), F32)


def prepare_kernel(
    place_ref, order_ref, mean_ref, harm_ref, links_ref, weight_in, flow_ref, jac_ref, source_ref, step_ref,
    mean_base, harm_base, index_ref, weight_ref, wsum_ref, mean_out, state_ref, jac_out, flow_out, source_out,
    full_ref, mean_acc, words_ref, mean_words, *, coeff,
):
    groups = mean_ref.shape[1] // LANES
    flips = place_ref[0] % 2 == 0
    rim = groups * LANES
    lane = lambda t: slice(t * LANES, (t + 1) * LANES)
    for g in range(groups // SUBS):
        total = None
        for f in range(FACES):
            link = packed(lambda t: links_ref[f : f + 1, lane(t)], g * SUBS)
            flipped = jnp.where(link >= rim, link ^ (rim // 2), link)
            index_ref[g * FACES + f] = jnp.where(flips, flipped, link)
            weight = packed(lambda t: weight_in[f : f + 1, lane(t)], g * SUBS)
            weight_ref[g * FACES + f] = weight
            total = weight if total is None else total + weight
        wsum_ref[g * SUBS : (g + 1) * SUBS, :] = total
    row = native_row(mean_ref, harm_ref)
    flow = native_row(mean_ref, flow_ref)
    for g in range(0, groups, SUBS):
        at = slice(g, g + SUBS)
        for r in range(VARS):
            mean_out[r, at, :] = packed(lambda t: row(r, t), g)
        for r in range(2 * VARS):
            state_ref[r, at, :] = packed(lambda t: row(VARS + r, t), g)
    for g in range(0, groups, SUBS):
        at = slice(g, g + SUBS)
        for r in range(2 * VARS):
            flow_out[r, at, :] = packed(lambda t: flow(VARS + r, t), g)
        for v in range(VARS):
            source_out[v, at, :] = packed(lambda t: source_ref[v : v + 1, lane(t)], g)
        for j in range(VARS):
            for i in range(VARS):
                jac_out[j * VARS + i, at, :] = packed(lambda t: jac_ref[j, i : i + 1, lane(t)], g)
    row = fields_row(mean_out, state_ref)
    load = fields_block(mean_out, state_ref)
    unit = pack_table(load, groups // SUBS, HARM_FIELDS, words_ref)
    mean_unit = pack_table(load, groups // SUBS, MEAN_FIELDS, mean_words)
    gather_fields(
        row, HARM_FIELDS, groups, words_ref, 0, index_ref, weight_ref, unit, zero_start, full_ref, VARS
    )
    begin, count, half = share_of(place_ref, index_ref)
    values = gather_into(
        row, MEAN_FIELDS, groups, mean_words, 0, index_ref, weight_ref, begin, count, mean_unit,
        [zero_start()] * VARS,
    )
    mean_acc[...] = jnp.zeros(mean_acc.shape, F32)
    for r, value in enumerate(values):
        mean_acc[r, half_rows(half), :] = value
    lead = place_ref[0] // 2 == 0
    for g in range(groups // SUBS):
        at = slice(g * SUBS, (g + 1) * SUBS)
        mean = [mean_out[v, at, :] for v in range(VARS)]
        state = [state_ref[r, at, :] for r in range(2 * VARS)]
        wsum = wsum_ref[at, :]
        scale = coeff * step_ref[at, :]
        flux = []
        for v in range(VARS):
            stress = state[v] * flow_out[v, at, :] + state[VARS + v] * flow_out[VARS + v, at, :]
            flux.append(jnp.where(lead, wsum * mean[v], 0.0) - mean_acc[v, at, :] - stress)
        for v, res in enumerate(transposed(jac_out, at, flux)):
            own = jnp.where(lead, mean[v] + scale * source_out[v, at, :], 0.0)
            mean_base[v, at, :] = own - scale * res
        gathered = [full_ref[r, at, :] for r in range(2 * VARS)]
        harm_step(order_ref, at, mean, state, state, gathered, wsum, scale, jac_out, flow_out, harm_base)


def fields_row(mean_ref, harm_ref):
    def row(r, h):
        return mean_ref[r, h : h + 1, :] if r < VARS else harm_ref[r - VARS, h : h + 1, :]

    return row


def fields_block(mean_ref, harm_ref):
    def load(r, g):
        at = slice(g * SUBS, (g + 1) * SUBS)
        return mean_ref[r, at, :] if r < VARS else harm_ref[r - VARS, at, :]

    return load


def rim_row(*rims):
    rows = rims[0].shape[1]
    return lambda r, h: rims[h // rows][r, h % rows : h % rows + 1, :]


def rim_block(*rims):
    blocks = rims[0].shape[1] // SUBS
    return lambda r, g: rims[g // blocks][r, g % blocks * SUBS : (g % blocks + 1) * SUBS, :]


def near_kernel(rim, index_ref, weight_ref, out_ref, words_ref):
    rows = rim.shape[1]
    first = (out_ref.shape[1] + rows) * LANES
    unit = pack_table(rim_block(rim), rows // SUBS, ALL_FIELDS, words_ref)
    gather_fields(
        rim_row(rim), ALL_FIELDS, rows, words_ref, first, index_ref, weight_ref, unit, zero_start, out_ref
    )


def transposed(jac_ref, at, flux):
    out = []
    for i in range(VARS):
        res = jac_ref[i, at, :] * flux[0]
        for j in range(1, VARS):
            res = res + jac_ref[j * VARS + i, at, :] * flux[j]
        out.append(res)
    return out


def harm_step(order_ref, at, mean, state, start, gathered, wsum, scale, jac_ref, flow_ref, out_ref):
    omega = BASE_FREQ * (order_ref[0].astype(F32) + 1.0)
    flux = [wsum * s - x for s, x in zip(state, gathered)]
    for part in range(2):
        res = transposed(jac_ref, at, flux[part * VARS : (part + 1) * VARS])
        for i in range(VARS):
            r = part * VARS + i
            turned = omega * state[(1 - part) * VARS + i]
            full = res[i] + turned if part == 0 else res[i] - turned
            full = full - mean[i] * flow_ref[r, at, :]
            out_ref[r, at, :] = start[r] - scale * full


def middle_kernel(
    place_ref, rim_a, rim_b, index_ref, weight_ref, mean_base, harm_base, jac_ref, flow_ref, step_ref,
    out_ref, part_ref, words_ref, mean_words, *, coeff,
):
    groups = mean_base.shape[1]
    rows = 2 * rim_a.shape[1]
    row, load = rim_row(rim_a, rim_b), rim_block(rim_a, rim_b)
    unit = pack_table(load, rows // SUBS, HARM_FIELDS, words_ref)
    mean_unit = pack_table(load, rows // SUBS, MEAN_FIELDS, mean_words)
    begin, count, half = share_of(place_ref, index_ref)
    values = gather_into(
        row, MEAN_FIELDS, rows, mean_words, groups * LANES, index_ref, weight_ref, begin, count, mean_unit,
        [zero_start()] * VARS,
    )
    for v in range(VARS):
        part_ref[v] = mean_base[v]
    at = half_rows(half)
    scale = coeff * step_ref[at, :]
    for v, res in enumerate(transposed(jac_ref, at, values)):
        part_ref[v, at, :] = mean_base[v, at, :] + scale * res
    for g in range(groups // SUBS):
        at = slice(g * SUBS, (g + 1) * SUBS)
        values = gather_into(
            row, HARM_FIELDS, rows, words_ref, groups * LANES, index_ref, weight_ref, g * FACES, FACES, unit,
            [zero_start()] * (2 * VARS),
        )
        scale = coeff * step_ref[at, :]
        new = []
        for first in range(0, 2 * VARS, VARS):
            for v, res in enumerate(transposed(jac_ref, at, values[first : first + VARS])):
                new.append(harm_base[first + v, at, :] + scale * res)
        for r, value in enumerate(new):
            out_ref[r, at, :] = value
        for v in range(VARS):
            part_ref[VARS + v, at, :] = new[v] * flow_ref[v, at, :] + new[VARS + v] * flow_ref[VARS + v, at, :]


def join_kernel(parts_ref, state_ref, tile_idx, mean_ref, stress_ref, pay_a, pay_b):
    for v in range(VARS):
        for ref, r in ((mean_ref, v), (stress_ref, VARS + v)):
            total = parts_ref[0, r]
            for k in range(1, HARM_DEVICES):
                total = total + parts_ref[k, r]
            ref[v] = total
    row = fields_row(mean_ref, state_ref)
    store_tiles(row, tile_idx, pay_a, pay_b, mean_ref.shape[1])


def own_kernel(
    order_ref, index_ref, weight_ref, wsum_ref, mean_ref, state_ref, mean_start, harm_start,
    jac_ref, flow_ref, source_ref, step_ref, stress_ref, mean_base, harm_base, full_ref, words_ref, *, coeff,
):
    groups = mean_ref.shape[1]
    unit = pack_table(fields_block(mean_ref, state_ref), groups // SUBS, ALL_FIELDS, words_ref)
    gather_fields(
        fields_row(mean_ref, state_ref), ALL_FIELDS, groups, words_ref, 0, index_ref, weight_ref, unit,
        zero_start, full_ref,
    )
    for g in range(groups // SUBS):
        at = slice(g * SUBS, (g + 1) * SUBS)
        mean = [mean_ref[v, at, :] for v in range(VARS)]
        state = [state_ref[r, at, :] for r in range(2 * VARS)]
        wsum = wsum_ref[at, :]
        scale = coeff * step_ref[at, :]
        flux = [wsum * m - full_ref[v, at, :] - stress_ref[v, at, :] for v, m in enumerate(mean)]
        for v, res in enumerate(transposed(jac_ref, at, flux)):
            mean_base[v, at, :] = mean_start[v, at, :] - scale * (res - source_ref[v, at, :])
        gathered = [full_ref[VARS + r, at, :] for r in range(2 * VARS)]
        start = [harm_start[r, at, :] for r in range(2 * VARS)]
        harm_step(order_ref, at, mean, state, start, gathered, wsum, scale, jac_ref, flow_ref, harm_base)


def close_kernel(
    rim, index_ref, weight_ref, jac_ref, step_ref, mean_base, harm_base, near_ref,
    mean_hbm, harm_hbm, full_ref, words_ref, mean_out, harm_out, sems, *, coeff,
):
    groups = mean_base.shape[1]
    rows = rim.shape[1]
    unit = pack_table(rim_block(rim), rows // SUBS, ALL_FIELDS, words_ref)
    base = fields_block(mean_base, harm_base)
    copies = []
    for g in range(groups // SUBS):
        at = slice(g * SUBS, (g + 1) * SUBS)
        full = gather_into(
            rim_row(rim), ALL_FIELDS, rows, words_ref, groups * LANES, index_ref, weight_ref, g * FACES, FACES,
            unit, [near_ref[r, at, :] for r in ALL_FIELDS],
        )
        scale = coeff * step_ref[at, :]
        for first in range(0, ROWS, VARS):
            for v, res in enumerate(transposed(jac_ref, at, full[first : first + VARS])):
                full_ref[first + v, at, :] = base(first + v, g) + scale * res
        for t in range(g * SUBS, (g + 1) * SUBS):
            lanes = slice(t * LANES, (t + 1) * LANES)
            mean_out[:, lanes] = stacked(lambda i: full_ref[i, t : t + 1, :], VARS)
            for v in range(VARS):
                harm_out[v, :, lanes] = stacked(lambda i: full_ref[(i + 1) * VARS + v, t : t + 1, :], 2)
        part = pl.ds(g * SUBS * LANES, SUBS * LANES)
        for i, (out, hbm) in enumerate(
            ((mean_out.at[:, part], mean_hbm.at[:, part]), (harm_out.at[:, :, part], harm_hbm.at[:, :, part]))
        ):
            copies.append(pltpu.make_async_copy(out, hbm, sems.at[2 * g + i]))
            copies[-1].start()
    for copy in copies:
        copy.wait()


def stacked(row, count):
    sub = lax.broadcasted_iota(jnp.int32, (count, LANES), 0)
    out = jnp.broadcast_to(row(0), (count, LANES))
    for i in range(1, count):
        out = jnp.where(sub == i, jnp.broadcast_to(row(i), (count, LANES)), out)
    return out


def held(*arrays):
    return [*(pltpu.VMEM(a.shape, a.dtype) for a in arrays), pltpu.SemaphoreType.DMA((SUBS,))]


def launch(body, out_shape, scalars, args, raw=(), scratch=()):
    smem = pl.BlockSpec(memory_space=pltpu.SMEM)
    vmem = pl.BlockSpec(memory_space=pltpu.VMEM)
    anywhere = pl.BlockSpec(memory_space=pl.ANY)
    return pl.pallas_call(
        body,
        out_shape=out_shape,
        in_specs=[smem] * len(scalars) + [anywhere] * len(raw) + [vmem] * len(args),
        out_specs=[anywhere if isinstance(s, jax.ShapeDtypeStruct) else vmem for s in out_shape],
        scratch_shapes=scratch,
    )(*scalars, *raw, *(pltpu.with_memory_space_constraint(a, pltpu.VMEM) for a in args))


def exchange(pay_a, pay_b):
    count = lax.axis_size("cells")
    near = [(b, b ^ 1) for b in range(count)]
    far = [(b, (b - 1 + 2 * (b % 2)) % count) for b in range(count)]
    rim_a = lax.ppermute(pay_a, "cells", far)
    rim_b = lax.ppermute(pay_b, "cells", near)
    return rim_a, rim_b


def shards(
    mean_adjoint,
    harm_adjoint,
    harm_flow,
    flux_jacobian,
    face_weight,
    face_links,
    face_tiles,
    pseudo_step,
    mean_source,
    harm_order,
):
    cells = mean_adjoint.shape[1]
    groups = cells // LANES
    halves = groups // SUBS
    rim_rows = face_tiles.shape[1] // LANES
    harm_adjoint, harm_flow = (
        a[0].swapaxes(0, 1) for a in (harm_adjoint, harm_flow)
    )
    place = (1 - lax.axis_index("cells") % 2 + 2 * lax.axis_index(HARM)).astype(jnp.int32)[None]
    step = pseudo_step.reshape(groups, LANES)
    mean_fields, harm_fields = struct(VARS, groups, LANES), struct(2 * VARS, groups, LANES)
    pays = (struct(ROWS, rim_rows, LANES), struct(ROWS, rim_rows, LANES))
    raw = (
        mean_adjoint, harm_adjoint, face_links, face_weight, harm_flow, flux_jacobian, mean_source, step
    )
    held_raw = tuple(struct(*a.shape, dtype=a.dtype) for a in raw)
    pay_a, pay_b, tile_idx, *inside, step = launch(
        open_kernel, pays + (struct(2, rim_rows, LANES, dtype=jnp.int32),) + held_raw, (place,), (),
        (face_tiles, *raw), [pltpu.VMEM(face_tiles.shape, jnp.int32), pltpu.SemaphoreType.DMA((9,))],
    )
    rim_a, rim_b = exchange(pay_a, pay_b)
    registers = FACES * halves
    words = lambda fields: struct(max(len(fields) // 3 * 2, 1), groups, LANES, dtype=jnp.int32)
    harm_words, mean_words = words(HARM_FIELDS), words(MEAN_FIELDS)
    mean_base, harm_base, index, weight, wsum, mean_start, harm_start, jac, flow, source = launch(
        lambda *refs: prepare_kernel(*refs, coeff=1.0 / SECTIONS),
        (
            mean_fields,
            harm_fields,
            struct(registers, SUBS, LANES, dtype=jnp.int32),
            struct(registers, SUBS, LANES),
            struct(groups, LANES),
            mean_fields,
            harm_fields,
            struct(VARS * VARS, groups, LANES),
            harm_fields,
            mean_fields,
        ),
        (place, harm_order), (*inside, step),
        scratch=[harm_fields, mean_fields, harm_words, mean_words],
    )
    state, part = launch(
        lambda *refs: middle_kernel(*refs, coeff=1.0 / SECTIONS), (harm_fields, harm_fields), (place,),
        (rim_a, rim_b, index, weight, mean_base, harm_base, jac, flow, step),
        scratch=[harm_words, mean_words],
    )
    parts = lax.all_gather(part, HARM)
    mean, stress, pay_a, pay_b = launch(join_kernel, (mean_fields, mean_fields) + pays, (), (parts, state, tile_idx))
    rim_a, rim_b = exchange(pay_a, pay_b)
    fields = struct(ROWS, groups, LANES)
    mean_base, harm_base = launch(
        lambda *refs: own_kernel(*refs, coeff=1.0), (mean_fields, harm_fields), (harm_order,),
        (index, weight, wsum, mean, state, mean_start, harm_start, jac, flow, source, step, stress),
        scratch=[fields, words(ALL_FIELDS)],
    )
    (near,) = launch(near_kernel, (fields,), (), (rim_b, index, weight), scratch=[words(ALL_FIELDS)])
    outs = [jax.ShapeDtypeStruct(s, F32) for s in ((VARS, cells), (VARS, 2, cells))]
    mean_new, harm_new = launch(
        lambda *refs: close_kernel(*refs, coeff=1.0), tuple(outs), (),
        (rim_a, index, weight, jac, step, mean_base, harm_base, near),
        scratch=[fields, words(ALL_FIELDS), *held(*outs)],
    )
    return mean_new, harm_new.swapaxes(0, 1)[None]


def solution(mesh):
    finer = Mesh(mesh.devices.reshape(mesh.shape["cells"], 2, 2), ("cells", *HARM))
    return jax.shard_map(
        shards,
        mesh=finer,
        in_specs=(
            P(None, "cells"),
            P(HARM, None, None, "cells"),
            P(HARM, None, None, "cells"),
            P(None, None, "cells"),
            P(None, "cells"),
            P(None, "cells"),
            P(None, "cells"),
            P("cells"),
            P(None, "cells"),
            P(HARM),
        ),
        out_specs=(P(None, "cells"), P(HARM, None, None, "cells")),
        check_vma=False,
    )
```
